32 devices in a mesh: dp: 2 (over x), space: 16 (over z, y, core).
Axes of the slice: x: 2, y: 2, z: 4, core: 2. Of those that a mesh axis runs over, the one named last changes fastest.
Arguments:
- tiles_in: bfloat16 [2, 64, 8, 8, 384], P('dp', 'space'), may hold values from -6 to 6
- upstream: bfloat16 [2, 64, 8, 8, 384], P('dp', 'space'), may hold values from -1.1953125 to 1.1953125
- pool_weight: float32 [2, 64], P('dp', 'space'), may hold values from 0.25 to 4
- slide_cot: float32 [2, 384], P('dp'), may hold values from -6 to 6
- adjacency: int32 [2, 64, 8], P('dp', 'space'), may hold values from -1 to 63, as said below
- counts: int32 [2, 16], P('dp', 'space'), may hold values from 1 to 4, as said below
- kernel: float32 [7, 7, 384], replicated, may hold values from -0.875 to 0.875
- norm_gain: float32 [384], replicated, may hold values from 0.5 to 1.5
- w_in: bfloat16 [384, 1536], replicated, may hold values from -0.3125 to 0.3125
- w_out: bfloat16 [1536, 384], replicated, may hold values from -0.15625 to 0.15625
- layer_scale: float32 [384], replicated, may hold values from 0.1 to 1
Outputs:
- embedding: float32 [2, 384], P('dp')
- grad_tiles: bfloat16 [2, 64, 8, 8, 384], P('dp', 'space')
- grad_w_out: float32 [1536, 384], P('space')
- grad_kernel: float32 [7, 7, 384], replicated
The draws below stay inside these ranges and needn't reach their ends.
Inputs may be any that keep to these rules, and one draw needn't show every extreme that they name: Slots form blocks of 4; block k of a slide is one row of tiles, its live tiles in its first counts slots in column order; the last block of every slide is full, and often another one too. `adjacency`: tiles lie on a grid: entries 0, 4, 5 name live slots of the block before the tile's own, entries 1, 6, 7 of the block after it, entries 2 and 3 of its own block. The lists are mutual (b is the north neighbour of a exactly when a is the south neighbour of b, and likewise for the other directions). Slots that are not live have no neighbours and are named by none.
All inputs are finite; a program needn't handle non-finite values.
Results may differ from the reference program's by a relative error of at most 0.011.
Values may be sent and summed in bfloat16 or wider, within the bound.
No kernel may reach another device: no remote copies, remote signals or barrier semaphores. Data moves between devices by JAX's collectives and lax.ppermute only.
A program may use at most 64 MiB of HBM per device.

```python
import math
import jax
import jax.numpy as jnp
from jax import lax

C = 384
HID = 1536
TILE = 8
CAP = 4
SLIDES = 2
SLOTS = 64


def geometry(key):
    blocks = SLOTS // CAP
    counts = jax.random.randint(jax.random.fold_in(key, 11), (SLIDES, blocks), 1, CAP + 1)
    fullest = jax.random.randint(jax.random.fold_in(key, 12), (SLIDES, 1), 0, blocks)
    block_ids = jnp.arange(blocks)[None, :]
    counts = jnp.where((block_ids == fullest) | (block_ids == blocks - 1), CAP, counts)
    offsets = jax.random.randint(jax.random.fold_in(key, 13), (SLIDES, blocks), 0, CAP + 1)
    return (counts.astype(jnp.int32), offsets.astype(jnp.int32))


def draw_counts(key, part):
    return geometry(key)[0]


def draw_adjacency(key, part):
    counts, offsets = geometry(key)
    blocks = SLOTS // CAP
    block_ids = jnp.arange(blocks, dtype=jnp.int32)
    slot_ids = jnp.arange(CAP, dtype=jnp.int32)
    column = offsets[:, :, None] + slot_ids[None, None, :]
    alive = slot_ids[None, None, :] < counts[:, :, None]
    moves = [(-1, 0), (1, 0), (0, -1), (0, 1), (-1, -1), (-1, 1), (1, -1), (1, 1)]
    lists = []
    for block_step, column_step in moves:
        other = block_ids + block_step
        inside = (other >= 0) & (other < blocks)
        clipped = jnp.clip(other, 0, blocks - 1)
        other_offset = offsets[:, clipped]
        other_count = counts[:, clipped]
        target = column + column_step - other_offset[:, :, None]
        usable = alive & inside[None, :, None] & (target >= 0) & (target < other_count[:, :, None])
        target_slot = clipped[None, :, None] * CAP + target
        lists.append(jnp.where(usable, target_slot, -1))
    return jnp.stack(lists, axis=-1).reshape(SLIDES, SLOTS, 8).astype(jnp.int32)


def levels(rng, dims, cuts, low, high):
    level = 1.0
    for position, blocks in cuts:
        draws = jax.random.uniform(jax.random.fold_in(jax.random.fold_in(rng, 6), position), (blocks,), jnp.float32, low / len(cuts), high / len(cuts))
        level = level * jnp.repeat(jnp.exp(draws), dims[position] // blocks).reshape((-1,) + (1,) * (len(dims) - 1 - position))
    return level


def normal_values(own_key, extent, spread, bound, split=(), held_as=jnp.bfloat16):
    gain = levels(own_key, extent, split, -0.22, 0.18) if split else 1.0
    array = jax.random.normal(own_key, extent, jnp.float32) * spread * gain
    return jnp.minimum(jnp.maximum(array, -bound), bound).astype(held_as)


def setup_inputs(seed: int = 0) -> dict:
    seeds = jax.random.split(jax.random.key(seed), 12)
    tiles_in = normal_values(seeds[0], (SLIDES, SLOTS, TILE, TILE, C), 1.0, 6.0, ((0, 2), (1, 16)))
    upstream = normal_values(seeds[1], (SLIDES, SLOTS, TILE, TILE, C), 0.2, 1.1953125, ((0, 2), (1, 16)))
    pool_weight = jnp.clip(jnp.exp(math.log(4.0) - 2.7725887 * jax.random.uniform(seeds[2], (SLIDES, SLOTS), jnp.float32) ** levels(seeds[2], (SLIDES, SLOTS), ((0, 2), (1, 16)), -0.2, 0.2)), 0.25, 4.0)
    slide_cot = normal_values(seeds[3], (SLIDES, C), 1.0, 6.0, ((0, 2),), jnp.float32)
    adjacency = draw_adjacency(jax.random.fold_in(seeds[11], 71), 0)
    counts = draw_counts(jax.random.fold_in(seeds[11], 71), 0)
    kernel = normal_values(seeds[6], (7, 7, C), 49 ** -0.5, 0.875, (), jnp.float32)
    norm_gain = jnp.clip(1.0 + 0.1 * jax.random.normal(seeds[7], (C,), jnp.float32), 0.5, 1.5)
    w_in = normal_values(seeds[8], (C, HID), C ** -0.5, 0.3125)
    w_out = normal_values(seeds[9], (HID, C), HID ** -0.5, 0.15625)
    layer_scale = jnp.clip(jnp.exp(jax.random.uniform(seeds[10], (C,), jnp.float32, math.log(0.1), math.log(1.0))), 0.1, 1.0)
    return dict(tiles_in=tiles_in, upstream=upstream, pool_weight=pool_weight, slide_cot=slide_cot, adjacency=adjacency, counts=counts, kernel=kernel, norm_gain=norm_gain, w_in=w_in, w_out=w_out, layer_scale=layer_scale)


sqrt_half = 0.7071067811865476
inv_root_two_pi = 0.3989422804014327

def depthwise(padded, kernel, tile_side):
    total = jnp.zeros(padded.shape[:1] + (tile_side, tile_side, padded.shape[3]), jnp.float32)
    for row_tap in range(7):
        for col_tap in range(7):
            window = padded[:, row_tap:row_tap + tile_side, col_tap:col_tap + tile_side, :].astype(jnp.float32)
            total = total + window * kernel[row_tap, col_tap]
    return total

def pick(source, wanted, offset):
    valid = wanted >= 0
    index = jnp.clip(wanted - offset, 0, source.shape[0] - 1).astype(jnp.int32)
    chosen = jnp.take(source, index, axis=0)
    return jnp.where(valid[:, None, None, None], chosen, jnp.zeros_like(chosen))

def frame(own, north_rows, south_rows, right_cols, left_cols, wanted, north_base, own_base, south_base):
    tile_side = own.shape[1]
    upper = jnp.concatenate([pick(north_rows, wanted[:, 4], north_base)[:, :, tile_side - 3:], pick(north_rows, wanted[:, 0], north_base), pick(north_rows, wanted[:, 5], north_base)[:, :, :3]], axis=2)
    middle = jnp.concatenate([pick(right_cols, wanted[:, 2], own_base), own, pick(left_cols, wanted[:, 3], own_base)], axis=2)
    lower = jnp.concatenate([pick(south_rows, wanted[:, 6], south_base)[:, :, tile_side - 3:], pick(south_rows, wanted[:, 1], south_base), pick(south_rows, wanted[:, 7], south_base)[:, :, :3]], axis=2)
    return jnp.concatenate([upper, middle, lower], axis=1)

def block_pass(padded, own, upstream, pool_weight, live, slide_cot, kernel, norm_gain, w_in, w_out, layer_scale):
    tile_side = own.shape[1]
    channels = own.shape[3]
    conv_out = depthwise(padded, kernel, tile_side)
    centred = conv_out - lax.optimization_barrier(jnp.mean(conv_out, axis=-1, keepdims=True))
    inv_std = lax.rsqrt(lax.optimization_barrier(jnp.mean(centred * centred, axis=-1, keepdims=True)) + 1e-06)
    normed = centred * inv_std
    lifted = (normed * norm_gain).astype(jnp.bfloat16).reshape(-1, channels)
    pre = jnp.dot(lifted, w_in, preferred_element_type=jnp.float32)
    cdf = 0.5 * (1.0 + jax.scipy.special.erf(pre * sqrt_half))
    activated = (pre * cdf).astype(jnp.bfloat16)
    mixed = jnp.dot(activated, w_out, preferred_element_type=jnp.float32).reshape(own.shape)
    block_out = own.astype(jnp.float32) + layer_scale * mixed
    weight_live = live * pool_weight
    emb_term = lax.optimization_barrier(jnp.sum(weight_live[:, None] * lax.optimization_barrier(jnp.sum(block_out, axis=(1, 2))), axis=0)) / tile_side
    extra = pool_weight[:, None] * slide_cot[None, :] / tile_side
    grad_out = live[:, None, None, None] * (upstream.astype(jnp.float32) + extra[:, None, None, :])
    grad_mixed = (grad_out * layer_scale).astype(jnp.bfloat16).reshape(-1, channels)
    grad_act = lax.dot_general(grad_mixed, w_out, (((1,), (1,)), ((), ())), preferred_element_type=jnp.float32)
    density = jnp.exp(-0.5 * pre * pre) * inv_root_two_pi
    grad_pre = (grad_act * (cdf + pre * density)).astype(jnp.bfloat16)
    grad_lift = lax.dot_general(grad_pre, w_in, (((1,), (1,)), ((), ())), preferred_element_type=jnp.float32)
    grad_normed = grad_lift.reshape(own.shape) * norm_gain
    grad_conv = inv_std * (grad_normed - lax.optimization_barrier(jnp.mean(grad_normed, axis=-1, keepdims=True)) - normed * lax.optimization_barrier(jnp.mean(grad_normed * normed, axis=-1, keepdims=True)))
    kernel_rows = []
    for row_tap in range(7):
        for col_tap in range(7):
            window = padded[:, row_tap:row_tap + tile_side, col_tap:col_tap + tile_side, :].astype(jnp.float32)
            kernel_rows.append(lax.optimization_barrier(jnp.sum(window * grad_conv, axis=(0, 1, 2))))
    kernel_grad = jnp.stack(kernel_rows).reshape(7, 7, channels)
    return (emb_term, grad_out, grad_conv, activated, grad_mixed, kernel_grad)

def reference(tiles_in, upstream, pool_weight, slide_cot, adjacency, counts, kernel, norm_gain, w_in, w_out, layer_scale):
    tile_side = TILE
    blocks = SLOTS // CAP
    embeddings = []
    gradients = []
    weight_total = jnp.zeros((HID, C), jnp.float32)
    kernel_total = jnp.zeros((7, 7, C), jnp.float32)
    for slide in range(SLIDES):
        own = tiles_in[slide]
        wanted = adjacency[slide]
        live = (jnp.arange(CAP, dtype=jnp.int32)[None, :] < counts[slide][:, None]).astype(jnp.float32).reshape(SLOTS)
        padded = frame(own, own[:, tile_side - 3:], own[:, :3], own[:, :, tile_side - 3:], own[:, :, :3], wanted, 0, 0, 0)
        cot = slide_cot[slide]

        def step(carry, parts):
            emb_acc, weight_acc, kernel_acc = carry
            pad_part, own_part, up_part, pool_part, live_part = parts
            emb_term, grad_out, grad_conv, activated, grad_mixed, kernel_grad = block_pass(pad_part, own_part, up_part, pool_part, live_part, cot, kernel, norm_gain, w_in, w_out, layer_scale)
            weight_acc = weight_acc + lax.dot_general(activated, grad_mixed, (((0,), (0,)), ((), ())), preferred_element_type=jnp.float32)
            return ((emb_acc + emb_term, weight_acc, kernel_acc + kernel_grad), (grad_out, grad_conv))
        parts = (padded.reshape((blocks, CAP) + padded.shape[1:]), own.reshape((blocks, CAP) + own.shape[1:]), upstream[slide].reshape((blocks, CAP) + own.shape[1:]), pool_weight[slide].reshape(blocks, CAP), live.reshape(blocks, CAP))
        start = (jnp.zeros((C,), jnp.float32), weight_total, kernel_total)
        (emb_sum, weight_total, kernel_total), (grad_out, grad_conv) = lax.scan(step, start, parts)
        grad_out = grad_out.reshape(own.shape)
        grad_conv = grad_conv.reshape(own.shape)
        padded_grad = frame(grad_conv, grad_conv[:, tile_side - 3:], grad_conv[:, :3], grad_conv[:, :, tile_side - 3:], grad_conv[:, :, :3], wanted, 0, 0, 0)
        back = depthwise(padded_grad, kernel[::-1, ::-1], tile_side)
        gradients.append(((grad_out + back) * live[:, None, None, None]).astype(jnp.bfloat16))
        embeddings.append(emb_sum)
    return (jnp.stack(embeddings), jnp.stack(gradients), weight_total, kernel_total)
```

```python
import functools

import jax
import jax.numpy as jnp
from jax import lax
from jax.experimental import pallas as pl
from jax.experimental.pallas import tpu as pltpu
from jax.sharding import PartitionSpec as P

sqrt_half = 0.7071067811865476
inv_root_two_pi = 0.3989422804014327
f32 = jnp.float32
bf16 = jnp.bfloat16
LANES = 128
SEPARATE = 2

VMEM = pl.BlockSpec(memory_space=pltpu.VMEM)
SMEM = pl.BlockSpec(memory_space=pltpu.SMEM)


def call(body, out_shape, in_specs, args, flops=0, scratch=(), name=None, limit=24 << 20):
    outs = out_shape if isinstance(out_shape, (list, tuple)) else [out_shape]
    total = sum(a.size * a.dtype.itemsize for a in list(args) + list(outs))
    return pl.pallas_call(
        body,
        out_shape=out_shape,
        in_specs=in_specs,
        out_specs=jax.tree.map(lambda _: VMEM, out_shape),
        scratch_shapes=scratch,
        name=name,
        compiler_params=pltpu.CompilerParams(vmem_limit_bytes=limit),
        cost_estimate=pl.CostEstimate(flops=flops, bytes_accessed=total, transcendentals=0),
    )(*args)


def struct(shape, dtype=f32):
    return jax.ShapeDtypeStruct(shape, dtype)


def passed_along(value, axis, steps):
    count = lax.axis_size(axis)
    leading, last = (max(0, -steps), min(count, count - steps))
    return lax.ppermute(value, axis, [(source, source + steps) for source in range(leading, last)])


def swapped(value, axis, bit):
    count = lax.axis_size(axis)
    return lax.ppermute(value, axis, [(source, source ^ bit) for source in range(count)])


def valid(entry):
    return jnp.where(entry >= 0, 1.0, 0.0).astype(f32)


def local(entry, capacity):
    return lax.rem(jnp.maximum(entry, 0), capacity)


def fill_row(put, left, middle, right):
    put(0, left)
    put(1, middle)
    put(2, right)


def place(pad_ref, tile, row, part, value, parts):
    for lane in range(parts):
        pad_ref[lane, tile, row, pl.ds(part * 8, 8), :] = value[:, lane * LANES : (lane + 1) * LANES]


def fill_middle(pad_ref, own_at, adj_ref, capacity, first_row, parts):
    for tile in range(capacity):
        west, east = adj_ref[tile, 2], adj_ref[tile, 3]
        for row in range(8):
            place(pad_ref, tile, first_row + row, 0, own_at(local(west, capacity), row) * valid(west), parts)
            place(pad_ref, tile, first_row + row, 1, own_at(tile, row), parts)
            place(pad_ref, tile, first_row + row, 2, own_at(local(east, capacity), row) * valid(east), parts)


def fill_edge(pad_ref, edge_ref, adj_ref, capacity, entries, first_row, parts):
    for tile in range(capacity):
        for part, entry in enumerate(entries):
            wanted = adj_ref[tile, entry]
            index, keep = local(wanted, capacity), valid(wanted)
            for row in range(3):
                value = edge_ref[index, row].astype(f32) * keep
                place(pad_ref, tile, first_row + row, part, value, parts)


UPPER, LOWER = (4, 0, 5), (6, 1, 7)


def convolve(pads, tap_row, finish, capacity, parts):
    for lane in range(parts):

        def one_tile(tile, _):
            sums = [None] * 8
            for col in range(7):
                taps = [tap_row(row, col, lane) for row in range(7)]
                for ref, rows, base in pads:
                    for held in range(rows):
                        window = ref[lane, tile, held, pl.ds(5 + col, 8), :]
                        for out in range(8):
                            tap = held + base - out
                            if 0 <= tap < 7:
                                term = window * taps[tap]
                                sums[out] = term if sums[out] is None else sums[out] + term
            finish(tile, lane, sums)
            return 0

        lax.fori_loop(0, capacity, one_tile, 0)


def lanes(lane):
    return slice(lane * LANES, (lane + 1) * LANES)


def edge_kernel(tiles_ref, north_ref, south_ref):
    north_ref[...] = tiles_ref[:, 5:8]
    south_ref[...] = tiles_ref[:, 0:3]


def early_kernel(
    adj_ref, counts_ref, pool_ref, tiles_ref, up_ref, cot_ref, kern_ref, scale_ref, w_out_ref,
    pad_ref, conv_ref, mixed_ref, act_grad_ref, own_sum_ref,
):
    capacity, parts = tiles_ref.shape[0], tiles_ref.shape[3] // LANES
    pixels = 64
    channels = tiles_ref.shape[3]
    own_sum = jnp.zeros((1, channels), f32)
    for tile in range(capacity):
        live = jnp.where(tile < counts_ref[0, 0], 1.0, 0.0).astype(f32)
        pool = pool_ref[0, tile]
        rows = slice(tile * pixels, (tile + 1) * pixels)
        out_grad = live * (up_ref[rows, :].astype(f32) + pool * cot_ref[...] * 0.125)
        mixed_ref[rows, 0:channels] = (out_grad * scale_ref[...]).astype(bf16)
        column = lax.broadcasted_iota(jnp.int32, (pixels, LANES), 1)
        mixed_ref[rows, channels:] = jnp.where(column == tile, 1.0, 0.0).astype(bf16)
        own = tiles_ref[tile].astype(f32)
        own_sum += live * pool * jnp.sum(own.reshape(pixels, channels), axis=0, keepdims=True)
    own_sum_ref[...] = own_sum
    act_grad_ref[...] = lax.dot_general(
        mixed_ref[:, 0:channels], w_out_ref[...], (((1,), (1,)), ((), ())), preferred_element_type=f32
    )
    fill_middle(pad_ref, lambda t, r: tiles_ref[t, r].astype(f32), adj_ref, capacity, 0, parts)

    def finish(tile, lane, sums):
        for row in range(8):
            conv_ref[pl.ds(tile * pixels + row * 8, 8), lanes(lane)] = sums[row]

    convolve(
        [(pad_ref, 8, 3)],
        lambda row, col, lane: kern_ref[row * 7 + col : row * 7 + col + 1, lanes(lane)],
        finish, capacity, parts,
    )


def forward_kernel(
    adj_ref, north_ref, south_ref, conv_ref, kern_ref, gain_ref, w_in_ref, mixed_ref, act_grad_ref,
    edge_ref, normed_ref, inv_ref, pre_grad_ref, weight_ref, pooled_ref, whole_ref,
):
    capacity, parts = adj_ref.shape[0], conv_ref.shape[1] // LANES
    channels = conv_ref.shape[1]
    pixels = 64
    fill_edge(edge_ref, north_ref, adj_ref, capacity, UPPER, 0, parts)
    fill_edge(edge_ref, south_ref, adj_ref, capacity, LOWER, 3, parts)

    def finish(tile, lane, sums):
        for row in range(8):
            at = pl.ds(tile * pixels + row * 8, 8)
            total = conv_ref[at, lanes(lane)]
            if sums[row] is not None:
                total = total + sums[row]
            whole_ref[at, lanes(lane)] = total

    convolve(
        [(edge_ref.at[:, :, 0:3], 3, 0), (edge_ref.at[:, :, 3:6], 3, 11)],
        lambda row, col, lane: kern_ref[row * 7 + col : row * 7 + col + 1, lanes(lane)],
        finish, capacity, parts,
    )
    conv = whole_ref[...]
    centred = conv - jnp.mean(conv, axis=-1, keepdims=True)
    inv_std = lax.rsqrt(jnp.mean(centred * centred, axis=-1, keepdims=True) + 1e-06)
    normed = centred * inv_std
    normed_ref[...] = normed
    inv_ref[...] = inv_std
    lifted = (normed * gain_ref[...]).astype(bf16)
    hidden = w_in_ref.shape[1]
    chunk = hidden // 4 if hidden % 512 == 0 else hidden
    for first in range(0, hidden, chunk):
        at = slice(first, first + chunk)
        pre = jnp.dot(lifted, w_in_ref[:, at], preferred_element_type=f32)
        cdf = 0.5 * (1.0 + lax.erf(pre * sqrt_half))
        activated = (pre * cdf).astype(bf16)
        density = jnp.exp(-0.5 * pre * pre) * inv_root_two_pi
        pre_grad_ref[:, at] = (act_grad_ref[:, at] * (cdf + pre * density)).astype(bf16)
        both = lax.dot_general(
            activated, mixed_ref[...], (((0,), (0,)), ((), ())), preferred_element_type=f32
        )
        weight_ref[at, :] = both[:, 0:channels]
        pooled_ref[at, :] = both[:, channels:]


def back_kernel(
    counts_ref, pool_ref, pre_grad_ref, w_in_ref, normed_ref, inv_ref, gain_ref, pooled_ref, w_out_ref,
    scale_ref, own_sum_ref, grad_ref, north_ref, south_ref, emb_ref,
):
    channels = gain_ref.shape[1]
    capacity = north_ref.shape[0]
    lift = lax.dot_general(
        pre_grad_ref[...], w_in_ref[...], (((1,), (1,)), ((), ())), preferred_element_type=f32
    )
    grad_normed = lift * gain_ref[...]
    normed = normed_ref[...]
    grad = inv_ref[...] * (
        grad_normed
        - jnp.mean(grad_normed, axis=-1, keepdims=True)
        - normed * jnp.mean(grad_normed * normed, axis=-1, keepdims=True)
    )
    grad_ref[...] = grad
    shaped = grad.reshape(capacity, 8, 8, channels)
    north_ref[...] = shaped[:, 5:8].astype(bf16)
    south_ref[...] = shaped[:, 0:3].astype(bf16)
    column = lax.broadcasted_iota(jnp.int32, (1, LANES), 1)
    weights = jnp.zeros((1, LANES), f32)
    for tile in range(capacity):
        amount = jnp.where(tile < counts_ref[0, 0], pool_ref[0, tile], 0.0)
        weights = jnp.where(column == tile, amount, weights)
    hidden = jnp.sum(pooled_ref[...] * weights, axis=1, keepdims=True)
    mixed = jnp.sum(hidden * w_out_ref[...].astype(f32), axis=0, keepdims=True)
    emb_ref[...] = (own_sum_ref[...] + scale_ref[...] * mixed) * 0.125


def taps_kernel(pad_ref, edge_ref, grad_ref, out_ref, part_ref):
    parts, capacity = pad_ref.shape[0], pad_ref.shape[1]
    for lane in range(parts):

        def one_column(col, _):
            def one_tile(tile, sums):
                sums = list(sums)
                grads = [grad_ref[pl.ds(tile * 64 + row * 8, 8), lanes(lane)] for row in range(8)]
                for held in range(14):
                    if 3 <= held < 11:
                        window = pad_ref[lane, tile, held - 3, pl.ds(5 + col, 8), :]
                    else:
                        row = held if held < 3 else held - 8
                        window = edge_ref[lane, tile, row, pl.ds(5 + col, 8), :]
                    for out in range(8):
                        tap = held - out
                        if 0 <= tap < 7:
                            sums[tap] = sums[tap] + window * grads[out]
                return tuple(sums)

            sums = lax.fori_loop(0, capacity, one_tile, tuple(jnp.zeros((8, LANES), f32) for _ in range(7)))
            for row in range(7):
                part_ref[row * 7 + col, :, lanes(lane)] = sums[row]
            return 0

        for col in range(7):
            one_column(col, 0)
    out_ref[...] = jnp.sum(part_ref[...], axis=1)


def final_kernel(
    adj_ref, counts_ref, pool_ref, grad_ref, north_ref, south_ref, kern_ref, up_ref, cot_ref,
    out_ref, pad_ref,
):
    capacity, parts = adj_ref.shape[0], grad_ref.shape[1] // LANES

    def own_at(tile, row):
        at = tile * 64 + row * 8
        return grad_ref[pl.ds(at if isinstance(at, int) else pl.multiple_of(at, 8), 8), :]

    fill_middle(pad_ref, own_at, adj_ref, capacity, 3, parts)
    fill_edge(pad_ref, north_ref, adj_ref, capacity, UPPER, 0, parts)
    fill_edge(pad_ref, south_ref, adj_ref, capacity, LOWER, 11, parts)

    def finish(tile, lane, sums):
        live = jnp.where(tile < counts_ref[0, 0], 1.0, 0.0).astype(f32)
        extra = pool_ref[0, tile] * cot_ref[:, lanes(lane)] * 0.125
        for row in range(8):
            at = pl.ds(tile * 64 + row * 8, 8)
            out_grad = live * (up_ref[at, lanes(lane)].astype(f32) + extra)
            out_ref[at, lanes(lane)] = (live * (out_grad + sums[row])).astype(bf16)

    convolve(
        [(pad_ref, 14, 0)],
        lambda row, col, lane: kern_ref[48 - row * 7 - col : 49 - row * 7 - col, lanes(lane)],
        finish, capacity, parts,
    )


def rounded(value):
    return lax.reduce_precision(value, 8, 7)


def halves(value, stage, side):
    axis = value.ndim - 3
    first = lax.index_in_dim(value, 0, axis, keepdims=False)
    second = lax.index_in_dim(value, 1, axis, keepdims=False)
    return jnp.where(side == 0, first, second), jnp.where(side == 0, second, first)


def packed(taps, emb):
    high = rounded(emb)
    pad = jnp.zeros((-(taps.shape[0] + 2) % 8, taps.shape[1]), bf16)
    return jnp.concatenate(
        [rounded(taps).astype(bf16), high.astype(bf16), (emb - high).astype(bf16), pad]
    )


def merged(taps, emb, got):
    count = taps.shape[0]
    high = rounded(emb)
    low = rounded(emb - high)
    got = got.astype(f32)
    taps = rounded(taps) + got[0:count]
    emb = (high + low) + (got[count : count + 1] + got[count + 1 : count + 2])
    return taps, emb


def per_device(
    tiles_in, upstream, pool_weight, slide_cot, adjacency, counts, kernel, norm_gain, w_in, w_out,
    layer_scale,
):
    own = tiles_in[0]
    capacity, side, _, channels = own.shape
    parts = channels // LANES
    hidden = w_in.shape[1]
    pixels = capacity * 64
    wanted = adjacency[0]
    up = upstream.reshape(pixels, channels)
    taps = kernel.reshape(49, channels)
    gain, scale = norm_gain[None, :], layer_scale[None, :]
    edge_shape = (capacity, 3, 8, channels)

    north, south = call(
        edge_kernel, [struct(edge_shape, bf16)] * 2, [VMEM], [own], name="edges"
    )
    north = passed_along(north, "space", 1)
    south = passed_along(south, "space", -1)

    pad, conv, mixed, act_grad, own_sum = call(
        early_kernel,
        [
            struct((parts, capacity, 8, 24, LANES)),
            struct((pixels, channels)),
            struct((pixels, channels + LANES), bf16),
            struct((pixels, hidden)),
            struct((1, channels)),
        ],
        [SMEM] * 3 + [VMEM] * 6,
        [wanted, counts, pool_weight, own, up, slide_cot, taps, scale, w_out],
        flops=2 * pixels * channels * hidden, name="early",
    )
    edge, normed, inv, pre_grad, weight, pooled = call(
        forward_kernel,
        [
            struct((parts, capacity, 6, 24, LANES)),
            struct((pixels, channels)),
            struct((pixels, 1)),
            struct((pixels, hidden), bf16),
            struct((hidden, channels)),
            struct((hidden, LANES)),
        ],
        [SMEM] + [VMEM] * 8,
        [wanted, north, south, conv, taps, gain, w_in, mixed, act_grad],
        flops=4 * pixels * channels * hidden, scratch=[pltpu.VMEM((pixels, channels), f32)],
        name="forward",
    )

    count = lax.axis_size("space")
    stages = count.bit_length() - 1
    place_of = lax.axis_index("space")
    pieces = weight.reshape((2,) * stages + (hidden // count, channels))
    keep, send = halves(pieces, 0, place_of % 2)
    got = swapped(send.astype(bf16), "space", 1)

    grad, grad_north, grad_south, emb = call(
        back_kernel,
        [
            struct((pixels, channels)),
            struct(edge_shape, bf16),
            struct(edge_shape, bf16),
            struct((1, channels)),
        ],
        [SMEM] * 2 + [VMEM] * 9,
        [counts, pool_weight, pre_grad, w_in, normed, inv, gain, pooled, w_out, scale, own_sum],
        flops=2 * pixels * channels * hidden, name="back",
    )
    grad_north = passed_along(grad_north, "space", 1)
    grad_south = passed_along(grad_south, "space", -1)

    tap_grad = call(
        taps_kernel, struct((49, channels)), [VMEM] * 3, [pad, edge, grad],
        scratch=[pltpu.VMEM((49, 8, channels), f32)], name="taps",
    )

    pieces = keep + got.astype(f32)
    for stage in range(1, stages):
        bit = 1 << stage
        keep, send = halves(pieces, stage, (place_of // bit) % 2)
        send = send.astype(bf16)
        if stage == SEPARATE:
            for early in range(SEPARATE):
                tap_grad, emb = merged(
                    tap_grad, emb, swapped(packed(tap_grad, emb), "space", 1 << early)
                )
        if stage >= SEPARATE:
            flat = send.reshape(-1, channels)
            load = swapped(jnp.concatenate([flat, packed(tap_grad, emb)]), "space", bit)
            got = load[0 : flat.shape[0]].reshape(send.shape)
            tap_grad, emb = merged(tap_grad, emb, load[flat.shape[0] :])
        else:
            got = swapped(send, "space", bit)
        pieces = keep + got.astype(f32)
    embedding = emb
    share = pieces
    bit = 1
    while bit < lax.axis_size("dp"):
        share = rounded(share)
        load = swapped(
            jnp.concatenate([share.astype(bf16), packed(tap_grad, emb)]), "dp", bit
        ).astype(f32)
        share = share + load[0 : share.shape[0]]
        tap_grad = rounded(tap_grad) + load[hidden // count : hidden // count + 49]
        bit *= 2

    grad_tiles = call(
        final_kernel, struct((pixels, channels), bf16),
        [SMEM] * 3 + [VMEM] * 6,
        [wanted, counts, pool_weight, grad, grad_north, grad_south, taps, up, slide_cot],
        scratch=[pltpu.VMEM((parts, capacity, 14, 24, LANES), f32)], name="final",
    )
    return (
        embedding,
        grad_tiles.reshape(tiles_in.shape),
        share,
        tap_grad.reshape(kernel.shape),
    )


def solution(mesh):
    return jax.shard_map(
        per_device,
        mesh=mesh,
        in_specs=(
            P("dp", "space", None, None, None),
            P("dp", "space", None, None, None),
            P("dp", "space"),
            P("dp", None),
            P("dp", "space", None),
            P("dp", "space"),
            P(),
            P(),
            P(),
            P(),
            P(),
        ),
        out_specs=(P("dp", None), P("dp", "space", None, None, None), P("space", None), P()),
        check_vma=False,
    )
```

```python
import functools

import jax
import jax.numpy as jnp
from jax import lax
from jax.experimental import pallas as pl
from jax.experimental.pallas import tpu as pltpu
from jax.sharding import PartitionSpec as P

sqrt_half = 0.7071067811865476
inv_root_two_pi = 0.3989422804014327
f32 = jnp.float32
bf16 = jnp.bfloat16
LANES = 128
SEPARATE = 2

VMEM = pl.BlockSpec(memory_space=pltpu.VMEM)
SMEM = pl.BlockSpec(memory_space=pltpu.SMEM)
HBM = pl.BlockSpec(memory_space=pltpu.HBM)
STATE = 56
TAPS = 49
EDGE_COST = 5_000_000_000


def call(body, out_shape, in_specs, args, flops=0, scratch=(), limit=16 << 20, out_specs=None):
    outs = out_shape if isinstance(out_shape, (list, tuple)) else [out_shape]
    total = sum(a.size * a.dtype.itemsize for a in list(args) + list(outs))
    return pl.pallas_call(
        body,
        out_shape=out_shape,
        in_specs=in_specs,
        out_specs=out_specs or jax.tree.map(lambda _: VMEM, out_shape),
        scratch_shapes=scratch,
        compiler_params=pltpu.CompilerParams(vmem_limit_bytes=limit),
        cost_estimate=pl.CostEstimate(flops=flops, bytes_accessed=total, transcendentals=0),
    )(*args)


def struct(shape, dtype=f32):
    return jax.ShapeDtypeStruct(shape, dtype)


def passed_along(value, axis, steps):
    count = lax.axis_size(axis)
    leading, last = (max(0, -steps), min(count, count - steps))
    return lax.ppermute(value, axis, [(source, source + steps) for source in range(leading, last)])


def swapped(value, axis, bit):
    count = lax.axis_size(axis)
    return lax.ppermute(value, axis, [(source, source ^ bit) for source in range(count)])


def valid(entry):
    return jnp.where(entry >= 0, 1.0, 0.0).astype(f32)


def local(entry, capacity):
    return lax.rem(jnp.maximum(entry, 0), capacity)


def place(pad_ref, tile, row, part, value, parts):
    for lane in range(parts):
        pad_ref[lane, tile, row, pl.ds(part * 8, 8), :] = value[:, lane * LANES : (lane + 1) * LANES]


def fill_middle(pad_ref, own_at, adj_ref, capacity, first_row, parts):
    for tile in range(capacity):
        west, east = adj_ref[tile, 2], adj_ref[tile, 3]
        for row in range(8):
            place(pad_ref, tile, first_row + row, 0, own_at(local(west, capacity), row) * valid(west), parts)
            place(pad_ref, tile, first_row + row, 1, own_at(tile, row), parts)
            place(pad_ref, tile, first_row + row, 2, own_at(local(east, capacity), row) * valid(east), parts)


def fill_edge(pad_ref, edge_ref, adj_ref, capacity, entries, first_row, parts):
    for tile in range(capacity):
        for part, entry in enumerate(entries):
            wanted = adj_ref[tile, entry]
            index, keep = local(wanted, capacity), valid(wanted)
            for row in range(3):
                value = edge_ref[index, row].astype(f32) * keep
                place(pad_ref, tile, first_row + row, part, value, parts)


UPPER, LOWER = (4, 0, 5), (6, 1, 7)


def convolve(pads, tap_row, finish, capacity, parts):
    for lane in range(parts):

        def one_tile(tile, _):
            sums = [None] * 8
            for col in range(7):
                taps = [tap_row(row, col, lane) for row in range(7)]
                for ref, rows, base in pads:
                    for held in range(rows):
                        window = ref[lane, tile, held, pl.ds(5 + col, 8), :]
                        for out in range(8):
                            tap = held + base - out
                            if 0 <= tap < 7:
                                term = window * taps[tap]
                                sums[out] = term if sums[out] is None else sums[out] + term
            finish(tile, lane, sums)
            return 0

        lax.fori_loop(0, capacity, one_tile, 0)


def lanes(lane):
    return slice(lane * LANES, (lane + 1) * LANES)


def edge_kernel(tiles_ref, north_ref, south_ref):
    north_ref[...] = tiles_ref[:, 5:8]
    south_ref[...] = tiles_ref[:, 0:3]


def early_kernel(
    adj_ref, counts_ref, pool_ref, cot_ref, scale_ref, kern_ref, tiles_ref, up_ref, w_out_ref,
    pad_ref, conv_ref, mixed_ref, act_grad_ref, own_sum_ref,
):
    capacity, parts = tiles_ref.shape[0], tiles_ref.shape[3] // LANES
    pixels = 64
    channels = tiles_ref.shape[3]
    fill_middle(pad_ref, lambda t, r: tiles_ref[t, r].astype(f32), adj_ref, capacity, 0, parts)
    own_sum = jnp.zeros((1, channels), f32)
    scale = scale_ref[...].reshape(1, channels)
    for tile in range(capacity):
        live = jnp.where(tile < counts_ref[0, 0], 1.0, 0.0).astype(f32)
        pool = pool_ref[0, tile]
        rows = slice(tile * pixels, (tile + 1) * pixels)
        out_grad = live * (up_ref[rows, :].astype(f32) + pool * cot_ref[...] * 0.125)
        mixed_ref[rows, 0:channels] = (out_grad * scale).astype(bf16)
        column = lax.broadcasted_iota(jnp.int32, (pixels, LANES), 1)
        mixed_ref[rows, channels:] = jnp.where(column == tile, 1.0, 0.0).astype(bf16)
        own = tiles_ref[tile].astype(f32)
        own_sum += live * pool * jnp.sum(own.reshape(pixels, channels), axis=0, keepdims=True)
    own_sum_ref[...] = own_sum
    act_grad_ref[...] = lax.dot_general(
        mixed_ref[:, 0:channels], w_out_ref[...], (((1,), (1,)), ((), ())), preferred_element_type=f32
    )

    def finish(tile, lane, sums):
        for row in range(8):
            conv_ref[pl.ds(tile * pixels + row * 8, 8), lanes(lane)] = sums[row]

    convolve(
        [(pad_ref, 8, 3)],
        lambda row, col, lane: kern_ref[row, col : col + 1, lanes(lane)],
        finish, capacity, parts,
    )


def split_pieces(value_ref, rows, place, stage, keep_ref, send_ref):
    side = lax.rem(lax.div(place, 1 << stage), 2)
    for pair in range(value_ref.shape[0] // (2 * rows)):
        here = pl.ds(pair * rows, rows)
        mine = pl.ds(pl.multiple_of((2 * pair + side) * rows, 8), rows)
        other = pl.ds(pl.multiple_of((2 * pair + 1 - side) * rows, 8), rows)
        keep_ref[here, :] = value_ref[mine, :]
        send_ref[here, :] = value_ref[other, :].astype(bf16)


def forward_kernel(
    rows, adj_ref, place_ref, north_ref, south_ref, conv_ref, kern_ref, gain_ref, w_in_ref, mixed_ref, act_grad_ref,
    edge_ref, normed_ref, inv_ref, pre_grad_ref, keep_ref, send_ref, pooled_ref, whole_ref, weight_ref,
):
    capacity, parts = adj_ref.shape[0], conv_ref.shape[1] // LANES
    channels = conv_ref.shape[1]
    pixels = 64
    fill_edge(edge_ref, north_ref, adj_ref, capacity, UPPER, 0, parts)
    fill_edge(edge_ref, south_ref, adj_ref, capacity, LOWER, 3, parts)

    def finish(tile, lane, sums):
        for row in range(8):
            at = pl.ds(tile * pixels + row * 8, 8)
            total = conv_ref[at, lanes(lane)]
            if sums[row] is not None:
                total = total + sums[row]
            whole_ref[at, lanes(lane)] = total

    convolve(
        [(edge_ref.at[:, :, 0:3], 3, 0), (edge_ref.at[:, :, 3:6], 3, 11)],
        lambda row, col, lane: kern_ref[row, col : col + 1, lanes(lane)],
        finish, capacity, parts,
    )
    conv = whole_ref[...]
    centred = conv - jnp.mean(conv, axis=-1, keepdims=True)
    inv_std = lax.rsqrt(jnp.mean(centred * centred, axis=-1, keepdims=True) + 1e-06)
    normed = centred * inv_std
    normed_ref[...] = normed
    inv_ref[...] = inv_std
    lifted = (normed * gain_ref[...].reshape(1, channels)).astype(bf16)
    hidden = w_in_ref.shape[1]
    chunk = hidden // 4 if hidden % 512 == 0 else hidden
    for first in range(0, hidden, chunk):
        at = slice(first, first + chunk)
        pre = jnp.dot(lifted, w_in_ref[:, at], preferred_element_type=f32)
        cdf = 0.5 * (1.0 + lax.erf(pre * sqrt_half))
        activated = (pre * cdf).astype(bf16)
        density = jnp.exp(-0.5 * pre * pre) * inv_root_two_pi
        pre_grad_ref[:, at] = (act_grad_ref[:, at] * (cdf + pre * density)).astype(bf16)
        both = lax.dot_general(
            activated, mixed_ref[...], (((0,), (0,)), ((), ())), preferred_element_type=f32
        )
        weight_ref[at, :] = both[:, 0:channels]
        pooled_ref[at, :] = both[:, channels:]
    split_pieces(weight_ref, rows, place_ref[0, 0], 0, keep_ref, send_ref)


def back_kernel(
    counts_ref, pool_ref, pre_grad_ref, w_in_ref, normed_ref, inv_ref, gain_ref, pooled_ref, w_out_ref,
    scale_ref, own_sum_ref, grad_ref, north_ref, south_ref, emb_ref,
):
    channels = normed_ref.shape[1]
    capacity = north_ref.shape[0]
    lift = lax.dot_general(
        pre_grad_ref[...], w_in_ref[...], (((1,), (1,)), ((), ())), preferred_element_type=f32
    )
    grad_normed = lift * gain_ref[...].reshape(1, channels)
    normed = normed_ref[...]
    grad = inv_ref[...] * (
        grad_normed
        - jnp.mean(grad_normed, axis=-1, keepdims=True)
        - normed * jnp.mean(grad_normed * normed, axis=-1, keepdims=True)
    )
    grad_ref[...] = grad
    shaped = grad.reshape(capacity, 8, 8, channels)
    north_ref[...] = shaped[:, 5:8].astype(bf16)
    south_ref[...] = shaped[:, 0:3].astype(bf16)
    column = lax.broadcasted_iota(jnp.int32, (1, LANES), 1)
    weights = jnp.zeros((1, LANES), f32)
    for tile in range(capacity):
        amount = jnp.where(tile < counts_ref[0, 0], pool_ref[0, tile], 0.0)
        weights = jnp.where(column == tile, amount, weights)
    hidden = jnp.sum(pooled_ref[...] * weights, axis=1, keepdims=True)
    mixed = jnp.sum(hidden * w_out_ref[...].astype(f32), axis=0, keepdims=True)
    emb_ref[...] = (own_sum_ref[...] + scale_ref[...].reshape(1, channels) * mixed) * 0.125


def taps_kernel(pad_ref, edge_ref, grad_ref, emb_ref, state_ref, pack_ref, part_ref):
    parts, capacity = pad_ref.shape[0], pad_ref.shape[1]
    for lane in range(parts):

        def one_column(col):
            def one_tile(tile, sums):
                sums = list(sums)
                grads = [grad_ref[pl.ds(tile * 64 + row * 8, 8), lanes(lane)] for row in range(8)]
                for held in range(14):
                    if 3 <= held < 11:
                        window = pad_ref[lane, tile, held - 3, pl.ds(5 + col, 8), :]
                    else:
                        row = held if held < 3 else held - 8
                        window = edge_ref[lane, tile, row, pl.ds(5 + col, 8), :]
                    for out in range(8):
                        tap = held - out
                        if 0 <= tap < 7:
                            sums[tap] = sums[tap] + window * grads[out]
                return tuple(sums)

            sums = lax.fori_loop(0, capacity, one_tile, tuple(jnp.zeros((8, LANES), f32) for _ in range(7)))
            for row in range(7):
                part_ref[row * 7 + col, :, lanes(lane)] = sums[row]
            return 0

        for col in range(7):
            one_column(col)
    state_ref[0:TAPS, :] = jnp.sum(part_ref[...], axis=1)
    state_ref[TAPS : TAPS + 1, :] = emb_ref[...]
    state_ref[TAPS + 1 :, :] = jnp.zeros((STATE - TAPS - 1, emb_ref.shape[1]), f32)
    pack_ref[...] = packed(state_ref)


def packed(state_ref):
    state = state_ref[...]
    high = state.astype(bf16)
    low = pltpu.roll(state - high.astype(f32), 1, 0)
    row = lax.broadcasted_iota(jnp.int32, state.shape, 0)
    return jnp.where(row == TAPS + 1, low, high.astype(f32)).astype(bf16)


def merged(state_ref, got):
    total = packed(state_ref).astype(f32) + got.astype(f32)
    row = lax.broadcasted_iota(jnp.int32, total.shape, 0)
    moved = pltpu.roll(total, STATE - 1, 0)
    total = jnp.where(row == TAPS, total + moved, total)
    return jnp.where(row > TAPS, 0.0, total)


def state_kernel(state_ref, got_ref, new_ref, pack_ref):
    new_ref[...] = merged(state_ref, got_ref[...])
    pack_ref[...] = packed(new_ref)


def merge_kernel(rows, stage, with_state, joins, symmetric, place_ref, keep_ref, got_ref, *refs):
    count = keep_ref.shape[0]
    refs = list(refs)
    state_ref = refs.pop(0) if with_state else None
    new_ref, send_ref = refs.pop(0), refs.pop(0)
    next_ref = refs.pop(0) if with_state else None
    value = keep_ref[...]
    if symmetric:
        value = value.astype(bf16).astype(f32)
    total = value + got_ref[0:count, :].astype(f32)
    if stage is None:
        new_ref[...] = total
        send_ref[0:count, :] = total.astype(bf16)
        sent = count
    else:
        sum_ref = refs.pop(0)
        sum_ref[...] = total
        split_pieces(sum_ref, rows, place_ref[0, 0], stage, new_ref, send_ref.at[0 : count // 2])
        sent = count // 2
    if with_state:
        next_ref[...] = merged(state_ref, got_ref[count:, :]) if joins else state_ref[...]
        send_ref[sent:, :] = packed(next_ref)


def finish_kernel(keep_ref, got_ref, state_ref, share_ref, taps_ref):
    count = keep_ref.shape[0]
    share_ref[...] = keep_ref[...].astype(bf16).astype(f32) + got_ref[0:count, :].astype(f32)
    total = packed(state_ref).astype(f32) + got_ref[count:, :].astype(f32)
    for row in range(7):
        taps_ref[row] = total[row * 7 : row * 7 + 7, :]


def final_kernel(
    adj_ref, counts_ref, pool_ref, grad_ref, north_ref, south_ref, kern_ref, up_ref, cot_ref,
    out_ref, pad_ref,
):
    capacity, parts = adj_ref.shape[0], grad_ref.shape[1] // LANES

    def own_at(tile, row):
        at = tile * 64 + row * 8
        return grad_ref[pl.ds(at if isinstance(at, int) else pl.multiple_of(at, 8), 8), :]

    fill_middle(pad_ref, own_at, adj_ref, capacity, 3, parts)
    fill_edge(pad_ref, north_ref, adj_ref, capacity, UPPER, 0, parts)
    fill_edge(pad_ref, south_ref, adj_ref, capacity, LOWER, 11, parts)

    def finish(tile, lane, sums):
        live = jnp.where(tile < counts_ref[0, 0], 1.0, 0.0).astype(f32)
        extra = pool_ref[0, tile] * cot_ref[:, lanes(lane)] * 0.125
        for row in range(8):
            at = pl.ds(tile * 64 + row * 8, 8)
            out_grad = live * (up_ref[at, lanes(lane)].astype(f32) + extra)
            out_ref[at, lanes(lane)] = (live * (out_grad + sums[row])).astype(bf16)

    convolve(
        [(pad_ref, 14, 0)],
        lambda row, col, lane: kern_ref[6 - row, 6 - col : 7 - col, lanes(lane)],
        finish, capacity, parts,
    )


def whole_pass(
    tiles_in, upstream, pool_weight, slide_cot, adjacency, counts, kernel, norm_gain, w_in, w_out,
    layer_scale,
):
    own = tiles_in[0]
    capacity, _, _, channels = own.shape
    parts = channels // LANES
    hidden = w_in.shape[1]
    pixels = capacity * 64
    up = upstream.reshape(pixels, channels)
    wanted = adjacency[0]
    edge_shape = (capacity, 3, 8, channels)
    count = lax.axis_size("space")
    stages = count.bit_length() - 1
    rows = hidden // count
    place = lax.axis_index("space").astype(jnp.int32).reshape(1, 1)

    north, south = call(edge_kernel, [struct(edge_shape, bf16)] * 2, [VMEM], [own], flops=EDGE_COST)
    north = passed_along(north, "space", 1)
    south = passed_along(south, "space", -1)

    pad, conv, mixed, act_grad, own_sum = call(
        early_kernel,
        [
            struct((parts, capacity, 8, 24, LANES)),
            struct((pixels, channels)),
            struct((pixels, channels + LANES), bf16),
            struct((pixels, hidden)),
            struct((1, channels)),
        ],
        [SMEM] * 3 + [VMEM] * 6,
        [wanted, counts, pool_weight, slide_cot, layer_scale, kernel, own, up, w_out],
        flops=2 * pixels * channels * hidden,
    )
    edge, normed, inv, pre_grad, keep, send, pooled = call(
        functools.partial(forward_kernel, rows),
        [
            struct((parts, capacity, 6, 24, LANES)),
            struct((pixels, channels)),
            struct((pixels, 1)),
            struct((pixels, hidden), bf16),
            struct((hidden // 2, channels)),
            struct((hidden // 2, channels), bf16),
            struct((hidden, LANES)),
        ],
        [SMEM] * 2 + [VMEM] * 8,
        [wanted, place, north, south, conv, kernel, norm_gain, w_in, mixed, act_grad],
        flops=4 * pixels * channels * hidden,
        scratch=[pltpu.VMEM((pixels, channels), f32), pltpu.VMEM((hidden, channels), f32)],
    )
    got = swapped(send, "space", 1)

    grad, grad_north, grad_south, emb = call(
        back_kernel,
        [
            struct((pixels, channels)),
            struct(edge_shape, bf16),
            struct(edge_shape, bf16),
            struct((1, channels)),
        ],
        [SMEM] * 2 + [VMEM] * 9,
        [counts, pool_weight, pre_grad, w_in, normed, inv, norm_gain, pooled, w_out, layer_scale, own_sum],
        flops=2 * pixels * channels * hidden,
    )
    grad_north = passed_along(grad_north, "space", 1)
    grad_south = passed_along(grad_south, "space", -1)

    state, pack = call(
        taps_kernel, [struct((STATE, channels)), struct((STATE, channels), bf16)],
        [VMEM] * 4, [pad, edge, grad, emb],
        scratch=[pltpu.VMEM((TAPS, 8, channels), f32)],
    )
    for stage in range(min(SEPARATE, stages)):
        new = swapped(pack, "space", 1 << stage)
        state, pack = call(
            state_kernel, [struct((STATE, channels)), struct((STATE, channels), bf16)],
            [VMEM] * 2, [state, new],
        )

    for stage in range(1, stages + 1):
        last = stage == stages
        with_state = stage >= SEPARATE
        held = hidden >> stage
        sent = held if last else held // 2
        shapes = [
            struct((sent, channels)),
            struct((sent + (STATE if with_state else 0), channels), bf16),
        ]
        operands = [place, keep, got]
        if with_state:
            shapes.append(struct((STATE, channels)))
            operands.append(state)
        results = call(
            functools.partial(
                merge_kernel, rows, None if last else stage, with_state, stage > SEPARATE, False
            ),
            shapes, [SMEM] + [VMEM] * (len(operands) - 1), operands,
            scratch=[] if last else [pltpu.VMEM((held, channels), f32)],
        )
        keep, send = results[:2]
        if with_state:
            state = results[2]
        if not last:
            got = swapped(send, "space", 1 << stage)
    embedding = state[TAPS : TAPS + 1]
    groups = lax.axis_size("dp")
    bit = 1
    while bit < groups:
        got = swapped(send, "dp", bit)
        bit *= 2
        if bit < groups:
            keep, send, state = call(
                functools.partial(merge_kernel, rows, None, True, True, True),
                [struct(keep.shape), struct(send.shape, bf16), struct(state.shape)],
                [SMEM] + [VMEM] * 3, [place, keep, got, state],
            )
    share, tap_grad = call(
        finish_kernel, [struct((rows, channels)), struct(kernel.shape)],
        [VMEM] * 3, [keep, got, state],
    )

    grad_tiles = call(
        final_kernel, struct((pixels, channels), bf16),
        [SMEM] * 3 + [VMEM] * 6,
        [wanted, counts, pool_weight, grad, grad_north, grad_south, kernel, up, slide_cot],
        scratch=[pltpu.VMEM((parts, capacity, 14, 24, LANES), f32)],
    )
    return (
        embedding,
        grad_tiles.reshape(tiles_in.shape),
        share,
        tap_grad,
    )


def solution(mesh):
    return jax.shard_map(
        whole_pass,
        mesh=mesh,
        in_specs=(
            P("dp", "space", None, None, None),
            P("dp", "space", None, None, None),
            P("dp", "space"),
            P("dp", None),
            P("dp", "space", None),
            P("dp", "space"),
            P(),
            P(),
            P(),
            P(),
            P(),
        ),
        out_specs=(P("dp", None), P("dp", "space", None, None, None), P("space", None), P()),
        check_vma=False,
    )
```

```python
import functools

import jax
import jax.numpy as jnp
from jax import lax
from jax.experimental import pallas as pl
from jax.experimental.pallas import tpu as pltpu
from jax.sharding import PartitionSpec as P

sqrt_half = 0.7071067811865476
inv_root_two_pi = 0.3989422804014327
f32 = jnp.float32
bf16 = jnp.bfloat16
LANES = 128

VMEM = pl.BlockSpec(memory_space=pltpu.VMEM)
SMEM = pl.BlockSpec(memory_space=pltpu.SMEM)
HBM = pl.BlockSpec(memory_space=pltpu.HBM)
STATE = 56
TAPS = 49
EDGE_COST = 5_000_000_000


def call(body, out_shape, in_specs, args, flops=0, scratch=(), limit=16 << 20, out_specs=None):
    outs = out_shape if isinstance(out_shape, (list, tuple)) else [out_shape]
    total = sum(a.size * a.dtype.itemsize for a in list(args) + list(outs))
    return pl.pallas_call(
        body,
        out_shape=out_shape,
        in_specs=in_specs,
        out_specs=out_specs or jax.tree.map(lambda _: VMEM, out_shape),
        scratch_shapes=scratch,
        compiler_params=pltpu.CompilerParams(vmem_limit_bytes=limit),
        cost_estimate=pl.CostEstimate(flops=flops, bytes_accessed=total, transcendentals=0),
    )(*args)


def struct(shape, dtype=f32):
    return jax.ShapeDtypeStruct(shape, dtype)


def swapped(value, axis, bit):
    count = lax.axis_size(axis)
    return lax.ppermute(value, axis, [(source, source ^ bit) for source in range(count)])


def crossed(value, axis):
    count = lax.axis_size(axis)
    firsts = range(1, count - 1, 2)
    return lax.ppermute(
        value, axis, [(n, n + 1) for n in firsts] + [(n + 1, n) for n in firsts]
    )


def valid(entry):
    return jnp.where(entry >= 0, 1.0, 0.0).astype(f32)


def local(entry, capacity):
    return lax.rem(jnp.maximum(entry, 0), capacity)


def place(pad_ref, tile, row, part, value, parts):
    for lane in range(parts):
        pad_ref[lane, tile, row, pl.ds(part * 8, 8), :] = value[:, lane * LANES : (lane + 1) * LANES]


def fill_middle(pad_ref, own_at, adj_ref, capacity, first_row, parts):
    for tile in range(capacity):
        west, east = adj_ref[tile, 2], adj_ref[tile, 3]
        for row in range(8):
            place(pad_ref, tile, first_row + row, 0, own_at(local(west, capacity), row) * valid(west), parts)
            place(pad_ref, tile, first_row + row, 1, own_at(tile, row), parts)
            place(pad_ref, tile, first_row + row, 2, own_at(local(east, capacity), row) * valid(east), parts)


def fill_edge(pad_ref, odd_ref, even_ref, odd, adj_ref, capacity, entries, first_row, parts):
    for tile in range(capacity):
        for part, entry in enumerate(entries):
            wanted = adj_ref[tile, entry]
            index, keep = local(wanted, capacity), valid(wanted)
            for row in range(3):
                value = odd_ref[index, row].astype(f32) * (keep * odd)
                value = value + even_ref[index, row].astype(f32) * (keep * (1.0 - odd))
                place(pad_ref, tile, first_row + row, part, value, parts)


def is_odd(place_ref):
    return lax.rem(place_ref[0, 0], 2).astype(f32)


UPPER, LOWER = (4, 0, 5), (6, 1, 7)


def convolve(pads, tap_row, finish, capacity, parts):
    for lane in range(parts):

        def one_tile(tile, _):
            sums = [None] * 8
            for col in range(7):
                taps = [tap_row(row, col, lane) for row in range(7)]
                for ref, rows, base in pads:
                    for held in range(rows):
                        window = ref[lane, tile, held, pl.ds(5 + col, 8), :]
                        for out in range(8):
                            tap = held + base - out
                            if 0 <= tap < 7:
                                term = window * taps[tap]
                                sums[out] = term if sums[out] is None else sums[out] + term
            finish(tile, lane, sums)
            return 0

        lax.fori_loop(0, capacity, one_tile, 0)


def lanes(lane):
    return slice(lane * LANES, (lane + 1) * LANES)


def swap_edges(last, first, odd, core_ref, cross_ref):
    core_ref[...] = (first * odd + last * (1.0 - odd)).astype(bf16)
    cross_ref[...] = (last * odd + first * (1.0 - odd)).astype(bf16)


def edge_kernel(place_ref, tiles_ref, core_ref, cross_ref):
    swap_edges(
        tiles_ref[:, 5:8].astype(f32), tiles_ref[:, 0:3].astype(f32), is_odd(place_ref), core_ref, cross_ref
    )


def early_kernel(
    adj_ref, counts_ref, pool_ref, cot_ref, scale_ref, kern_ref, tiles_ref, up_ref, w_out_ref,
    pad_ref, conv_ref, mixed_ref, act_grad_ref, own_sum_ref,
):
    capacity, parts = tiles_ref.shape[0], tiles_ref.shape[3] // LANES
    pixels = 64
    channels = tiles_ref.shape[3]
    fill_middle(pad_ref, lambda t, r: tiles_ref[t, r].astype(f32), adj_ref, capacity, 0, parts)
    own_sum = jnp.zeros((1, channels), f32)
    scale = scale_ref[...].reshape(1, channels)
    for tile in range(capacity):
        live = jnp.where(tile < counts_ref[0, 0], 1.0, 0.0).astype(f32)
        pool = pool_ref[0, tile]
        rows = slice(tile * pixels, (tile + 1) * pixels)
        out_grad = live * (up_ref[rows, :].astype(f32) + pool * cot_ref[...] * 0.125)
        mixed_ref[rows, 0:channels] = (out_grad * scale).astype(bf16)
        column = lax.broadcasted_iota(jnp.int32, (pixels, LANES), 1)
        mixed_ref[rows, channels:] = jnp.where(column == tile, 1.0, 0.0).astype(bf16)
        own = tiles_ref[tile].astype(f32)
        own_sum += live * pool * jnp.sum(own.reshape(pixels, channels), axis=0, keepdims=True)
    own_sum_ref[...] = own_sum
    act_grad_ref[...] = lax.dot_general(
        mixed_ref[:, 0:channels], w_out_ref[...], (((1,), (1,)), ((), ())), preferred_element_type=f32
    )

    def finish(tile, lane, sums):
        for row in range(8):
            conv_ref[pl.ds(tile * pixels + row * 8, 8), lanes(lane)] = sums[row]

    convolve(
        [(pad_ref, 8, 3)],
        lambda row, col, lane: kern_ref[row, col : col + 1, lanes(lane)],
        finish, capacity, parts,
    )


def split_pieces(value_ref, rows, place_ref, stage, keep_ref, send_ref):
    side = lax.rem(lax.div(place_ref[0, 0], 1 << stage), 2)
    for pair in range(value_ref.shape[0] // (2 * rows)):
        here = pl.ds(pair * rows, rows)
        mine = pl.ds(pl.multiple_of((2 * pair + side) * rows, 8), rows)
        other = pl.ds(pl.multiple_of((2 * pair + 1 - side) * rows, 8), rows)
        keep_ref[here, :] = value_ref[mine, :]
        send_ref[here, :] = value_ref[other, :].astype(bf16)


def forward_kernel(
    rows, adj_ref, place_ref, core_ref, cross_ref, conv_ref, kern_ref, gain_ref, w_in_ref, mixed_ref, act_grad_ref,
    edge_ref, normed_ref, inv_ref, pre_grad_ref, keep_ref, send_ref, pooled_ref, whole_ref, weight_ref,
):
    capacity, parts = adj_ref.shape[0], conv_ref.shape[1] // LANES
    channels = conv_ref.shape[1]
    pixels = 64
    odd = is_odd(place_ref)
    fill_edge(edge_ref, core_ref, cross_ref, odd, adj_ref, capacity, UPPER, 0, parts)
    fill_edge(edge_ref, cross_ref, core_ref, odd, adj_ref, capacity, LOWER, 3, parts)

    def finish(tile, lane, sums):
        for row in range(8):
            at = pl.ds(tile * pixels + row * 8, 8)
            total = conv_ref[at, lanes(lane)]
            if sums[row] is not None:
                total = total + sums[row]
            whole_ref[at, lanes(lane)] = total

    convolve(
        [(edge_ref.at[:, :, 0:3], 3, 0), (edge_ref.at[:, :, 3:6], 3, 11)],
        lambda row, col, lane: kern_ref[row, col : col + 1, lanes(lane)],
        finish, capacity, parts,
    )
    conv = whole_ref[...]
    centred = conv - jnp.mean(conv, axis=-1, keepdims=True)
    inv_std = lax.rsqrt(jnp.mean(centred * centred, axis=-1, keepdims=True) + 1e-06)
    normed = centred * inv_std
    normed_ref[...] = normed
    inv_ref[...] = inv_std
    lifted = (normed * gain_ref[...].reshape(1, channels)).astype(bf16)
    hidden = w_in_ref.shape[1]
    chunk = hidden // 4 if hidden % 512 == 0 else hidden
    for first in range(0, hidden, chunk):
        at = slice(first, first + chunk)
        pre = jnp.dot(lifted, w_in_ref[:, at], preferred_element_type=f32)
        cdf = 0.5 * (1.0 + lax.erf(pre * sqrt_half))
        activated = (pre * cdf).astype(bf16)
        density = jnp.exp(-0.5 * pre * pre) * inv_root_two_pi
        pre_grad_ref[:, at] = (act_grad_ref[:, at] * (cdf + pre * density)).astype(bf16)
        both = lax.dot_general(
            activated, mixed_ref[...], (((0,), (0,)), ((), ())), preferred_element_type=f32
        )
        weight_ref[at, :] = both[:, 0:channels]
        pooled_ref[at, :] = both[:, channels:]
    split_pieces(weight_ref, rows, place_ref, 0, keep_ref, send_ref)


def back_kernel(
    place_ref, counts_ref, pool_ref, pre_grad_ref, w_in_ref, normed_ref, inv_ref, gain_ref, pooled_ref, w_out_ref,
    scale_ref, own_sum_ref, grad_ref, core_ref, cross_ref, emb_ref,
):
    channels = normed_ref.shape[1]
    capacity = core_ref.shape[0]
    lift = lax.dot_general(
        pre_grad_ref[...], w_in_ref[...], (((1,), (1,)), ((), ())), preferred_element_type=f32
    )
    grad_normed = lift * gain_ref[...].reshape(1, channels)
    normed = normed_ref[...]
    grad = inv_ref[...] * (
        grad_normed
        - jnp.mean(grad_normed, axis=-1, keepdims=True)
        - normed * jnp.mean(grad_normed * normed, axis=-1, keepdims=True)
    )
    grad_ref[...] = grad
    shaped = grad.reshape(capacity, 8, 8, channels)
    swap_edges(shaped[:, 5:8], shaped[:, 0:3], is_odd(place_ref), core_ref, cross_ref)
    column = lax.broadcasted_iota(jnp.int32, (1, LANES), 1)
    weights = jnp.zeros((1, LANES), f32)
    for tile in range(capacity):
        amount = jnp.where(tile < counts_ref[0, 0], pool_ref[0, tile], 0.0)
        weights = jnp.where(column == tile, amount, weights)
    hidden = jnp.sum(pooled_ref[...] * weights, axis=1, keepdims=True)
    mixed = jnp.sum(hidden * w_out_ref[...].astype(f32), axis=0, keepdims=True)
    emb_ref[...] = (own_sum_ref[...] + scale_ref[...].reshape(1, channels) * mixed) * 0.125


def taps_kernel(pad_ref, edge_ref, grad_ref, emb_ref, state_ref, pack_ref, part_ref):
    parts, capacity = pad_ref.shape[0], pad_ref.shape[1]
    for lane in range(parts):

        def one_column(col):
            def one_tile(tile, sums):
                sums = list(sums)
                grads = [grad_ref[pl.ds(tile * 64 + row * 8, 8), lanes(lane)] for row in range(8)]
                for held in range(14):
                    if 3 <= held < 11:
                        window = pad_ref[lane, tile, held - 3, pl.ds(5 + col, 8), :]
                    else:
                        row = held if held < 3 else held - 8
                        window = edge_ref[lane, tile, row, pl.ds(5 + col, 8), :]
                    for out in range(8):
                        tap = held - out
                        if 0 <= tap < 7:
                            sums[tap] = sums[tap] + window * grads[out]
                return tuple(sums)

            sums = lax.fori_loop(0, capacity, one_tile, tuple(jnp.zeros((8, LANES), f32) for _ in range(7)))
            for row in range(7):
                part_ref[row * 7 + col, :, lanes(lane)] = sums[row]
            return 0

        for col in range(7):
            one_column(col)
    state_ref[0:TAPS, :] = jnp.sum(part_ref[...], axis=1)
    state_ref[TAPS : TAPS + 1, :] = emb_ref[...]
    state_ref[TAPS + 1 :, :] = jnp.zeros((STATE - TAPS - 1, emb_ref.shape[1]), f32)
    pack_ref[...] = packed(state_ref)


def packed(state_ref):
    state = state_ref[...]
    high = state.astype(bf16)
    low = pltpu.roll(state - high.astype(f32), 1, 0)
    row = lax.broadcasted_iota(jnp.int32, state.shape, 0)
    return jnp.where(row == TAPS + 1, low, high.astype(f32)).astype(bf16)


def merged(state_ref, got, with_embedding=True):
    total = packed(state_ref).astype(f32) + got.astype(f32)
    row = lax.broadcasted_iota(jnp.int32, total.shape, 0)
    if with_embedding:
        embedding = total + pltpu.roll(total, STATE - 1, 0)
    else:
        embedding = state_ref[...]
    return jnp.where(row < TAPS, total, jnp.where(row == TAPS, embedding, 0.0))


def state_kernel(with_embedding, state_ref, got_ref, new_ref, pack_ref):
    new_ref[...] = merged(state_ref, got_ref[...], with_embedding)
    pack_ref[...] = packed(new_ref)


def merge_kernel(splits, terms, place_ref, *refs):
    sums, refs = refs[: 2 * terms], refs[2 * terms :]
    outs = max(1, len(splits))
    keeps, sends, sum_ref = refs[0 : 2 * outs : 2], refs[1 : 2 * outs : 2], refs[2 * outs]
    first = 0
    for keep_ref, got_ref in zip(sums[0::2], sums[1::2]):
        count = keep_ref.shape[0]
        sum_ref[first : first + count, :] = keep_ref[...] + got_ref[...].astype(f32)
        first += count
    for keep_ref, send_ref, (start, count, rows, bit) in zip(keeps, sends, splits):
        split_pieces(sum_ref.at[start : start + count], rows, place_ref, bit, keep_ref, send_ref)
    if not splits:
        keeps[0][...] = sum_ref[...]
        sends[0][...] = sum_ref[...].astype(bf16)


def pair_kernel(keep_ref, got_ref, new_ref, send_ref):
    total = keep_ref[...].astype(bf16).astype(f32) + got_ref[...].astype(f32)
    new_ref[...] = total
    send_ref[...] = total.astype(bf16)


def finish_kernel(keep_ref, got_ref, state_ref, new_ref, share_ref, taps_ref, emb_ref):
    share_ref[...] = keep_ref[...].astype(bf16).astype(f32) + got_ref[...].astype(f32)
    total = merged(state_ref, new_ref[...])
    for row in range(7):
        taps_ref[row] = total[row * 7 : row * 7 + 7, :]
    emb_ref[...] = total[TAPS : TAPS + 1, :]


def final_kernel(
    adj_ref, place_ref, counts_ref, pool_ref, grad_ref, core_ref, cross_ref, kern_ref, up_ref, cot_ref,
    out_ref, pad_ref,
):
    capacity, parts = adj_ref.shape[0], grad_ref.shape[1] // LANES

    def own_at(tile, row):
        at = tile * 64 + row * 8
        return grad_ref[pl.ds(at if isinstance(at, int) else pl.multiple_of(at, 8), 8), :]

    fill_middle(pad_ref, own_at, adj_ref, capacity, 3, parts)
    odd = is_odd(place_ref)
    fill_edge(pad_ref, core_ref, cross_ref, odd, adj_ref, capacity, UPPER, 0, parts)
    fill_edge(pad_ref, cross_ref, core_ref, odd, adj_ref, capacity, LOWER, 11, parts)

    def finish(tile, lane, sums):
        live = jnp.where(tile < counts_ref[0, 0], 1.0, 0.0).astype(f32)
        extra = pool_ref[0, tile] * cot_ref[:, lanes(lane)] * 0.125
        for row in range(8):
            at = pl.ds(tile * 64 + row * 8, 8)
            out_grad = live * (up_ref[at, lanes(lane)].astype(f32) + extra)
            out_ref[at, lanes(lane)] = (live * (out_grad + sums[row])).astype(bf16)

    convolve(
        [(pad_ref, 14, 0)],
        lambda row, col, lane: kern_ref[6 - row, 6 - col : 7 - col, lanes(lane)],
        finish, capacity, parts,
    )


def whole_pass(
    tiles_in, upstream, pool_weight, slide_cot, adjacency, counts, kernel, norm_gain, w_in, w_out,
    layer_scale,
):
    own = tiles_in[0]
    capacity, _, _, channels = own.shape
    parts = channels // LANES
    hidden = w_in.shape[1]
    pixels = capacity * 64
    up = upstream.reshape(pixels, channels)
    wanted = adjacency[0]
    edge_shape = (capacity, 3, 8, channels)
    count = lax.axis_size("space")
    stages = count.bit_length() - 1
    rows = hidden // count
    place = lax.axis_index("space").astype(jnp.int32).reshape(1, 1)

    core, cross = call(edge_kernel, [struct(edge_shape, bf16)] * 2, [SMEM, VMEM], [place, own], flops=EDGE_COST)
    cross = crossed(cross, "space")
    core = swapped(core, "space", 1)

    pad, conv, mixed, act_grad, own_sum = call(
        early_kernel,
        [
            struct((parts, capacity, 8, 24, LANES)),
            struct((pixels, channels)),
            struct((pixels, channels + LANES), bf16),
            struct((pixels, hidden)),
            struct((1, channels)),
        ],
        [SMEM] * 3 + [VMEM] * 6,
        [wanted, counts, pool_weight, slide_cot, layer_scale, kernel, own, up, w_out],
        flops=2 * pixels * channels * hidden,
    )
    edge, normed, inv, pre_grad, keep, send, pooled = call(
        functools.partial(forward_kernel, rows),
        [
            struct((parts, capacity, 6, 24, LANES)),
            struct((pixels, channels)),
            struct((pixels, 1)),
            struct((pixels, hidden), bf16),
            struct((hidden // 2, channels)),
            struct((hidden // 2, channels), bf16),
            struct((hidden, LANES)),
        ],
        [SMEM] * 2 + [VMEM] * 8,
        [wanted, place, core, cross, conv, kernel, norm_gain, w_in, mixed, act_grad],
        flops=4 * pixels * channels * hidden,
        scratch=[pltpu.VMEM((pixels, channels), f32), pltpu.VMEM((hidden, channels), f32)],
    )
    got = swapped(send, "space", 1)

    grad, core, cross, emb = call(
        back_kernel,
        [
            struct((pixels, channels)),
            struct(edge_shape, bf16),
            struct(edge_shape, bf16),
            struct((1, channels)),
        ],
        [SMEM] * 3 + [VMEM] * 9,
        [place, counts, pool_weight, pre_grad, w_in, normed, inv, norm_gain, pooled, w_out, layer_scale, own_sum],
        flops=2 * pixels * channels * hidden,
    )
    cross = crossed(cross, "space")
    core = swapped(core, "space", 1)

    def merge(parts_, splits):
        held = sum(keep.shape[0] for keep, _ in parts_)
        shapes = []
        for size in [count // 2 for _, count, _, _ in splits] or [held]:
            shapes += [struct((size, channels)), struct((size, channels), bf16)]
        operands = [array for pair in parts_ for array in pair]
        out = call(
            functools.partial(merge_kernel, splits, len(parts_)), shapes,
            [SMEM] + [VMEM] * len(operands), [place] + operands,
            scratch=[pltpu.VMEM((held, channels), f32)],
        )
        return list(zip(out[0::2], out[1::2]))

    half = hidden // 4
    (keep_a, send_a), (keep_b, send_b) = merge([(keep, got)], [(0, half, rows, 1), (half, half, 2 * rows, 2)])
    got_a = swapped(send_a, "space", 2)
    got_b = swapped(send_b, "space", 4)
    half //= 2
    (keep_a, send_a), (keep_b, send_b) = merge(
        [(keep_a, got_a), (keep_b, got_b)], [(0, half, rows, 2), (half, half, rows, 1)]
    )
    got_a = swapped(send_a, "space", 4)
    got_b = swapped(send_b, "space", 2)
    held = [(keep_a, got_a), (keep_b, got_b)]
    for stage in range(3, stages):
        size = hidden >> stage
        ((keep, send),) = merge(held, [(0, size, rows, stage)])
        got = swapped(send, "space", 1 << stage)
        held = [(keep, got)]
    ((share, send),) = merge(held, [])
    groups = lax.axis_size("dp")
    bit = 1
    while bit < groups:
        got = swapped(send, "dp", bit)
        bit *= 2
        if bit < groups:
            share, send = call(pair_kernel, [struct(share.shape), struct(send.shape, bf16)], [VMEM] * 2, [share, got])

    state, pack = call(
        taps_kernel, [struct((STATE, channels)), struct((STATE, channels), bf16)],
        [VMEM] * 4, [pad, edge, grad, emb],
        scratch=[pltpu.VMEM((TAPS, 8, channels), f32)],
    )
    steps = [("space", 1)] + [("dp", 1 << n) for n in range(groups.bit_length() - 1)]
    steps += [("space", 1 << n) for n in range(1, stages)]
    for axis, bit in steps:
        new = swapped(pack, axis, bit)
        if (axis, bit) != steps[-1]:
            state, pack = call(
                functools.partial(state_kernel, axis == "space"),
                [struct((STATE, channels)), struct((STATE, channels), bf16)],
                [VMEM] * 2, [state, new],
            )

    share, tap_grad, embedding = call(
        finish_kernel, [struct((rows, channels)), struct(kernel.shape), struct((1, channels))],
        [VMEM] * 4, [share, got, state, new],
    )

    grad_tiles = call(
        final_kernel, struct((pixels, channels), bf16),
        [SMEM] * 4 + [VMEM] * 6,
        [wanted, place, counts, pool_weight, grad, core, cross, kernel, up, slide_cot],
        scratch=[pltpu.VMEM((parts, capacity, 14, 24, LANES), f32)],
    )
    return (
        embedding,
        grad_tiles.reshape(tiles_in.shape),
        share,
        tap_grad,
    )


def solution(mesh):
    return jax.shard_map(
        whole_pass,
        mesh=mesh,
        in_specs=(
            P("dp", "space", None, None, None),
            P("dp", "space", None, None, None),
            P("dp", "space"),
            P("dp", None),
            P("dp", "space", None),
            P("dp", "space"),
            P(),
            P(),
            P(),
            P(),
            P(),
        ),
        out_specs=(P("dp", None), P("dp", "space", None, None, None), P("space", None), P()),
        check_vma=False,
    )
```

```python
import functools

import jax
import jax.numpy as jnp
from jax import lax
from jax.experimental import pallas as pl
from jax.experimental.pallas import tpu as pltpu
from jax.sharding import PartitionSpec as P

sqrt_half = 0.7071067811865476
inv_root_two_pi = 0.3989422804014327
f32 = jnp.float32
bf16 = jnp.bfloat16
LANES = 128

VMEM = pl.BlockSpec(memory_space=pltpu.VMEM)
SMEM = pl.BlockSpec(memory_space=pltpu.SMEM)
HBM = pl.BlockSpec(memory_space=pltpu.HBM)
STATE = 56
TAPS = 49
CHUNK = 384
BACK_CHUNK = 512
EDGE_COST = 5_000_000_000


def call(body, out_shape, in_specs, args, flops=0, scratch=(), limit=16 << 20, out_specs=None):
    outs = out_shape if isinstance(out_shape, (list, tuple)) else [out_shape]
    total = sum(a.size * a.dtype.itemsize for a in list(args) + list(outs))
    return pl.pallas_call(
        body,
        out_shape=out_shape,
        in_specs=in_specs,
        out_specs=out_specs or jax.tree.map(lambda _: VMEM, out_shape),
        scratch_shapes=scratch,
        compiler_params=pltpu.CompilerParams(vmem_limit_bytes=limit),
        cost_estimate=pl.CostEstimate(flops=flops, bytes_accessed=total, transcendentals=0),
    )(*args)


def struct(shape, dtype=f32):
    return jax.ShapeDtypeStruct(shape, dtype)


def swapped(value, axis, bit):
    count = lax.axis_size(axis)
    return lax.ppermute(value, axis, [(source, source ^ bit) for source in range(count)])


def crossed(value, axis):
    count = lax.axis_size(axis)
    firsts = range(1, count - 1, 2)
    return lax.ppermute(
        value, axis, [(n, n + 1) for n in firsts] + [(n + 1, n) for n in firsts]
    )


def valid(entry):
    return jnp.where(entry >= 0, 1.0, 0.0).astype(f32)


def local(entry, capacity):
    return lax.rem(jnp.maximum(entry, 0), capacity)


def place(pad_ref, tile, row, part, value, parts):
    for lane in range(parts):
        pad_ref[lane, tile, row, pl.ds(part * 8, 8), :] = value[:, lane * LANES : (lane + 1) * LANES]


def fill_middle(pad_ref, own_at, adj_ref, capacity, first_row, parts):
    for tile in range(capacity):
        west, east = adj_ref[tile, 2], adj_ref[tile, 3]
        for row in range(8):
            place(pad_ref, tile, first_row + row, 0, own_at(local(west, capacity), row) * valid(west), parts)
            place(pad_ref, tile, first_row + row, 1, own_at(tile, row), parts)
            place(pad_ref, tile, first_row + row, 2, own_at(local(east, capacity), row) * valid(east), parts)


def fill_edge(pad_ref, odd_ref, even_ref, odd, adj_ref, capacity, entries, first_row, parts):
    for tile in range(capacity):
        for part, entry in enumerate(entries):
            wanted = adj_ref[tile, entry]
            index, keep = local(wanted, capacity), valid(wanted)
            for row in range(3):
                value = odd_ref[index, row].astype(f32) * (keep * odd)
                value = value + even_ref[index, row].astype(f32) * (keep * (1.0 - odd))
                place(pad_ref, tile, first_row + row, part, value, parts)


def is_live(counts_ref, tile):
    return jnp.where(tile < counts_ref[...], 1.0, 0.0).astype(f32)


def is_odd(place_ref):
    return lax.rem(place_ref[0, 0], 2).astype(f32)


UPPER, LOWER = (4, 0, 5), (6, 1, 7)


def convolve(pads, tap_row, finish, capacity, parts):
    for lane in range(parts):

        def one_tile(tile):
            sums = [None] * 8
            for col in range(7):
                taps = [tap_row(row, col, lane) for row in range(7)]
                for ref, rows, base in pads:
                    for held in range(rows):
                        window = ref[lane, tile, held, pl.ds(5 + col, 8), :]
                        for out in range(8):
                            tap = held + base - out
                            if 0 <= tap < 7:
                                term = window * taps[tap]
                                sums[out] = term if sums[out] is None else sums[out] + term
            finish(tile, lane, sums)
            return 0

        for tile in range(capacity):
            one_tile(tile)


def lanes(lane):
    return slice(lane * LANES, (lane + 1) * LANES)


def swap_edges(last, first, odd, core_ref, cross_ref):
    core_ref[...] = (first * odd + last * (1.0 - odd)).astype(bf16)
    cross_ref[...] = (last * odd + first * (1.0 - odd)).astype(bf16)


def edge_kernel(place_ref, counts_ref, tiles_ref, core_ref, cross_ref):
    swap_edges(
        tiles_ref[:, 5:8].astype(f32), tiles_ref[:, 0:3].astype(f32), is_odd(place_ref), core_ref, cross_ref
    )


def early_kernel(
    adj_ref, counts_ref, pool_ref, cot_ref, scale_ref, kern_ref, tiles_ref, up_ref, w_out_ref,
    pad_ref, conv_ref, mixed_ref, act_grad_ref, own_sum_ref,
):
    capacity, parts = tiles_ref.shape[0], tiles_ref.shape[3] // LANES
    pixels = 64
    channels = tiles_ref.shape[3]
    fill_middle(pad_ref, lambda t, r: tiles_ref[t, r].astype(f32), adj_ref, capacity, 0, parts)
    own_sum = jnp.zeros((1, channels), f32)
    scale = scale_ref[...].reshape(1, channels)
    for tile in range(capacity):
        live = is_live(counts_ref, tile)
        pool = pool_ref[0, tile]
        rows = slice(tile * pixels, (tile + 1) * pixels)
        out_grad = live * (up_ref[rows, :].astype(f32) + pool * cot_ref[...] * 0.125)
        mixed_ref[rows, 0:channels] = (out_grad * scale).astype(bf16)
        column = lax.broadcasted_iota(jnp.int32, (pixels, LANES), 1)
        mixed_ref[rows, channels:] = jnp.where(column == tile, 1.0, 0.0).astype(bf16)
        own = tiles_ref[tile].astype(f32)
        own_sum += live * pool * jnp.sum(own.reshape(pixels, channels), axis=0, keepdims=True)
    own_sum_ref[...] = own_sum
    act_grad_ref[...] = lax.dot_general(
        mixed_ref[:, 0:channels], w_out_ref[...], (((1,), (1,)), ((), ())), preferred_element_type=f32
    )

    def finish(tile, lane, sums):
        for row in range(8):
            conv_ref[pl.ds(tile * pixels + row * 8, 8), lanes(lane)] = sums[row]

    convolve(
        [(pad_ref, 8, 3)],
        lambda row, col, lane: kern_ref[row, col : col + 1, lanes(lane)],
        finish, capacity, parts,
    )


def split_pieces(value_ref, rows, place_ref, stage, keep_ref, send_ref):
    side = lax.rem(lax.div(place_ref[0, 0], 1 << stage), 2)
    for pair in range(value_ref.shape[0] // (2 * rows)):
        here = pl.ds(pair * rows, rows)
        mine = pl.ds(pl.multiple_of((2 * pair + side) * rows, 8), rows)
        other = pl.ds(pl.multiple_of((2 * pair + 1 - side) * rows, 8), rows)
        keep_ref[here, :] = value_ref[mine, :]
        send_ref[here, :] = value_ref[other, :].astype(bf16)


def forward_kernel(
    rows, adj_ref, place_ref, core_ref, cross_ref, conv_ref, kern_ref, gain_ref, w_in_ref, mixed_ref,
    edge_ref, normed_ref, inv_ref, pre_ref, cdf_ref, keep_ref, send_ref, pooled_ref, whole_ref,
):
    capacity, parts = adj_ref.shape[0], conv_ref.shape[1] // LANES
    channels = conv_ref.shape[1]
    pixels = 64
    odd = is_odd(place_ref)
    fill_edge(edge_ref, core_ref, cross_ref, odd, adj_ref, capacity, UPPER, 0, parts)
    fill_edge(edge_ref, cross_ref, core_ref, odd, adj_ref, capacity, LOWER, 3, parts)

    def finish(tile, lane, sums):
        for row in range(8):
            at = pl.ds(tile * pixels + row * 8, 8)
            total = conv_ref[at, lanes(lane)]
            if sums[row] is not None:
                total = total + sums[row]
            whole_ref[at, lanes(lane)] = total

    convolve(
        [(edge_ref.at[:, :, 0:3], 3, 0), (edge_ref.at[:, :, 3:6], 3, 11)],
        lambda row, col, lane: kern_ref[row, col : col + 1, lanes(lane)],
        finish, capacity, parts,
    )
    conv = whole_ref[...]
    centred = conv - jnp.mean(conv, axis=-1, keepdims=True)
    inv_std = lax.rsqrt(jnp.mean(centred * centred, axis=-1, keepdims=True) + 1e-06)
    normed = centred * inv_std
    normed_ref[...] = normed
    inv_ref[...] = inv_std
    lifted = (normed * gain_ref[...].reshape(1, channels)).astype(bf16)
    hidden = w_in_ref.shape[1]
    side = lax.rem(place_ref[0, 0], 2)
    chunk = CHUNK if hidden % CHUNK == 0 and CHUNK % (2 * rows) == 0 else hidden

    def project(first):
        return jnp.dot(lifted, w_in_ref[:, first : first + chunk], preferred_element_type=f32)

    following = project(0)
    for first in range(0, hidden, chunk):
        at = slice(first, first + chunk)
        pre = following
        if first + chunk < hidden:
            following = project(first + chunk)
        cdf = 0.5 * (1.0 + lax.erf(pre * sqrt_half))
        pre_ref[:, at] = pre
        cdf_ref[:, at] = cdf
        activated = (pre * cdf).astype(bf16)
        both = lax.dot_general(
            activated, mixed_ref[...], (((0,), (0,)), ((), ())), preferred_element_type=f32
        )
        pooled_ref[at, :] = both[:, channels:]
        for block in range(0, chunk, 2 * rows):
            even = both[block : block + rows, 0:channels]
            odd_rows = both[block + rows : block + 2 * rows, 0:channels]
            out = pl.ds((first + block) // 2, rows)
            keep_ref[out, :] = jnp.where(side == 0, even, odd_rows)
            send_ref[out, :] = jnp.where(side == 0, odd_rows, even).astype(bf16)


def back_kernel(
    place_ref, counts_ref, pool_ref, pre_ref, cdf_ref, act_grad_ref, w_in_ref, normed_ref, inv_ref, gain_ref, pooled_ref, w_out_ref,
    scale_ref, own_sum_ref, grad_ref, core_ref, cross_ref, emb_ref,
):
    channels = normed_ref.shape[1]
    capacity = core_ref.shape[0]
    hidden = w_in_ref.shape[1]
    chunk = BACK_CHUNK if hidden % BACK_CHUNK == 0 else hidden
    lift = None
    for first in range(0, hidden, chunk):
        at = slice(first, first + chunk)
        pre = pre_ref[:, at]
        density = jnp.exp(-0.5 * pre * pre) * inv_root_two_pi
        pre_grad = (act_grad_ref[:, at] * (cdf_ref[:, at] + pre * density)).astype(bf16)
        term = lax.dot_general(
            pre_grad, w_in_ref[:, at], (((1,), (1,)), ((), ())), preferred_element_type=f32
        )
        lift = term if lift is None else lift + term
    grad_normed = lift * gain_ref[...].reshape(1, channels)
    normed = normed_ref[...]
    grad = inv_ref[...] * (
        grad_normed
        - jnp.mean(grad_normed, axis=-1, keepdims=True)
        - normed * jnp.mean(grad_normed * normed, axis=-1, keepdims=True)
    )
    grad_ref[...] = grad
    shaped = grad.reshape(capacity, 8, 8, channels)
    swap_edges(shaped[:, 5:8], shaped[:, 0:3], is_odd(place_ref), core_ref, cross_ref)
    column = lax.broadcasted_iota(jnp.int32, (1, LANES), 1)
    weights = jnp.zeros((1, LANES), f32)
    for tile in range(capacity):
        amount = is_live(counts_ref, tile) * pool_ref[0, tile]
        weights = jnp.where(column == tile, amount, weights)
    hidden = jnp.sum(pooled_ref[...] * weights, axis=1, keepdims=True)
    mixed = jnp.sum(hidden * w_out_ref[...].astype(f32), axis=0, keepdims=True)
    emb_ref[...] = (own_sum_ref[...] + scale_ref[...].reshape(1, channels) * mixed) * 0.125


def taps_kernel(pad_ref, edge_ref, grad_ref, emb_ref, state_ref, pack_ref, part_ref):
    parts, capacity = pad_ref.shape[0], pad_ref.shape[1]
    for lane in range(parts):

        def one_column(col):
            def one_tile(tile, sums):
                sums = list(sums)
                grads = [grad_ref[pl.ds(tile * 64 + row * 8, 8), lanes(lane)] for row in range(8)]
                for held in range(14):
                    if 3 <= held < 11:
                        window = pad_ref[lane, tile, held - 3, pl.ds(5 + col, 8), :]
                    else:
                        row = held if held < 3 else held - 8
                        window = edge_ref[lane, tile, row, pl.ds(5 + col, 8), :]
                    for out in range(8):
                        tap = held - out
                        if 0 <= tap < 7:
                            sums[tap] = sums[tap] + window * grads[out]
                return tuple(sums)

            sums = tuple(jnp.zeros((8, LANES), f32) for _ in range(7))
            for tile in range(capacity):
                sums = one_tile(tile, sums)
            for row in range(7):
                part_ref[row * 7 + col, :, lanes(lane)] = sums[row]
            return 0

        for col in range(7):
            one_column(col)
    state_ref[0:TAPS, :] = jnp.sum(part_ref[...], axis=1)
    state_ref[TAPS : TAPS + 1, :] = emb_ref[...]
    state_ref[TAPS + 1 :, :] = jnp.zeros((STATE - TAPS - 1, emb_ref.shape[1]), f32)
    pack_ref[...] = packed(state_ref)


def packed(state_ref):
    state = state_ref[...]
    high = state.astype(bf16)
    low = pltpu.roll(state - high.astype(f32), 1, 0)
    row = lax.broadcasted_iota(jnp.int32, state.shape, 0)
    return jnp.where(row == TAPS + 1, low, high.astype(f32)).astype(bf16)


def merged(state_ref, got, with_embedding=True):
    total = packed(state_ref).astype(f32) + got.astype(f32)
    row = lax.broadcasted_iota(jnp.int32, total.shape, 0)
    if with_embedding:
        embedding = total + pltpu.roll(total, STATE - 1, 0)
    else:
        embedding = state_ref[...]
    return jnp.where(row < TAPS, total, jnp.where(row == TAPS, embedding, 0.0))


def state_kernel(with_embedding, state_ref, got_ref, new_ref, pack_ref):
    new_ref[...] = merged(state_ref, got_ref[...], with_embedding)
    pack_ref[...] = packed(new_ref)


def merge_kernel(splits, terms, place_ref, *refs):
    sums, refs = refs[: 2 * terms], refs[2 * terms :]
    outs = max(1, len(splits))
    keeps, sends, sum_ref = refs[0 : 2 * outs : 2], refs[1 : 2 * outs : 2], refs[2 * outs]
    first = 0
    for keep_ref, got_ref in zip(sums[0::2], sums[1::2]):
        count = keep_ref.shape[0]
        sum_ref[first : first + count, :] = keep_ref[...] + got_ref[...].astype(f32)
        first += count
    for keep_ref, send_ref, (start, count, rows, bit) in zip(keeps, sends, splits):
        split_pieces(sum_ref.at[start : start + count], rows, place_ref, bit, keep_ref, send_ref)
    if not splits:
        keeps[0][...] = sum_ref[...]
        sends[0][...] = sum_ref[...].astype(bf16)


def pair_kernel(keep_ref, got_ref, new_ref, send_ref):
    total = keep_ref[...].astype(bf16).astype(f32) + got_ref[...].astype(f32)
    new_ref[...] = total
    send_ref[...] = total.astype(bf16)


def finish_kernel(keep_ref, got_ref, state_ref, new_ref, share_ref, taps_ref, emb_ref):
    share_ref[...] = keep_ref[...].astype(bf16).astype(f32) + got_ref[...].astype(f32)
    total = merged(state_ref, new_ref[...])
    for row in range(7):
        taps_ref[row] = total[row * 7 : row * 7 + 7, :]
    emb_ref[...] = total[TAPS : TAPS + 1, :]


def middle_kernel(adj_ref, grad_ref, kern_ref, out_ref, pad_ref):
    capacity, parts = adj_ref.shape[0], grad_ref.shape[1] // LANES

    def own_at(tile, row):
        at = tile * 64 + row * 8
        return grad_ref[pl.ds(at if isinstance(at, int) else pl.multiple_of(at, 8), 8), :]

    fill_middle(pad_ref, own_at, adj_ref, capacity, 0, parts)

    def finish(tile, lane, sums):
        for row in range(8):
            out_ref[pl.ds(tile * 64 + row * 8, 8), lanes(lane)] = sums[row]

    convolve(
        [(pad_ref, 8, 3)],
        lambda row, col, lane: kern_ref[6 - row, 6 - col : 7 - col, lanes(lane)],
        finish, capacity, parts,
    )


def outer_kernel(
    adj_ref, place_ref, counts_ref, pool_ref, part_ref, core_ref, cross_ref, kern_ref, up_ref, cot_ref,
    out_ref, pad_ref,
):
    capacity, parts = adj_ref.shape[0], part_ref.shape[1] // LANES
    odd = is_odd(place_ref)
    fill_edge(pad_ref, core_ref, cross_ref, odd, adj_ref, capacity, UPPER, 0, parts)
    fill_edge(pad_ref, cross_ref, core_ref, odd, adj_ref, capacity, LOWER, 3, parts)

    def finish(tile, lane, sums):
        live = is_live(counts_ref, tile)
        extra = pool_ref[0, tile] * cot_ref[:, lanes(lane)] * 0.125
        for row in range(8):
            at = pl.ds(tile * 64 + row * 8, 8)
            total = live * (up_ref[at, lanes(lane)].astype(f32) + extra) + part_ref[at, lanes(lane)]
            if sums[row] is not None:
                total = total + sums[row]
            out_ref[at, lanes(lane)] = (live * total).astype(bf16)

    convolve(
        [(pad_ref.at[:, :, 0:3], 3, 0), (pad_ref.at[:, :, 3:6], 3, 11)],
        lambda row, col, lane: kern_ref[6 - row, 6 - col : 7 - col, lanes(lane)],
        finish, capacity, parts,
    )


def whole_pass(
    tiles_in, upstream, pool_weight, slide_cot, adjacency, counts, kernel, norm_gain, w_in, w_out,
    layer_scale,
):
    own = tiles_in[0]
    capacity, _, _, channels = own.shape
    parts = channels // LANES
    hidden = w_in.shape[1]
    pixels = capacity * 64
    up = upstream.reshape(pixels, channels)
    wanted = adjacency[0]
    edge_shape = (capacity, 3, 8, channels)
    count = lax.axis_size("space")
    stages = count.bit_length() - 1
    rows = hidden // count
    place = lax.axis_index("space").astype(jnp.int32).reshape(1, 1)

    core, cross = call(
        edge_kernel, [struct(edge_shape, bf16)] * 2, [SMEM, VMEM, VMEM], [place, counts, own],
        flops=EDGE_COST,
    )
    cross = crossed(cross, "space")
    core = swapped(core, "space", 1)

    pad, conv, mixed, act_grad, own_sum = call(
        early_kernel,
        [
            struct((parts, capacity, 8, 24, LANES)),
            struct((pixels, channels)),
            struct((pixels, channels + LANES), bf16),
            struct((pixels, hidden)),
            struct((1, channels)),
        ],
        [SMEM, VMEM, SMEM] + [VMEM] * 6,
        [wanted, counts, pool_weight, slide_cot, layer_scale, kernel, own, up, w_out],
        flops=2 * pixels * channels * hidden,
    )
    edge, normed, inv, pre, cdf, keep, send, pooled = call(
        functools.partial(forward_kernel, rows),
        [
            struct((parts, capacity, 6, 24, LANES)),
            struct((pixels, channels)),
            struct((pixels, 1)),
            struct((pixels, hidden)),
            struct((pixels, hidden)),
            struct((hidden // 2, channels)),
            struct((hidden // 2, channels), bf16),
            struct((hidden, LANES)),
        ],
        [SMEM] * 2 + [VMEM] * 7,
        [wanted, place, core, cross, conv, kernel, norm_gain, w_in, mixed],
        flops=4 * pixels * channels * hidden,
        scratch=[pltpu.VMEM((pixels, channels), f32)],
    )
    got = swapped(send, "space", 1)

    grad, core, cross, emb = call(
        back_kernel,
        [
            struct((pixels, channels)),
            struct(edge_shape, bf16),
            struct(edge_shape, bf16),
            struct((1, channels)),
        ],
        [SMEM, VMEM, SMEM] + [VMEM] * 11,
        [place, counts, pool_weight, pre, cdf, act_grad, w_in, normed, inv, norm_gain, pooled, w_out, layer_scale, own_sum],
        flops=2 * pixels * channels * hidden,
    )
    cross = crossed(cross, "space")
    core = swapped(core, "space", 1)

    def merge(parts_, splits):
        held = sum(keep.shape[0] for keep, _ in parts_)
        shapes = []
        for size in [count // 2 for _, count, _, _ in splits] or [held]:
            shapes += [struct((size, channels)), struct((size, channels), bf16)]
        operands = [array for pair in parts_ for array in pair]
        out = call(
            functools.partial(merge_kernel, splits, len(parts_)), shapes,
            [SMEM] + [VMEM] * len(operands), [place] + operands,
            scratch=[pltpu.VMEM((held, channels), f32)],
        )
        return list(zip(out[0::2], out[1::2]))

    half = hidden // 4
    (keep_a, send_a), (keep_b, send_b) = merge([(keep, got)], [(0, half, rows, 1), (half, half, 2 * rows, 2)])
    got_a = swapped(send_a, "space", 2)
    got_b = swapped(send_b, "space", 4)
    half //= 2
    (keep_a, send_a), (keep_b, send_b) = merge(
        [(keep_a, got_a), (keep_b, got_b)], [(0, half, rows, 2), (half, half, rows, 1)]
    )
    got_a = swapped(send_a, "space", 4)
    got_b = swapped(send_b, "space", 2)
    held = [(keep_a, got_a), (keep_b, got_b)]
    for stage in range(3, stages):
        size = hidden >> stage
        ((keep, send),) = merge(held, [(0, size, rows, stage)])
        got = swapped(send, "space", 1 << stage)
        held = [(keep, got)]
    ((share, send),) = merge(held, [])
    groups = lax.axis_size("dp")
    bit = 1
    while bit < groups:
        got = swapped(send, "dp", bit)
        bit *= 2
        if bit < groups:
            share, send = call(pair_kernel, [struct(share.shape), struct(send.shape, bf16)], [VMEM] * 2, [share, got])

    state, pack = call(
        taps_kernel, [struct((STATE, channels)), struct((STATE, channels), bf16)],
        [VMEM] * 4, [pad, edge, grad, emb],
        scratch=[pltpu.VMEM((TAPS, 8, channels), f32)],
    )
    steps = [("space", 1)] + [("dp", 1 << n) for n in range(groups.bit_length() - 1)]
    steps += [("space", 1 << n) for n in range(1, stages)]
    for axis, bit in steps:
        new = swapped(pack, axis, bit)
        if (axis, bit) != steps[-1]:
            state, pack = call(
                functools.partial(state_kernel, axis == "space"),
                [struct((STATE, channels)), struct((STATE, channels), bf16)],
                [VMEM] * 2, [state, new],
            )

    share, tap_grad, embedding = call(
        finish_kernel, [struct((rows, channels)), struct(kernel.shape), struct((1, channels))],
        [VMEM] * 4, [share, got, state, new],
    )

    part = call(
        middle_kernel, struct((pixels, channels)), [SMEM] + [VMEM] * 2, [wanted, grad, kernel],
        scratch=[pltpu.VMEM((parts, capacity, 8, 24, LANES), f32)],
    )
    grad_tiles = call(
        outer_kernel, struct((pixels, channels), bf16),
        [SMEM] * 2 + [VMEM, SMEM] + [VMEM] * 6,
        [wanted, place, counts, pool_weight, part, core, cross, kernel, up, slide_cot],
        scratch=[pltpu.VMEM((parts, capacity, 6, 24, LANES), f32)],
    )
    return (
        embedding,
        grad_tiles.reshape(tiles_in.shape),
        share,
        tap_grad,
    )


def solution(mesh):
    return jax.shard_map(
        whole_pass,
        mesh=mesh,
        in_specs=(
            P("dp", "space", None, None, None),
            P("dp", "space", None, None, None),
            P("dp", "space"),
            P("dp", None),
            P("dp", "space", None),
            P("dp", "space"),
            P(),
            P(),
            P(),
            P(),
            P(),
        ),
        out_specs=(P("dp", None), P("dp", "space", None, None, None), P("space", None), P()),
        check_vma=False,
    )
```

```python
import functools

import jax
import jax.numpy as jnp
from jax import lax
from jax.experimental import pallas as pl
from jax.experimental.pallas import tpu as pltpu
from jax.sharding import PartitionSpec as P

sqrt_half = 0.7071067811865476
inv_root_two_pi = 0.3989422804014327
f32 = jnp.float32
bf16 = jnp.bfloat16
LANES = 128

VMEM = pl.BlockSpec(memory_space=pltpu.VMEM)
SMEM = pl.BlockSpec(memory_space=pltpu.SMEM)
HBM = pl.BlockSpec(memory_space=pltpu.HBM)
STATE = 56
TAPS = 49
CHUNK = 384
BACK_CHUNK = 512
EDGE_COST = 5_000_000_000


def call(body, out_shape, in_specs, args, flops=0, scratch=(), limit=16 << 20, out_specs=None):
    outs = out_shape if isinstance(out_shape, (list, tuple)) else [out_shape]
    total = sum(a.size * a.dtype.itemsize for a in list(args) + list(outs))
    return pl.pallas_call(
        body,
        out_shape=out_shape,
        in_specs=in_specs,
        out_specs=out_specs or jax.tree.map(lambda _: VMEM, out_shape),
        scratch_shapes=scratch,
        compiler_params=pltpu.CompilerParams(vmem_limit_bytes=limit),
        cost_estimate=pl.CostEstimate(flops=flops, bytes_accessed=total, transcendentals=0),
    )(*args)


def struct(shape, dtype=f32):
    return jax.ShapeDtypeStruct(shape, dtype)


def swapped(value, axis, bit):
    count = lax.axis_size(axis)
    return lax.ppermute(value, axis, [(source, source ^ bit) for source in range(count)])


def crossed(value, axis):
    count = lax.axis_size(axis)
    firsts = range(1, count - 1, 2)
    return lax.ppermute(
        value, axis, [(n, n + 1) for n in firsts] + [(n + 1, n) for n in firsts]
    )


def valid(entry):
    return jnp.where(entry >= 0, 1.0, 0.0).astype(f32)


def local(entry, capacity):
    return lax.rem(jnp.maximum(entry, 0), capacity)


def place(pad_ref, tile, row, part, value, parts):
    for lane in range(parts):
        pad_ref[lane, tile, row, pl.ds(part * 8, 8), :] = value[:, lane * LANES : (lane + 1) * LANES]


def fill_middle(pad_ref, own_at, adj_ref, capacity, first_row, parts):
    for tile in range(capacity):
        west, east = adj_ref[tile, 2], adj_ref[tile, 3]
        for row in range(8):
            place(pad_ref, tile, first_row + row, 0, own_at(local(west, capacity), row) * valid(west), parts)
            place(pad_ref, tile, first_row + row, 1, own_at(tile, row), parts)
            place(pad_ref, tile, first_row + row, 2, own_at(local(east, capacity), row) * valid(east), parts)


def fill_edge(pad_ref, odd_ref, even_ref, odd, adj_ref, capacity, entries, first_row, parts):
    for tile in range(capacity):
        for part, entry in enumerate(entries):
            wanted = adj_ref[tile, entry]
            index, keep = local(wanted, capacity), valid(wanted)
            for row in range(3):
                value = odd_ref[index, row].astype(f32) * (keep * odd)
                value = value + even_ref[index, row].astype(f32) * (keep * (1.0 - odd))
                place(pad_ref, tile, first_row + row, part, value, parts)


def is_live(counts_ref, tile):
    return jnp.where(tile < counts_ref[...], 1.0, 0.0).astype(f32)


def is_odd(place_ref):
    return lax.rem(place_ref[0, 0], 2).astype(f32)


UPPER, LOWER = (4, 0, 5), (6, 1, 7)


def convolve(pads, tap_row, finish, capacity, parts, between=()):
    for lane in range(parts):

        def one_tile(tile):
            sums = [None] * 8
            for col in range(7):
                taps = [tap_row(row, col, lane) for row in range(7)]
                for ref, rows, base in pads:
                    for held in range(rows):
                        window = ref[lane, tile, held, pl.ds(5 + col, 8), :]
                        for out in range(8):
                            tap = held + base - out
                            if 0 <= tap < 7:
                                term = window * taps[tap]
                                sums[out] = term if sums[out] is None else sums[out] + term
            finish(tile, lane, sums)
            return 0

        for tile in range(capacity):
            one_tile(tile)
            if lane * capacity + tile < len(between):
                between[lane * capacity + tile]()


def lanes(lane):
    return slice(lane * LANES, (lane + 1) * LANES)


def swap_edges(last, first, odd, core_ref, cross_ref):
    core_ref[...] = (first * odd + last * (1.0 - odd)).astype(bf16)
    cross_ref[...] = (last * odd + first * (1.0 - odd)).astype(bf16)


def edge_kernel(place_ref, tiles_ref, core_ref, cross_ref):
    swap_edges(
        tiles_ref[:, 5:8].astype(f32), tiles_ref[:, 0:3].astype(f32), is_odd(place_ref), core_ref, cross_ref
    )


def early_kernel(
    adj_ref, counts_ref, pool_ref, cot_ref, scale_ref, kern_ref, tiles_ref, up_ref, w_out_ref,
    pad_ref, conv_ref, mixed_ref, act_grad_ref, own_sum_ref,
):
    capacity, parts = tiles_ref.shape[0], tiles_ref.shape[3] // LANES
    pixels = 64
    channels = tiles_ref.shape[3]
    fill_middle(pad_ref, lambda t, r: tiles_ref[t, r].astype(f32), adj_ref, capacity, 0, parts)
    own_sum = jnp.zeros((1, channels), f32)
    scale = scale_ref[...].reshape(1, channels)
    for tile in range(capacity):
        live = is_live(counts_ref, tile)
        pool = pool_ref[0, tile]
        rows = slice(tile * pixels, (tile + 1) * pixels)
        out_grad = live * (up_ref[rows, :].astype(f32) + pool * cot_ref[...] * 0.125)
        mixed_ref[rows, 0:channels] = (out_grad * scale).astype(bf16)
        column = lax.broadcasted_iota(jnp.int32, (pixels, LANES), 1)
        mixed_ref[rows, channels:] = jnp.where(column == tile, 1.0, 0.0).astype(bf16)
        own = tiles_ref[tile].astype(f32)
        own_sum += live * pool * jnp.sum(own.reshape(pixels, channels), axis=0, keepdims=True)
    own_sum_ref[...] = own_sum

    def product(at):
        act_grad_ref[:, at] = lax.dot_general(
            mixed_ref[:, 0:channels], w_out_ref[at, :], (((1,), (1,)), ((), ())), preferred_element_type=f32
        )

    hidden = w_out_ref.shape[0]
    step = 256 if hidden % 256 == 0 else hidden
    products = [functools.partial(product, slice(n, n + step)) for n in range(0, hidden, step)]

    def finish(tile, lane, sums):
        for row in range(8):
            conv_ref[pl.ds(tile * pixels + row * 8, 8), lanes(lane)] = sums[row]

    convolve(
        [(pad_ref, 8, 3)],
        lambda row, col, lane: kern_ref[row, col : col + 1, lanes(lane)],
        finish, capacity, parts, products,
    )


def split_pieces(value_ref, rows, place_ref, stage, keep_ref, send_ref):
    side = lax.rem(lax.div(place_ref[0, 0], 1 << stage), 2)
    for pair in range(value_ref.shape[0] // (2 * rows)):
        here = pl.ds(pair * rows, rows)
        mine = pl.ds(pl.multiple_of((2 * pair + side) * rows, 8), rows)
        other = pl.ds(pl.multiple_of((2 * pair + 1 - side) * rows, 8), rows)
        keep_ref[here, :] = value_ref[mine, :]
        send_ref[here, :] = value_ref[other, :].astype(bf16)


def forward_kernel(
    rows, adj_ref, place_ref, core_ref, cross_ref, conv_ref, kern_ref, gain_ref, w_in_ref, mixed_ref,
    edge_ref, normed_ref, inv_ref, pre_ref, cdf_ref, keep_ref, send_ref, pooled_ref, whole_ref,
):
    capacity, parts = adj_ref.shape[0], conv_ref.shape[1] // LANES
    channels = conv_ref.shape[1]
    pixels = 64
    odd = is_odd(place_ref)
    fill_edge(edge_ref, core_ref, cross_ref, odd, adj_ref, capacity, UPPER, 0, parts)
    fill_edge(edge_ref, cross_ref, core_ref, odd, adj_ref, capacity, LOWER, 3, parts)

    def finish(tile, lane, sums):
        for row in range(8):
            at = pl.ds(tile * pixels + row * 8, 8)
            total = conv_ref[at, lanes(lane)]
            if sums[row] is not None:
                total = total + sums[row]
            whole_ref[at, lanes(lane)] = total

    convolve(
        [(edge_ref.at[:, :, 0:3], 3, 0), (edge_ref.at[:, :, 3:6], 3, 11)],
        lambda row, col, lane: kern_ref[row, col : col + 1, lanes(lane)],
        finish, capacity, parts,
    )
    conv = whole_ref[...]
    centred = conv - jnp.mean(conv, axis=-1, keepdims=True)
    inv_std = lax.rsqrt(jnp.mean(centred * centred, axis=-1, keepdims=True) + 1e-06)
    normed = centred * inv_std
    normed_ref[...] = normed
    inv_ref[...] = inv_std
    lifted = (normed * gain_ref[...].reshape(1, channels)).astype(bf16)
    hidden = w_in_ref.shape[1]
    side = lax.rem(place_ref[0, 0], 2)
    chunk = CHUNK if hidden % CHUNK == 0 and CHUNK % (2 * rows) == 0 else hidden

    def project(first):
        return jnp.dot(lifted, w_in_ref[:, first : first + chunk], preferred_element_type=f32)

    following = project(0)
    for first in range(0, hidden, chunk):
        at = slice(first, first + chunk)
        pre = following
        if first + chunk < hidden:
            following = project(first + chunk)
        cdf = 0.5 * (1.0 + lax.erf(pre * sqrt_half))
        pre_ref[:, at] = pre
        cdf_ref[:, at] = cdf
        activated = (pre * cdf).astype(bf16)
        both = lax.dot_general(
            activated, mixed_ref[...], (((0,), (0,)), ((), ())), preferred_element_type=f32
        )
        pooled_ref[at, :] = both[:, channels:]
        for block in range(0, chunk, 2 * rows):
            even = both[block : block + rows, 0:channels]
            odd_rows = both[block + rows : block + 2 * rows, 0:channels]
            out = pl.ds((first + block) // 2, rows)
            keep_ref[out, :] = jnp.where(side == 0, even, odd_rows)
            send_ref[out, :] = jnp.where(side == 0, odd_rows, even).astype(bf16)


def back_kernel(
    place_ref, counts_ref, pool_ref, pre_ref, cdf_ref, act_grad_ref, w_in_ref, normed_ref, inv_ref, gain_ref, pooled_ref, w_out_ref,
    scale_ref, own_sum_ref, grad_ref, core_ref, cross_ref, emb_ref,
):
    channels = normed_ref.shape[1]
    capacity = core_ref.shape[0]
    hidden = w_in_ref.shape[1]
    chunk = BACK_CHUNK if hidden % BACK_CHUNK == 0 else hidden
    lift = None
    for first in range(0, hidden, chunk):
        at = slice(first, first + chunk)
        pre = pre_ref[:, at]
        density = jnp.exp(-0.5 * pre * pre) * inv_root_two_pi
        pre_grad = (act_grad_ref[:, at] * (cdf_ref[:, at] + pre * density)).astype(bf16)
        term = lax.dot_general(
            pre_grad, w_in_ref[:, at], (((1,), (1,)), ((), ())), preferred_element_type=f32
        )
        lift = term if lift is None else lift + term
    grad_normed = lift * gain_ref[...].reshape(1, channels)
    normed = normed_ref[...]
    grad = inv_ref[...] * (
        grad_normed
        - jnp.mean(grad_normed, axis=-1, keepdims=True)
        - normed * jnp.mean(grad_normed * normed, axis=-1, keepdims=True)
    )
    grad_ref[...] = grad
    shaped = grad.reshape(capacity, 8, 8, channels)
    swap_edges(shaped[:, 5:8], shaped[:, 0:3], is_odd(place_ref), core_ref, cross_ref)
    column = lax.broadcasted_iota(jnp.int32, (1, LANES), 1)
    weights = jnp.zeros((1, LANES), f32)
    for tile in range(capacity):
        amount = is_live(counts_ref, tile) * pool_ref[0, tile]
        weights = jnp.where(column == tile, amount, weights)
    hidden = jnp.sum(pooled_ref[...] * weights, axis=1, keepdims=True)
    mixed = jnp.sum(hidden * w_out_ref[...].astype(f32), axis=0, keepdims=True)
    emb_ref[...] = (own_sum_ref[...] + scale_ref[...].reshape(1, channels) * mixed) * 0.125


def taps_kernel(pad_ref, edge_ref, grad_ref, emb_ref, state_ref, pack_ref, part_ref):
    parts, capacity = pad_ref.shape[0], pad_ref.shape[1]
    for lane in range(parts):

        def one_column(col):
            def one_tile(tile, sums):
                sums = list(sums)
                grads = [grad_ref[pl.ds(tile * 64 + row * 8, 8), lanes(lane)] for row in range(8)]
                for held in range(14):
                    if 3 <= held < 11:
                        window = pad_ref[lane, tile, held - 3, pl.ds(5 + col, 8), :]
                    else:
                        row = held if held < 3 else held - 8
                        window = edge_ref[lane, tile, row, pl.ds(5 + col, 8), :]
                    for out in range(8):
                        tap = held - out
                        if 0 <= tap < 7:
                            sums[tap] = sums[tap] + window * grads[out]
                return tuple(sums)

            sums = tuple(jnp.zeros((8, LANES), f32) for _ in range(7))
            for tile in range(capacity):
                sums = one_tile(tile, sums)
            for row in range(7):
                part_ref[row * 7 + col, :, lanes(lane)] = sums[row]
            return 0

        for col in range(7):
            one_column(col)
    state_ref[0:TAPS, :] = jnp.sum(part_ref[...], axis=1)
    state_ref[TAPS : TAPS + 1, :] = emb_ref[...]
    state_ref[TAPS + 1 :, :] = jnp.zeros((STATE - TAPS - 1, emb_ref.shape[1]), f32)
    pack_ref[...] = packed(state_ref)


def packed(state_ref):
    state = state_ref[...]
    high = state.astype(bf16)
    low = pltpu.roll(state - high.astype(f32), 1, 0)
    row = lax.broadcasted_iota(jnp.int32, state.shape, 0)
    return jnp.where(row == TAPS + 1, low, high.astype(f32)).astype(bf16)


def merged(state_ref, got, with_embedding=True):
    total = packed(state_ref).astype(f32) + got.astype(f32)
    row = lax.broadcasted_iota(jnp.int32, total.shape, 0)
    if with_embedding:
        embedding = total + pltpu.roll(total, STATE - 1, 0)
    else:
        embedding = state_ref[...]
    return jnp.where(row < TAPS, total, jnp.where(row == TAPS, embedding, 0.0))


def state_kernel(with_embedding, state_ref, got_ref, new_ref, pack_ref):
    new_ref[...] = merged(state_ref, got_ref[...], with_embedding)
    pack_ref[...] = packed(new_ref)


def merge_kernel(splits, terms, place_ref, *refs):
    sums, refs = refs[: 2 * terms], refs[2 * terms :]
    outs = max(1, len(splits))
    keeps, sends, sum_ref = refs[0 : 2 * outs : 2], refs[1 : 2 * outs : 2], refs[2 * outs]
    first = 0
    for keep_ref, got_ref in zip(sums[0::2], sums[1::2]):
        count = keep_ref.shape[0]
        sum_ref[first : first + count, :] = keep_ref[...] + got_ref[...].astype(f32)
        first += count
    for keep_ref, send_ref, (start, count, rows, bit) in zip(keeps, sends, splits):
        split_pieces(sum_ref.at[start : start + count], rows, place_ref, bit, keep_ref, send_ref)
    if not splits:
        keeps[0][...] = sum_ref[...]
        sends[0][...] = sum_ref[...].astype(bf16)


def pair_kernel(keep_ref, got_ref, new_ref, send_ref):
    total = keep_ref[...].astype(bf16).astype(f32) + got_ref[...].astype(f32)
    new_ref[...] = total
    send_ref[...] = total.astype(bf16)


def finish_kernel(keep_ref, got_ref, state_ref, new_ref, share_ref, taps_ref, emb_ref):
    share_ref[...] = keep_ref[...].astype(bf16).astype(f32) + got_ref[...].astype(f32)
    total = merged(state_ref, new_ref[...])
    for row in range(7):
        taps_ref[row] = total[row * 7 : row * 7 + 7, :]
    emb_ref[...] = total[TAPS : TAPS + 1, :]


def middle_kernel(adj_ref, grad_ref, kern_ref, out_ref, pad_ref):
    capacity, parts = adj_ref.shape[0], grad_ref.shape[1] // LANES

    def own_at(tile, row):
        at = tile * 64 + row * 8
        return grad_ref[pl.ds(at if isinstance(at, int) else pl.multiple_of(at, 8), 8), :]

    fill_middle(pad_ref, own_at, adj_ref, capacity, 0, parts)

    def finish(tile, lane, sums):
        for row in range(8):
            out_ref[pl.ds(tile * 64 + row * 8, 8), lanes(lane)] = sums[row]

    convolve(
        [(pad_ref, 8, 3)],
        lambda row, col, lane: kern_ref[6 - row, 6 - col : 7 - col, lanes(lane)],
        finish, capacity, parts,
    )


def outer_kernel(
    adj_ref, place_ref, counts_ref, pool_ref, part_ref, core_ref, cross_ref, kern_ref, up_ref, cot_ref,
    out_ref, pad_ref,
):
    capacity, parts = adj_ref.shape[0], part_ref.shape[1] // LANES
    odd = is_odd(place_ref)
    fill_edge(pad_ref, core_ref, cross_ref, odd, adj_ref, capacity, UPPER, 0, parts)
    fill_edge(pad_ref, cross_ref, core_ref, odd, adj_ref, capacity, LOWER, 3, parts)

    def finish(tile, lane, sums):
        live = is_live(counts_ref, tile)
        extra = pool_ref[0, tile] * cot_ref[:, lanes(lane)] * 0.125
        for row in range(8):
            at = pl.ds(tile * 64 + row * 8, 8)
            total = live * (up_ref[at, lanes(lane)].astype(f32) + extra) + part_ref[at, lanes(lane)]
            if sums[row] is not None:
                total = total + sums[row]
            out_ref[at, lanes(lane)] = (live * total).astype(bf16)

    convolve(
        [(pad_ref.at[:, :, 0:3], 3, 0), (pad_ref.at[:, :, 3:6], 3, 11)],
        lambda row, col, lane: kern_ref[6 - row, 6 - col : 7 - col, lanes(lane)],
        finish, capacity, parts,
    )


def whole_pass(
    tiles_in, upstream, pool_weight, slide_cot, adjacency, counts, kernel, norm_gain, w_in, w_out,
    layer_scale,
):
    own = tiles_in[0]
    capacity, _, _, channels = own.shape
    parts = channels // LANES
    hidden = w_in.shape[1]
    pixels = capacity * 64
    up = upstream.reshape(pixels, channels)
    wanted = adjacency[0]
    edge_shape = (capacity, 3, 8, channels)
    count = lax.axis_size("space")
    stages = count.bit_length() - 1
    rows = hidden // count
    place = lax.axis_index("space").astype(jnp.int32).reshape(1, 1)

    core, cross = call(
        edge_kernel, [struct(edge_shape, bf16)] * 2, [SMEM, VMEM], [place, own],
        flops=EDGE_COST,
    )
    cross = crossed(cross, "space")
    core = swapped(core, "space", 1)

    pad, conv, mixed, act_grad, own_sum = call(
        early_kernel,
        [
            struct((parts, capacity, 8, 24, LANES)),
            struct((pixels, channels)),
            struct((pixels, channels + LANES), bf16),
            struct((pixels, hidden)),
            struct((1, channels)),
        ],
        [SMEM, VMEM, SMEM] + [VMEM] * 6,
        [wanted, counts, pool_weight, slide_cot, layer_scale, kernel, own, up, w_out],
        flops=2 * pixels * channels * hidden,
    )
    edge, normed, inv, pre, cdf, keep, send, pooled = call(
        functools.partial(forward_kernel, rows),
        [
            struct((parts, capacity, 6, 24, LANES)),
            struct((pixels, channels)),
            struct((pixels, 1)),
            struct((pixels, hidden)),
            struct((pixels, hidden)),
            struct((hidden // 2, channels)),
            struct((hidden // 2, channels), bf16),
            struct((hidden, LANES)),
        ],
        [SMEM] * 2 + [VMEM] * 7,
        [wanted, place, core, cross, conv, kernel, norm_gain, w_in, mixed],
        flops=4 * pixels * channels * hidden,
        scratch=[pltpu.VMEM((pixels, channels), f32)],
    )
    got = swapped(send, "space", 1)

    grad, core, cross, emb = call(
        back_kernel,
        [
            struct((pixels, channels)),
            struct(edge_shape, bf16),
            struct(edge_shape, bf16),
            struct((1, channels)),
        ],
        [SMEM, VMEM, SMEM] + [VMEM] * 11,
        [place, counts, pool_weight, pre, cdf, act_grad, w_in, normed, inv, norm_gain, pooled, w_out, layer_scale, own_sum],
        flops=2 * pixels * channels * hidden,
    )
    cross = crossed(cross, "space")
    core = swapped(core, "space", 1)

    def merge(parts_, splits):
        held = sum(keep.shape[0] for keep, _ in parts_)
        shapes = []
        for size in [count // 2 for _, count, _, _ in splits] or [held]:
            shapes += [struct((size, channels)), struct((size, channels), bf16)]
        operands = [array for pair in parts_ for array in pair]
        out = call(
            functools.partial(merge_kernel, splits, len(parts_)), shapes,
            [SMEM] + [VMEM] * len(operands), [place] + operands,
            scratch=[pltpu.VMEM((held, channels), f32)],
        )
        return list(zip(out[0::2], out[1::2]))

    half = hidden // 4
    (keep_a, send_a), (keep_b, send_b) = merge([(keep, got)], [(0, half, rows, 1), (half, half, 2 * rows, 2)])
    got_a = swapped(send_a, "space", 2)
    got_b = swapped(send_b, "space", 4)
    half //= 2
    (keep_a, send_a), (keep_b, send_b) = merge(
        [(keep_a, got_a), (keep_b, got_b)], [(0, half, rows, 2), (half, half, rows, 1)]
    )
    got_a = swapped(send_a, "space", 4)
    got_b = swapped(send_b, "space", 2)
    held = [(keep_a, got_a), (keep_b, got_b)]
    for stage in range(3, stages):
        size = hidden >> stage
        ((keep, send),) = merge(held, [(0, size, rows, stage)])
        got = swapped(send, "space", 1 << stage)
        held = [(keep, got)]
    ((share, send),) = merge(held, [])
    groups = lax.axis_size("dp")
    bit = 1
    while bit < groups:
        got = swapped(send, "dp", bit)
        bit *= 2
        if bit < groups:
            share, send = call(pair_kernel, [struct(share.shape), struct(send.shape, bf16)], [VMEM] * 2, [share, got])

    state, pack = call(
        taps_kernel, [struct((STATE, channels)), struct((STATE, channels), bf16)],
        [VMEM] * 4, [pad, edge, grad, emb],
        scratch=[pltpu.VMEM((TAPS, 8, channels), f32)],
    )
    steps = [("space", 1)] + [("dp", 1 << n) for n in range(groups.bit_length() - 1)]
    steps += [("space", 1 << n) for n in range(1, stages)]
    for axis, bit in steps:
        new = swapped(pack, axis, bit)
        if (axis, bit) != steps[-1]:
            state, pack = call(
                functools.partial(state_kernel, axis == "space"),
                [struct((STATE, channels)), struct((STATE, channels), bf16)],
                [VMEM] * 2, [state, new],
            )

    share, tap_grad, embedding = call(
        finish_kernel, [struct((rows, channels)), struct(kernel.shape), struct((1, channels))],
        [VMEM] * 4, [share, got, state, new],
    )

    part = call(
        middle_kernel, struct((pixels, channels)), [SMEM] + [VMEM] * 2, [wanted, grad, kernel],
        scratch=[pltpu.VMEM((parts, capacity, 8, 24, LANES), f32)],
    )
    grad_tiles = call(
        outer_kernel, struct((pixels, channels), bf16),
        [SMEM] * 2 + [VMEM, SMEM] + [VMEM] * 6,
        [wanted, place, counts, pool_weight, part, core, cross, kernel, up, slide_cot],
        scratch=[pltpu.VMEM((parts, capacity, 6, 24, LANES), f32)],
    )
    return (
        embedding,
        grad_tiles.reshape(tiles_in.shape),
        share,
        tap_grad,
    )


def solution(mesh):
    return jax.shard_map(
        whole_pass,
        mesh=mesh,
        in_specs=(
            P("dp", "space", None, None, None),
            P("dp", "space", None, None, None),
            P("dp", "space"),
            P("dp", None),
            P("dp", "space", None),
            P("dp", "space"),
            P(),
            P(),
            P(),
            P(),
            P(),
        ),
        out_specs=(P("dp", None), P("dp", "space", None, None, None), P("space", None), P()),
        check_vma=False,
    )
```

```python
import functools

import jax
import jax.numpy as jnp
from jax import lax
from jax.experimental import pallas as pl
from jax.experimental.pallas import tpu as pltpu
from jax.sharding import PartitionSpec as P

sqrt_half = 0.7071067811865476
inv_root_two_pi = 0.3989422804014327
f32 = jnp.float32
bf16 = jnp.bfloat16
LANES = 128

VMEM = pl.BlockSpec(memory_space=pltpu.VMEM)
SMEM = pl.BlockSpec(memory_space=pltpu.SMEM)
HBM = pl.BlockSpec(memory_space=pltpu.HBM)
STATE = 56
TAPS = 49
CHUNK = 384
BACK_CHUNK = 512
EDGE_COST = 5_000_000_000


def call(body, out_shape, in_specs, args, flops=0, scratch=(), limit=16 << 20, out_specs=None):
    outs = out_shape if isinstance(out_shape, (list, tuple)) else [out_shape]
    total = sum(a.size * a.dtype.itemsize for a in list(args) + list(outs))
    return pl.pallas_call(
        body,
        out_shape=out_shape,
        in_specs=in_specs,
        out_specs=out_specs or jax.tree.map(lambda _: VMEM, out_shape),
        scratch_shapes=scratch,
        compiler_params=pltpu.CompilerParams(vmem_limit_bytes=limit),
        cost_estimate=pl.CostEstimate(flops=flops, bytes_accessed=total, transcendentals=0),
    )(*args)


def struct(shape, dtype=f32):
    return jax.ShapeDtypeStruct(shape, dtype)


def swapped(value, axis, bit):
    count = lax.axis_size(axis)
    return lax.ppermute(value, axis, [(source, source ^ bit) for source in range(count)])


def crossed(value):
    groups, count = lax.axis_size("dp"), lax.axis_size("space")
    targets = []
    for group in range(groups):
        for n in range(count):
            step = 1 if n % 2 else -1
            if 0 <= n + step < count:
                targets.append((group * count + n, group * count + n + step))
            elif (group ^ 1) < groups:
                targets.append((group * count + n, (group ^ 1) * count + n))
    return lax.ppermute(value, ("dp", "space"), targets)


def valid(entry):
    return jnp.where(entry >= 0, 1.0, 0.0).astype(f32)


def local(entry, capacity):
    return lax.rem(jnp.maximum(entry, 0), capacity)


def place(pad_ref, tile, row, part, value, parts):
    for lane in range(parts):
        pad_ref[lane, tile, row, pl.ds(part * 8, 8), :] = value[:, lane * LANES : (lane + 1) * LANES]


def fill_middle(pad_ref, own_at, adj_ref, capacity, first_row, parts):
    for tile in range(capacity):
        west, east = adj_ref[tile, 2], adj_ref[tile, 3]
        for row in range(8):
            place(pad_ref, tile, first_row + row, 0, own_at(local(west, capacity), row) * valid(west), parts)
            place(pad_ref, tile, first_row + row, 1, own_at(tile, row), parts)
            place(pad_ref, tile, first_row + row, 2, own_at(local(east, capacity), row) * valid(east), parts)


def fill_edge(pad_ref, odd_ref, even_ref, odd, adj_ref, capacity, entries, first_row, parts):
    for tile in range(capacity):
        for part, entry in enumerate(entries):
            wanted = adj_ref[tile, entry]
            index, keep = local(wanted, capacity), valid(wanted)
            for row in range(3):
                value = odd_ref[index, row].astype(f32) * (keep * odd)
                value = value + even_ref[index, row].astype(f32) * (keep * (1.0 - odd))
                place(pad_ref, tile, first_row + row, part, value, parts)


def is_live(counts_ref, tile):
    return jnp.where(tile < counts_ref[...], 1.0, 0.0).astype(f32)


def is_odd(place_ref):
    return lax.rem(place_ref[0, 0], 2).astype(f32)


UPPER, LOWER = (4, 0, 5), (6, 1, 7)


def convolve(pads, tap_row, finish, capacity, parts, between=()):
    for lane in range(parts):

        def one_tile(tile):
            sums = [None] * 8
            for col in range(7):
                taps = [tap_row(row, col, lane) for row in range(7)]
                for ref, rows, base in pads:
                    for held in range(rows):
                        window = ref[lane, tile, held, pl.ds(5 + col, 8), :]
                        for out in range(8):
                            tap = held + base - out
                            if 0 <= tap < 7:
                                term = window * taps[tap]
                                sums[out] = term if sums[out] is None else sums[out] + term
            finish(tile, lane, sums)
            return 0

        for tile in range(capacity):
            one_tile(tile)
            if lane * capacity + tile < len(between):
                between[lane * capacity + tile]()


def lanes(lane):
    return slice(lane * LANES, (lane + 1) * LANES)


def swap_edges(last, first, odd, core_ref, cross_ref):
    core_ref[...] = (first * odd + last * (1.0 - odd)).astype(bf16)
    cross_ref[...] = (last * odd + first * (1.0 - odd)).astype(bf16)


def edge_kernel(place_ref, tiles_ref, core_ref, cross_ref):
    swap_edges(
        tiles_ref[:, 5:8].astype(f32), tiles_ref[:, 0:3].astype(f32), is_odd(place_ref), core_ref, cross_ref
    )


def early_kernel(
    adj_ref, counts_ref, pool_ref, cot_ref, scale_ref, kern_ref, tiles_ref, up_ref, w_out_ref,
    pad_ref, conv_ref, mixed_ref, act_grad_ref, own_sum_ref,
):
    capacity, parts = tiles_ref.shape[0], tiles_ref.shape[3] // LANES
    pixels = 64
    channels = tiles_ref.shape[3]
    fill_middle(pad_ref, lambda t, r: tiles_ref[t, r].astype(f32), adj_ref, capacity, 0, parts)
    own_sum = jnp.zeros((1, channels), f32)
    scale = scale_ref[...].reshape(1, channels)
    for tile in range(capacity):
        live = is_live(counts_ref, tile)
        pool = pool_ref[0, tile]
        rows = slice(tile * pixels, (tile + 1) * pixels)
        out_grad = live * (up_ref[rows, :].astype(f32) + pool * cot_ref[...] * 0.125)
        mixed_ref[rows, 0:channels] = (out_grad * scale).astype(bf16)
        column = lax.broadcasted_iota(jnp.int32, (pixels, LANES), 1)
        mixed_ref[rows, channels:] = jnp.where(column == tile, 1.0, 0.0).astype(bf16)
        own = tiles_ref[tile].astype(f32)
        own_sum += live * pool * jnp.sum(own.reshape(pixels, channels), axis=0, keepdims=True)
    own_sum_ref[...] = own_sum

    def product(at):
        act_grad_ref[:, at] = lax.dot_general(
            mixed_ref[:, 0:channels], w_out_ref[at, :], (((1,), (1,)), ((), ())), preferred_element_type=f32
        )

    hidden = w_out_ref.shape[0]
    step = 256 if hidden % 256 == 0 else hidden
    products = [functools.partial(product, slice(n, n + step)) for n in range(0, hidden, step)]

    def finish(tile, lane, sums):
        for row in range(8):
            conv_ref[pl.ds(tile * pixels + row * 8, 8), lanes(lane)] = sums[row]

    convolve(
        [(pad_ref, 8, 3)],
        lambda row, col, lane: kern_ref[row, col : col + 1, lanes(lane)],
        finish, capacity, parts, products,
    )


def split_pieces(value_ref, rows, place_ref, stage, keep_ref, send_ref):
    side = lax.rem(lax.div(place_ref[0, 0], 1 << stage), 2)
    for pair in range(value_ref.shape[0] // (2 * rows)):
        here = pl.ds(pair * rows, rows)
        mine = pl.ds(pl.multiple_of((2 * pair + side) * rows, 8), rows)
        other = pl.ds(pl.multiple_of((2 * pair + 1 - side) * rows, 8), rows)
        keep_ref[here, :] = value_ref[mine, :]
        send_ref[here, :] = value_ref[other, :].astype(bf16)


def forward_kernel(
    rows, adj_ref, place_ref, core_ref, cross_ref, conv_ref, kern_ref, gain_ref, w_in_ref, mixed_ref,
    edge_ref, normed_ref, inv_ref, pre_ref, cdf_ref, keep_ref, send_ref, pooled_ref, whole_ref,
):
    capacity, parts = adj_ref.shape[0], conv_ref.shape[1] // LANES
    channels = conv_ref.shape[1]
    pixels = 64
    odd = is_odd(place_ref)
    fill_edge(edge_ref, core_ref, cross_ref, odd, adj_ref, capacity, UPPER, 0, parts)
    fill_edge(edge_ref, cross_ref, core_ref, odd, adj_ref, capacity, LOWER, 3, parts)

    def finish(tile, lane, sums):
        for row in range(8):
            at = pl.ds(tile * pixels + row * 8, 8)
            total = conv_ref[at, lanes(lane)]
            if sums[row] is not None:
                total = total + sums[row]
            whole_ref[at, lanes(lane)] = total

    convolve(
        [(edge_ref.at[:, :, 0:3], 3, 0), (edge_ref.at[:, :, 3:6], 3, 11)],
        lambda row, col, lane: kern_ref[row, col : col + 1, lanes(lane)],
        finish, capacity, parts,
    )
    conv = whole_ref[...]
    centred = conv - jnp.mean(conv, axis=-1, keepdims=True)
    inv_std = lax.rsqrt(jnp.mean(centred * centred, axis=-1, keepdims=True) + 1e-06)
    normed = centred * inv_std
    normed_ref[...] = normed
    inv_ref[...] = inv_std
    lifted = (normed * gain_ref[...].reshape(1, channels)).astype(bf16)
    hidden = w_in_ref.shape[1]
    side = lax.rem(place_ref[0, 0], 2)
    chunk = CHUNK if hidden % CHUNK == 0 and CHUNK % (2 * rows) == 0 else hidden

    def project(first):
        return jnp.dot(lifted, w_in_ref[:, first : first + chunk], preferred_element_type=f32)

    following = project(0)
    for first in range(0, hidden, chunk):
        at = slice(first, first + chunk)
        pre = following
        if first + chunk < hidden:
            following = project(first + chunk)
        cdf = 0.5 * (1.0 + lax.erf(pre * sqrt_half))
        pre_ref[:, at] = pre
        cdf_ref[:, at] = cdf
        activated = (pre * cdf).astype(bf16)
        both = lax.dot_general(
            activated, mixed_ref[...], (((0,), (0,)), ((), ())), preferred_element_type=f32
        )
        pooled_ref[at, :] = both[:, channels:]
        for block in range(0, chunk, 2 * rows):
            even = both[block : block + rows, 0:channels]
            odd_rows = both[block + rows : block + 2 * rows, 0:channels]
            out = pl.ds((first + block) // 2, rows)
            keep_ref[out, :] = jnp.where(side == 0, even, odd_rows)
            send_ref[out, :] = jnp.where(side == 0, odd_rows, even).astype(bf16)


def back_kernel(
    place_ref, counts_ref, pool_ref, pre_ref, cdf_ref, act_grad_ref, w_in_ref, normed_ref, inv_ref, gain_ref, pooled_ref, w_out_ref,
    scale_ref, own_sum_ref, grad_ref, core_ref, cross_ref, emb_ref,
):
    channels = normed_ref.shape[1]
    capacity = core_ref.shape[0]
    hidden = w_in_ref.shape[1]
    chunk = BACK_CHUNK if hidden % BACK_CHUNK == 0 else hidden
    lift = None
    for first in range(0, hidden, chunk):
        at = slice(first, first + chunk)
        pre = pre_ref[:, at]
        density = jnp.exp(-0.5 * pre * pre) * inv_root_two_pi
        pre_grad = (act_grad_ref[:, at] * (cdf_ref[:, at] + pre * density)).astype(bf16)
        term = lax.dot_general(
            pre_grad, w_in_ref[:, at], (((1,), (1,)), ((), ())), preferred_element_type=f32
        )
        lift = term if lift is None else lift + term
    grad_normed = lift * gain_ref[...].reshape(1, channels)
    normed = normed_ref[...]
    grad = inv_ref[...] * (
        grad_normed
        - jnp.mean(grad_normed, axis=-1, keepdims=True)
        - normed * jnp.mean(grad_normed * normed, axis=-1, keepdims=True)
    )
    grad_ref[...] = grad
    shaped = grad.reshape(capacity, 8, 8, channels)
    swap_edges(shaped[:, 5:8], shaped[:, 0:3], is_odd(place_ref), core_ref, cross_ref)
    column = lax.broadcasted_iota(jnp.int32, (1, LANES), 1)
    weights = jnp.zeros((1, LANES), f32)
    for tile in range(capacity):
        amount = is_live(counts_ref, tile) * pool_ref[0, tile]
        weights = jnp.where(column == tile, amount, weights)
    hidden = jnp.sum(pooled_ref[...] * weights, axis=1, keepdims=True)
    mixed = jnp.sum(hidden * w_out_ref[...].astype(f32), axis=0, keepdims=True)
    emb_ref[...] = (own_sum_ref[...] + scale_ref[...].reshape(1, channels) * mixed) * 0.125


def taps_kernel(pad_ref, edge_ref, grad_ref, emb_ref, state_ref, pack_ref, part_ref):
    parts, capacity = pad_ref.shape[0], pad_ref.shape[1]
    for lane in range(parts):

        def one_column(col):
            def one_tile(tile, sums):
                sums = list(sums)
                grads = [grad_ref[pl.ds(tile * 64 + row * 8, 8), lanes(lane)] for row in range(8)]
                for held in range(14):
                    if 3 <= held < 11:
                        window = pad_ref[lane, tile, held - 3, pl.ds(5 + col, 8), :]
                    else:
                        row = held if held < 3 else held - 8
                        window = edge_ref[lane, tile, row, pl.ds(5 + col, 8), :]
                    for out in range(8):
                        tap = held - out
                        if 0 <= tap < 7:
                            sums[tap] = sums[tap] + window * grads[out]
                return tuple(sums)

            sums = tuple(jnp.zeros((8, LANES), f32) for _ in range(7))
            for tile in range(capacity):
                sums = one_tile(tile, sums)
            for row in range(7):
                part_ref[row * 7 + col, :, lanes(lane)] = sums[row]
            return 0

        for col in range(7):
            one_column(col)
    state_ref[0:TAPS, :] = jnp.sum(part_ref[...], axis=1)
    state_ref[TAPS : TAPS + 1, :] = emb_ref[...]
    state_ref[TAPS + 1 :, :] = jnp.zeros((STATE - TAPS - 1, emb_ref.shape[1]), f32)
    pack_ref[...] = packed(state_ref)


def packed(state_ref):
    state = state_ref[...]
    high = state.astype(bf16)
    low = pltpu.roll(state - high.astype(f32), 1, 0)
    row = lax.broadcasted_iota(jnp.int32, state.shape, 0)
    return jnp.where(row == TAPS + 1, low, high.astype(f32)).astype(bf16)


def merged(state_ref, got, with_embedding=True):
    total = packed(state_ref).astype(f32) + got.astype(f32)
    row = lax.broadcasted_iota(jnp.int32, total.shape, 0)
    if with_embedding:
        embedding = total + pltpu.roll(total, STATE - 1, 0)
    else:
        embedding = state_ref[...]
    return jnp.where(row < TAPS, total, jnp.where(row == TAPS, embedding, 0.0))


def state_kernel(with_embedding, state_ref, got_ref, new_ref, pack_ref):
    new_ref[...] = merged(state_ref, got_ref[...], with_embedding)
    pack_ref[...] = packed(new_ref)


def merge_kernel(splits, terms, place_ref, *refs):
    sums, refs = refs[: 2 * terms], refs[2 * terms :]
    outs = max(1, len(splits))
    keeps, sends, sum_ref = refs[0 : 2 * outs : 2], refs[1 : 2 * outs : 2], refs[2 * outs]
    first = 0
    for keep_ref, got_ref in zip(sums[0::2], sums[1::2]):
        count = keep_ref.shape[0]
        sum_ref[first : first + count, :] = keep_ref[...] + got_ref[...].astype(f32)
        first += count
    for keep_ref, send_ref, (start, count, rows, bit) in zip(keeps, sends, splits):
        split_pieces(sum_ref.at[start : start + count], rows, place_ref, bit, keep_ref, send_ref)
    if not splits:
        keeps[0][...] = sum_ref[...]
        sends[0][...] = sum_ref[...].astype(bf16)


def pair_kernel(keep_ref, got_ref, new_ref, send_ref):
    total = keep_ref[...].astype(bf16).astype(f32) + got_ref[...].astype(f32)
    new_ref[...] = total
    send_ref[...] = total.astype(bf16)


def finish_kernel(keep_ref, got_ref, state_ref, new_ref, share_ref, taps_ref, emb_ref):
    share_ref[...] = keep_ref[...].astype(bf16).astype(f32) + got_ref[...].astype(f32)
    total = merged(state_ref, new_ref[...])
    for row in range(7):
        taps_ref[row] = total[row * 7 : row * 7 + 7, :]
    emb_ref[...] = total[TAPS : TAPS + 1, :]


def middle_kernel(adj_ref, grad_ref, kern_ref, out_ref, pad_ref):
    capacity, parts = adj_ref.shape[0], grad_ref.shape[1] // LANES

    def own_at(tile, row):
        at = tile * 64 + row * 8
        return grad_ref[pl.ds(at if isinstance(at, int) else pl.multiple_of(at, 8), 8), :]

    fill_middle(pad_ref, own_at, adj_ref, capacity, 0, parts)

    def finish(tile, lane, sums):
        for row in range(8):
            out_ref[pl.ds(tile * 64 + row * 8, 8), lanes(lane)] = sums[row]

    convolve(
        [(pad_ref, 8, 3)],
        lambda row, col, lane: kern_ref[6 - row, 6 - col : 7 - col, lanes(lane)],
        finish, capacity, parts,
    )


def outer_kernel(
    adj_ref, place_ref, counts_ref, pool_ref, part_ref, core_ref, cross_ref, kern_ref, up_ref, cot_ref,
    out_ref, pad_ref,
):
    capacity, parts = adj_ref.shape[0], part_ref.shape[1] // LANES
    odd = is_odd(place_ref)
    fill_edge(pad_ref, core_ref, cross_ref, odd, adj_ref, capacity, UPPER, 0, parts)
    fill_edge(pad_ref, cross_ref, core_ref, odd, adj_ref, capacity, LOWER, 3, parts)

    def finish(tile, lane, sums):
        live = is_live(counts_ref, tile)
        extra = pool_ref[0, tile] * cot_ref[:, lanes(lane)] * 0.125
        for row in range(8):
            at = pl.ds(tile * 64 + row * 8, 8)
            total = live * (up_ref[at, lanes(lane)].astype(f32) + extra) + part_ref[at, lanes(lane)]
            if sums[row] is not None:
                total = total + sums[row]
            out_ref[at, lanes(lane)] = (live * total).astype(bf16)

    convolve(
        [(pad_ref.at[:, :, 0:3], 3, 0), (pad_ref.at[:, :, 3:6], 3, 11)],
        lambda row, col, lane: kern_ref[6 - row, 6 - col : 7 - col, lanes(lane)],
        finish, capacity, parts,
    )


def whole_pass(
    tiles_in, upstream, pool_weight, slide_cot, adjacency, counts, kernel, norm_gain, w_in, w_out,
    layer_scale,
):
    own = tiles_in[0]
    capacity, _, _, channels = own.shape
    parts = channels // LANES
    hidden = w_in.shape[1]
    pixels = capacity * 64
    up = upstream.reshape(pixels, channels)
    wanted = adjacency[0]
    edge_shape = (capacity, 3, 8, channels)
    count = lax.axis_size("space")
    stages = count.bit_length() - 1
    rows = hidden // count
    place = lax.axis_index("space").astype(jnp.int32).reshape(1, 1)

    core, cross = call(
        edge_kernel, [struct(edge_shape, bf16)] * 2, [SMEM, VMEM], [place, own],
        flops=EDGE_COST,
    )
    cross = crossed(cross)
    core = swapped(core, "space", 1)

    pad, conv, mixed, act_grad, own_sum = call(
        early_kernel,
        [
            struct((parts, capacity, 8, 24, LANES)),
            struct((pixels, channels)),
            struct((pixels, channels + LANES), bf16),
            struct((pixels, hidden)),
            struct((1, channels)),
        ],
        [SMEM, VMEM, SMEM] + [VMEM] * 6,
        [wanted, counts, pool_weight, slide_cot, layer_scale, kernel, own, up, w_out],
        flops=2 * pixels * channels * hidden,
    )
    edge, normed, inv, pre, cdf, keep, send, pooled = call(
        functools.partial(forward_kernel, rows),
        [
            struct((parts, capacity, 6, 24, LANES)),
            struct((pixels, channels)),
            struct((pixels, 1)),
            struct((pixels, hidden)),
            struct((pixels, hidden)),
            struct((hidden // 2, channels)),
            struct((hidden // 2, channels), bf16),
            struct((hidden, LANES)),
        ],
        [SMEM] * 2 + [VMEM] * 7,
        [wanted, place, core, cross, conv, kernel, norm_gain, w_in, mixed],
        flops=4 * pixels * channels * hidden,
        scratch=[pltpu.VMEM((pixels, channels), f32)],
    )
    got = swapped(send, "space", 1)

    grad, core, cross, emb = call(
        back_kernel,
        [
            struct((pixels, channels)),
            struct(edge_shape, bf16),
            struct(edge_shape, bf16),
            struct((1, channels)),
        ],
        [SMEM, VMEM, SMEM] + [VMEM] * 11,
        [place, counts, pool_weight, pre, cdf, act_grad, w_in, normed, inv, norm_gain, pooled, w_out, layer_scale, own_sum],
        flops=2 * pixels * channels * hidden,
    )
    cross = crossed(cross)
    core = swapped(core, "space", 1)

    def merge(parts_, splits):
        held = sum(keep.shape[0] for keep, _ in parts_)
        shapes = []
        for size in [count // 2 for _, count, _, _ in splits] or [held]:
            shapes += [struct((size, channels)), struct((size, channels), bf16)]
        operands = [array for pair in parts_ for array in pair]
        out = call(
            functools.partial(merge_kernel, splits, len(parts_)), shapes,
            [SMEM] + [VMEM] * len(operands), [place] + operands,
            scratch=[pltpu.VMEM((held, channels), f32)],
        )
        return list(zip(out[0::2], out[1::2]))

    half = hidden // 4
    (keep_a, send_a), (keep_b, send_b) = merge([(keep, got)], [(0, half, rows, 1), (half, half, 2 * rows, 2)])
    got_a = swapped(send_a, "space", 2)
    got_b = swapped(send_b, "space", 4)
    half //= 2
    (keep_a, send_a), (keep_b, send_b) = merge(
        [(keep_a, got_a), (keep_b, got_b)], [(0, half, rows, 2), (half, half, rows, 1)]
    )
    got_a = swapped(send_a, "space", 4)
    got_b = swapped(send_b, "space", 2)
    held = [(keep_a, got_a), (keep_b, got_b)]
    for stage in range(3, stages):
        size = hidden >> stage
        ((keep, send),) = merge(held, [(0, size, rows, stage)])
        got = swapped(send, "space", 1 << stage)
        held = [(keep, got)]
    ((share, send),) = merge(held, [])
    groups = lax.axis_size("dp")
    bit = 1
    while bit < groups:
        got = swapped(send, "dp", bit)
        bit *= 2
        if bit < groups:
            share, send = call(pair_kernel, [struct(share.shape), struct(send.shape, bf16)], [VMEM] * 2, [share, got])

    state, pack = call(
        taps_kernel, [struct((STATE, channels)), struct((STATE, channels), bf16)],
        [VMEM] * 4, [pad, edge, grad, emb],
        scratch=[pltpu.VMEM((TAPS, 8, channels), f32)],
    )
    steps = [("space", 1)] + [("dp", 1 << n) for n in range(groups.bit_length() - 1)]
    steps += [("space", 1 << n) for n in range(1, stages)]
    for axis, bit in steps:
        new = swapped(pack, axis, bit)
        if (axis, bit) != steps[-1]:
            state, pack = call(
                functools.partial(state_kernel, axis == "space"),
                [struct((STATE, channels)), struct((STATE, channels), bf16)],
                [VMEM] * 2, [state, new],
            )

    share, tap_grad, embedding = call(
        finish_kernel, [struct((rows, channels)), struct(kernel.shape), struct((1, channels))],
        [VMEM] * 4, [share, got, state, new],
    )

    part = call(
        middle_kernel, struct((pixels, channels)), [SMEM] + [VMEM] * 2, [wanted, grad, kernel],
        scratch=[pltpu.VMEM((parts, capacity, 8, 24, LANES), f32)],
    )
    grad_tiles = call(
        outer_kernel, struct((pixels, channels), bf16),
        [SMEM] * 2 + [VMEM, SMEM] + [VMEM] * 6,
        [wanted, place, counts, pool_weight, part, core, cross, kernel, up, slide_cot],
        scratch=[pltpu.VMEM((parts, capacity, 6, 24, LANES), f32)],
    )
    return (
        embedding,
        grad_tiles.reshape(tiles_in.shape),
        share,
        tap_grad,
    )


def solution(mesh):
    return jax.shard_map(
        whole_pass,
        mesh=mesh,
        in_specs=(
            P("dp", "space", None, None, None),
            P("dp", "space", None, None, None),
            P("dp", "space"),
            P("dp", None),
            P("dp", "space", None),
            P("dp", "space"),
            P(),
            P(),
            P(),
            P(),
            P(),
        ),
        out_specs=(P("dp", None), P("dp", "space", None, None, None), P("space", None), P()),
        check_vma=False,
    )
```

```python
import functools

import jax
import jax.numpy as jnp
from jax import lax
from jax.experimental import pallas as pl
from jax.experimental.pallas import tpu as pltpu
from jax.sharding import PartitionSpec as P

sqrt_half = 0.7071067811865476
inv_root_two_pi = 0.3989422804014327
f32 = jnp.float32
bf16 = jnp.bfloat16
LANES = 128

VMEM = pl.BlockSpec(memory_space=pltpu.VMEM)
SMEM = pl.BlockSpec(memory_space=pltpu.SMEM)
HBM = pl.BlockSpec(memory_space=pltpu.HBM)
STATE = 56
TAPS = 49
CHUNK = 384
BACK_CHUNK = 384
EDGE_COST = 5_000_000_000


def call(body, out_shape, in_specs, args, flops=0, scratch=(), limit=16 << 20, out_specs=None):
    outs = out_shape if isinstance(out_shape, (list, tuple)) else [out_shape]
    total = sum(a.size * a.dtype.itemsize for a in list(args) + list(outs))
    return pl.pallas_call(
        body,
        out_shape=out_shape,
        in_specs=in_specs,
        out_specs=out_specs or jax.tree.map(lambda _: VMEM, out_shape),
        scratch_shapes=scratch,
        compiler_params=pltpu.CompilerParams(vmem_limit_bytes=limit),
        cost_estimate=pl.CostEstimate(flops=flops, bytes_accessed=total, transcendentals=0),
    )(*args)


def struct(shape, dtype=f32):
    return jax.ShapeDtypeStruct(shape, dtype)


def swapped(value, axis, bit):
    count = lax.axis_size(axis)
    return lax.ppermute(value, axis, [(source, source ^ bit) for source in range(count)])


def crossed(value):
    groups, count = lax.axis_size("dp"), lax.axis_size("space")
    targets = []
    for group in range(groups):
        for n in range(count):
            step = 1 if n % 2 else -1
            if 0 <= n + step < count:
                targets.append((group * count + n, group * count + n + step))
            elif (group ^ 1) < groups:
                targets.append((group * count + n, (group ^ 1) * count + n))
    return lax.ppermute(value, ("dp", "space"), targets)


def valid(entry):
    return jnp.where(entry >= 0, 1.0, 0.0).astype(f32)


def local(entry, capacity):
    return lax.rem(jnp.maximum(entry, 0), capacity)


def place(pad_ref, tile, row, part, value, parts):
    for lane in range(parts):
        pad_ref[lane, tile, row, pl.ds(part * 8, 8), :] = value[:, lane * LANES : (lane + 1) * LANES]


def fill_middle(pad_ref, own_at, adj_ref, capacity, first_row, parts):
    for tile in range(capacity):
        west, east = adj_ref[tile, 2], adj_ref[tile, 3]
        for row in range(8):
            place(pad_ref, tile, first_row + row, 0, own_at(local(west, capacity), row) * valid(west), parts)
            place(pad_ref, tile, first_row + row, 1, own_at(tile, row), parts)
            place(pad_ref, tile, first_row + row, 2, own_at(local(east, capacity), row) * valid(east), parts)


def fill_edge(pad_ref, odd_ref, even_ref, odd, adj_ref, capacity, entries, first_row, parts):
    for tile in range(capacity):
        for part, entry in enumerate(entries):
            wanted = adj_ref[tile, entry]
            index, keep = local(wanted, capacity), valid(wanted)
            for row in range(3):
                value = odd_ref[index, row].astype(f32) * (keep * odd)
                value = value + even_ref[index, row].astype(f32) * (keep * (1.0 - odd))
                place(pad_ref, tile, first_row + row, part, value, parts)


def is_live(counts_ref, tile):
    return jnp.where(tile < counts_ref[...], 1.0, 0.0).astype(f32)


def is_odd(place_ref):
    return lax.rem(place_ref[0, 0], 2).astype(f32)


UPPER, LOWER = (4, 0, 5), (6, 1, 7)


def convolve(pads, tap_row, finish, capacity, parts, between=()):
    for lane in range(parts):

        def one_tile(tile):
            sums = [None] * 8
            for col in range(7):
                taps = [tap_row(row, col, lane) for row in range(7)]
                for ref, rows, base in pads:
                    for held in range(rows):
                        window = ref[lane, tile, held, pl.ds(5 + col, 8), :]
                        for out in range(8):
                            tap = held + base - out
                            if 0 <= tap < 7:
                                term = window * taps[tap]
                                sums[out] = term if sums[out] is None else sums[out] + term
            finish(tile, lane, sums)
            return 0

        for tile in range(capacity):
            one_tile(tile)
            if lane * capacity + tile < len(between):
                between[lane * capacity + tile]()


def lanes(lane):
    return slice(lane * LANES, (lane + 1) * LANES)


def swap_edges(last, first, odd, core_ref, cross_ref):
    core_ref[...] = (first * odd + last * (1.0 - odd)).astype(bf16)
    cross_ref[...] = (last * odd + first * (1.0 - odd)).astype(bf16)


def edge_kernel(place_ref, tiles_ref, core_ref, cross_ref):
    swap_edges(
        tiles_ref[:, 5:8].astype(f32), tiles_ref[:, 0:3].astype(f32), is_odd(place_ref), core_ref, cross_ref
    )


def early_kernel(
    adj_ref, counts_ref, pool_ref, cot_ref, scale_ref, kern_ref, tiles_ref, up_ref, w_out_ref,
    pad_ref, conv_ref, mixed_ref, act_grad_ref, own_sum_ref,
):
    capacity, parts = tiles_ref.shape[0], tiles_ref.shape[3] // LANES
    pixels = 64
    channels = tiles_ref.shape[3]
    fill_middle(pad_ref, lambda t, r: tiles_ref[t, r].astype(f32), adj_ref, capacity, 0, parts)
    own_sum = jnp.zeros((1, channels), f32)
    scale = scale_ref[...].reshape(1, channels)
    for tile in range(capacity):
        live = is_live(counts_ref, tile)
        pool = pool_ref[0, tile]
        rows = slice(tile * pixels, (tile + 1) * pixels)
        out_grad = live * (up_ref[rows, :].astype(f32) + pool * cot_ref[...] * 0.125)
        mixed_ref[rows, 0:channels] = (out_grad * scale).astype(bf16)
        column = lax.broadcasted_iota(jnp.int32, (pixels, LANES), 1)
        mixed_ref[rows, channels:] = jnp.where(column == tile, 1.0, 0.0).astype(bf16)
        own = tiles_ref[tile].astype(f32)
        own_sum += live * pool * jnp.sum(own.reshape(pixels, channels), axis=0, keepdims=True)
    own_sum_ref[...] = own_sum

    def product(at):
        act_grad_ref[:, at] = lax.dot_general(
            mixed_ref[:, 0:channels], w_out_ref[at, :], (((1,), (1,)), ((), ())), preferred_element_type=f32
        )

    hidden = w_out_ref.shape[0]
    step = 256 if hidden % 256 == 0 else hidden
    products = [functools.partial(product, slice(n, n + step)) for n in range(0, hidden, step)]

    def finish(tile, lane, sums):
        for row in range(8):
            conv_ref[pl.ds(tile * pixels + row * 8, 8), lanes(lane)] = sums[row]

    convolve(
        [(pad_ref, 8, 3)],
        lambda row, col, lane: kern_ref[row, col : col + 1, lanes(lane)],
        finish, capacity, parts, products,
    )


def split_pieces(value_ref, rows, place_ref, stage, keep_ref, send_ref):
    side = lax.rem(lax.div(place_ref[0, 0], 1 << stage), 2)
    for pair in range(value_ref.shape[0] // (2 * rows)):
        here = pl.ds(pair * rows, rows)
        mine = pl.ds(pl.multiple_of((2 * pair + side) * rows, 8), rows)
        other = pl.ds(pl.multiple_of((2 * pair + 1 - side) * rows, 8), rows)
        keep_ref[here, :] = value_ref[mine, :]
        send_ref[here, :] = value_ref[other, :].astype(bf16)


def forward_kernel(
    rows, adj_ref, place_ref, core_ref, cross_ref, conv_ref, kern_ref, gain_ref, w_in_ref, mixed_ref,
    edge_ref, normed_ref, inv_ref, lifted_ref, *outs,
):
    *outs, whole_ref = outs
    capacity, parts = adj_ref.shape[0], conv_ref.shape[1] // LANES
    channels = conv_ref.shape[1]
    pixels = 64
    odd = is_odd(place_ref)
    fill_edge(edge_ref, core_ref, cross_ref, odd, adj_ref, capacity, UPPER, 0, parts)
    fill_edge(edge_ref, cross_ref, core_ref, odd, adj_ref, capacity, LOWER, 3, parts)

    def finish(tile, lane, sums):
        for row in range(8):
            at = pl.ds(tile * pixels + row * 8, 8)
            total = conv_ref[at, lanes(lane)]
            if sums[row] is not None:
                total = total + sums[row]
            whole_ref[at, lanes(lane)] = total

    convolve(
        [(edge_ref.at[:, :, 0:3], 3, 0), (edge_ref.at[:, :, 3:6], 3, 11)],
        lambda row, col, lane: kern_ref[row, col : col + 1, lanes(lane)],
        finish, capacity, parts,
    )
    conv = whole_ref[...]
    centred = conv - jnp.mean(conv, axis=-1, keepdims=True)
    inv_std = lax.rsqrt(jnp.mean(centred * centred, axis=-1, keepdims=True) + 1e-06)
    normed = centred * inv_std
    normed_ref[...] = normed
    inv_ref[...] = inv_std
    lifted_ref[...] = (normed * gain_ref[...].reshape(1, channels)).astype(bf16)
    expand(rows, 0, place_ref, lifted_ref, w_in_ref, mixed_ref, *outs)


def rest_kernel(rows, place_ref, lifted_ref, w_in_ref, mixed_ref, *outs):
    expand(rows, w_in_ref.shape[1] // 2, place_ref, lifted_ref, w_in_ref, mixed_ref, *outs)


def expand(rows, base, place_ref, lifted_ref, w_in_ref, mixed_ref, pre_ref, cdf_ref, keep_ref, send_ref, pooled_ref):
    channels = lifted_ref.shape[1]
    hidden = pre_ref.shape[1]
    side = lax.rem(place_ref[0, 0], 2)
    chunk = CHUNK if hidden % CHUNK == 0 and CHUNK % (2 * rows) == 0 else hidden
    lifted = lifted_ref[...]

    def project(first):
        return jnp.dot(lifted, w_in_ref[:, base + first : base + first + chunk], preferred_element_type=f32)

    following = project(0)
    for first in range(0, hidden, chunk):
        at = slice(first, first + chunk)
        pre = following
        if first + chunk < hidden:
            following = project(first + chunk)
        cdf = 0.5 * (1.0 + lax.erf(pre * sqrt_half))
        pre_ref[:, at] = pre
        cdf_ref[:, at] = cdf
        activated = (pre * cdf).astype(bf16)
        both = lax.dot_general(
            activated, mixed_ref[...], (((0,), (0,)), ((), ())), preferred_element_type=f32
        )
        pooled_ref[at, :] = both[:, channels:]
        for block in range(0, chunk, 2 * rows):
            even = both[block : block + rows, 0:channels]
            odd_rows = both[block + rows : block + 2 * rows, 0:channels]
            out = pl.ds((first + block) // 2, rows)
            keep_ref[out, :] = jnp.where(side == 0, even, odd_rows)
            send_ref[out, :] = jnp.where(side == 0, odd_rows, even).astype(bf16)


def back_kernel(
    place_ref, counts_ref, pool_ref, pre_a_ref, cdf_a_ref, pre_b_ref, cdf_b_ref, act_grad_ref, w_in_ref,
    normed_ref, inv_ref, gain_ref, pooled_a_ref, pooled_b_ref, w_out_ref,
    scale_ref, own_sum_ref, grad_ref, core_ref, cross_ref, emb_ref,
):
    channels = normed_ref.shape[1]
    capacity = core_ref.shape[0]
    half = w_in_ref.shape[1] // 2
    chunk = BACK_CHUNK if half % BACK_CHUNK == 0 else half
    lift = None
    for base, pre_ref, cdf_ref in ((0, pre_a_ref, cdf_a_ref), (half, pre_b_ref, cdf_b_ref)):
        for first in range(0, half, chunk):
            at = slice(first, first + chunk)
            whole = slice(base + first, base + first + chunk)
            pre = pre_ref[:, at]
            density = jnp.exp(-0.5 * pre * pre) * inv_root_two_pi
            pre_grad = (act_grad_ref[:, whole] * (cdf_ref[:, at] + pre * density)).astype(bf16)
            term = lax.dot_general(
                pre_grad, w_in_ref[:, whole], (((1,), (1,)), ((), ())), preferred_element_type=f32
            )
            lift = term if lift is None else lift + term
    grad_normed = lift * gain_ref[...].reshape(1, channels)
    normed = normed_ref[...]
    grad = inv_ref[...] * (
        grad_normed
        - jnp.mean(grad_normed, axis=-1, keepdims=True)
        - normed * jnp.mean(grad_normed * normed, axis=-1, keepdims=True)
    )
    grad_ref[...] = grad
    shaped = grad.reshape(capacity, 8, 8, channels)
    swap_edges(shaped[:, 5:8], shaped[:, 0:3], is_odd(place_ref), core_ref, cross_ref)
    column = lax.broadcasted_iota(jnp.int32, (1, LANES), 1)
    weights = jnp.zeros((1, LANES), f32)
    for tile in range(capacity):
        amount = is_live(counts_ref, tile) * pool_ref[0, tile]
        weights = jnp.where(column == tile, amount, weights)
    mixed = jnp.zeros((1, channels), f32)
    for base, pooled_ref in ((0, pooled_a_ref), (half, pooled_b_ref)):
        hidden = jnp.sum(pooled_ref[...] * weights, axis=1, keepdims=True)
        mixed += jnp.sum(hidden * w_out_ref[base : base + half, :].astype(f32), axis=0, keepdims=True)
    emb_ref[...] = (own_sum_ref[...] + scale_ref[...].reshape(1, channels) * mixed) * 0.125


def taps_kernel(pad_ref, edge_ref, grad_ref, emb_ref, state_ref, pack_ref, part_ref):
    parts, capacity = pad_ref.shape[0], pad_ref.shape[1]
    for lane in range(parts):

        def one_column(col):
            def one_tile(tile, sums):
                sums = list(sums)
                grads = [grad_ref[pl.ds(tile * 64 + row * 8, 8), lanes(lane)] for row in range(8)]
                for held in range(14):
                    if 3 <= held < 11:
                        window = pad_ref[lane, tile, held - 3, pl.ds(5 + col, 8), :]
                    else:
                        row = held if held < 3 else held - 8
                        window = edge_ref[lane, tile, row, pl.ds(5 + col, 8), :]
                    for out in range(8):
                        tap = held - out
                        if 0 <= tap < 7:
                            sums[tap] = sums[tap] + window * grads[out]
                return tuple(sums)

            sums = tuple(jnp.zeros((8, LANES), f32) for _ in range(7))
            for tile in range(capacity):
                sums = one_tile(tile, sums)
            for row in range(7):
                part_ref[row * 7 + col, :, lanes(lane)] = sums[row]
            return 0

        for col in range(7):
            one_column(col)
    state_ref[0:TAPS, :] = jnp.sum(part_ref[...], axis=1)
    state_ref[TAPS : TAPS + 1, :] = emb_ref[...]
    state_ref[TAPS + 1 :, :] = jnp.zeros((STATE - TAPS - 1, emb_ref.shape[1]), f32)
    pack_ref[...] = packed(state_ref)


def packed(state_ref):
    state = state_ref[...]
    high = state.astype(bf16)
    low = pltpu.roll(state - high.astype(f32), 1, 0)
    row = lax.broadcasted_iota(jnp.int32, state.shape, 0)
    return jnp.where(row == TAPS + 1, low, high.astype(f32)).astype(bf16)


def merged(state_ref, got, with_embedding=True):
    total = packed(state_ref).astype(f32) + got.astype(f32)
    row = lax.broadcasted_iota(jnp.int32, total.shape, 0)
    if with_embedding:
        embedding = total + pltpu.roll(total, STATE - 1, 0)
    else:
        embedding = state_ref[...]
    return jnp.where(row < TAPS, total, jnp.where(row == TAPS, embedding, 0.0))


def state_kernel(with_embedding, state_ref, got_ref, new_ref, pack_ref):
    new_ref[...] = merged(state_ref, got_ref[...], with_embedding)
    pack_ref[...] = packed(new_ref)


def merge_kernel(splits, terms, place_ref, *refs):
    sums, refs = refs[: 2 * terms], refs[2 * terms :]
    outs = max(1, len(splits))
    keeps, sends, sum_ref = refs[0 : 2 * outs : 2], refs[1 : 2 * outs : 2], refs[2 * outs]
    first = 0
    for keep_ref, got_ref in zip(sums[0::2], sums[1::2]):
        count = keep_ref.shape[0]
        sum_ref[first : first + count, :] = keep_ref[...] + got_ref[...].astype(f32)
        first += count
    for keep_ref, send_ref, (start, count, rows, bit) in zip(keeps, sends, splits):
        split_pieces(sum_ref.at[start : start + count], rows, place_ref, bit, keep_ref, send_ref)
    if not splits:
        keeps[0][...] = sum_ref[...]
        sends[0][...] = sum_ref[...].astype(bf16)


def pair_kernel(keep_ref, got_ref, new_ref, send_ref):
    total = keep_ref[...].astype(bf16).astype(f32) + got_ref[...].astype(f32)
    new_ref[...] = total
    send_ref[...] = total.astype(bf16)


def finish_kernel(keep_ref, got_ref, state_ref, new_ref, share_ref, taps_ref, emb_ref):
    share_ref[...] = keep_ref[...].astype(bf16).astype(f32) + got_ref[...].astype(f32)
    total = merged(state_ref, new_ref[...])
    for row in range(7):
        taps_ref[row] = total[row * 7 : row * 7 + 7, :]
    emb_ref[...] = total[TAPS : TAPS + 1, :]


def middle_kernel(adj_ref, grad_ref, kern_ref, out_ref, pad_ref):
    capacity, parts = adj_ref.shape[0], grad_ref.shape[1] // LANES

    def own_at(tile, row):
        at = tile * 64 + row * 8
        return grad_ref[pl.ds(at if isinstance(at, int) else pl.multiple_of(at, 8), 8), :]

    fill_middle(pad_ref, own_at, adj_ref, capacity, 0, parts)

    def finish(tile, lane, sums):
        for row in range(8):
            out_ref[pl.ds(tile * 64 + row * 8, 8), lanes(lane)] = sums[row]

    convolve(
        [(pad_ref, 8, 3)],
        lambda row, col, lane: kern_ref[6 - row, 6 - col : 7 - col, lanes(lane)],
        finish, capacity, parts,
    )


def outer_kernel(
    adj_ref, place_ref, counts_ref, pool_ref, part_ref, core_ref, cross_ref, kern_ref, up_ref, cot_ref,
    out_ref, pad_ref,
):
    capacity, parts = adj_ref.shape[0], part_ref.shape[1] // LANES
    odd = is_odd(place_ref)
    fill_edge(pad_ref, core_ref, cross_ref, odd, adj_ref, capacity, UPPER, 0, parts)
    fill_edge(pad_ref, cross_ref, core_ref, odd, adj_ref, capacity, LOWER, 3, parts)

    def finish(tile, lane, sums):
        live = is_live(counts_ref, tile)
        extra = pool_ref[0, tile] * cot_ref[:, lanes(lane)] * 0.125
        for row in range(8):
            at = pl.ds(tile * 64 + row * 8, 8)
            total = live * (up_ref[at, lanes(lane)].astype(f32) + extra) + part_ref[at, lanes(lane)]
            if sums[row] is not None:
                total = total + sums[row]
            out_ref[at, lanes(lane)] = (live * total).astype(bf16)

    convolve(
        [(pad_ref.at[:, :, 0:3], 3, 0), (pad_ref.at[:, :, 3:6], 3, 11)],
        lambda row, col, lane: kern_ref[6 - row, 6 - col : 7 - col, lanes(lane)],
        finish, capacity, parts,
    )


def whole_pass(
    tiles_in, upstream, pool_weight, slide_cot, adjacency, counts, kernel, norm_gain, w_in, w_out,
    layer_scale,
):
    own = tiles_in[0]
    capacity, _, _, channels = own.shape
    parts = channels // LANES
    hidden = w_in.shape[1]
    pixels = capacity * 64
    up = upstream.reshape(pixels, channels)
    wanted = adjacency[0]
    edge_shape = (capacity, 3, 8, channels)
    count = lax.axis_size("space")
    stages = count.bit_length() - 1
    rows = hidden // count
    place = lax.axis_index("space").astype(jnp.int32).reshape(1, 1)

    core, cross = call(
        edge_kernel, [struct(edge_shape, bf16)] * 2, [SMEM, VMEM], [place, own],
        flops=EDGE_COST,
    )
    cross = crossed(cross)
    core = swapped(core, "space", 1)

    pad, conv, mixed, act_grad, own_sum = call(
        early_kernel,
        [
            struct((parts, capacity, 8, 24, LANES)),
            struct((pixels, channels)),
            struct((pixels, channels + LANES), bf16),
            struct((pixels, hidden)),
            struct((1, channels)),
        ],
        [SMEM, VMEM, SMEM] + [VMEM] * 6,
        [wanted, counts, pool_weight, slide_cot, layer_scale, kernel, own, up, w_out],
        flops=2 * pixels * channels * hidden,
    )
    half = hidden // 2
    expanded = [
        struct((pixels, half)),
        struct((pixels, half)),
        struct((half // 2, channels)),
        struct((half // 2, channels), bf16),
        struct((half, LANES)),
    ]
    edge, normed, inv, lifted, pre_a, cdf_a, keep_a, send_a, pooled_a = call(
        functools.partial(forward_kernel, rows),
        [
            struct((parts, capacity, 6, 24, LANES)),
            struct((pixels, channels)),
            struct((pixels, 1)),
            struct((pixels, channels), bf16),
        ] + expanded,
        [SMEM] * 2 + [VMEM] * 7,
        [wanted, place, core, cross, conv, kernel, norm_gain, w_in, mixed],
        flops=2 * pixels * channels * hidden,
        scratch=[pltpu.VMEM((pixels, channels), f32)],
    )
    got_a = swapped(send_a, "space", 1)
    pre_b, cdf_b, keep_b, send_b, pooled_b = call(
        functools.partial(rest_kernel, rows), expanded, [SMEM] + [VMEM] * 3, [place, lifted, w_in, mixed],
        flops=2 * pixels * channels * hidden,
    )
    got_b = swapped(send_b, "space", 1)

    grad, core, cross, emb = call(
        back_kernel,
        [
            struct((pixels, channels)),
            struct(edge_shape, bf16),
            struct(edge_shape, bf16),
            struct((1, channels)),
        ],
        [SMEM, VMEM, SMEM] + [VMEM] * 14,
        [place, counts, pool_weight, pre_a, cdf_a, pre_b, cdf_b, act_grad, w_in, normed, inv, norm_gain,
         pooled_a, pooled_b, w_out, layer_scale, own_sum],
        flops=2 * pixels * channels * hidden,
    )
    cross = crossed(cross)
    core = swapped(core, "space", 1)

    def merge(parts_, splits):
        held = sum(keep.shape[0] for keep, _ in parts_)
        shapes = []
        for size in [count // 2 for _, count, _, _ in splits] or [held]:
            shapes += [struct((size, channels)), struct((size, channels), bf16)]
        operands = [array for pair in parts_ for array in pair]
        out = call(
            functools.partial(merge_kernel, splits, len(parts_)), shapes,
            [SMEM] + [VMEM] * len(operands), [place] + operands,
            scratch=[pltpu.VMEM((held, channels), f32)],
        )
        return list(zip(out[0::2], out[1::2]))

    half = hidden // 4
    ((keep_a, send_a),) = merge([(keep_a, got_a)], [(0, half, rows, 1)])
    got_a = swapped(send_a, "space", 2)
    ((keep_b, send_b),) = merge([(keep_b, got_b)], [(0, half, 2 * rows, 2)])
    got_b = swapped(send_b, "space", 4)
    half //= 2
    (keep_a, send_a), (keep_b, send_b) = merge(
        [(keep_a, got_a), (keep_b, got_b)], [(0, half, rows, 2), (half, half, rows, 1)]
    )
    got_a = swapped(send_a, "space", 4)
    got_b = swapped(send_b, "space", 2)
    held = [(keep_a, got_a), (keep_b, got_b)]
    for stage in range(3, stages):
        size = hidden >> stage
        ((keep, send),) = merge(held, [(0, size, rows, stage)])
        got = swapped(send, "space", 1 << stage)
        held = [(keep, got)]
    ((share, send),) = merge(held, [])
    groups = lax.axis_size("dp")
    bit = 1
    while bit < groups:
        got = swapped(send, "dp", bit)
        bit *= 2
        if bit < groups:
            share, send = call(pair_kernel, [struct(share.shape), struct(send.shape, bf16)], [VMEM] * 2, [share, got])

    state, pack = call(
        taps_kernel, [struct((STATE, channels)), struct((STATE, channels), bf16)],
        [VMEM] * 4, [pad, edge, grad, emb],
        scratch=[pltpu.VMEM((TAPS, 8, channels), f32)],
    )
    steps = [("space", 1)] + [("dp", 1 << n) for n in range(groups.bit_length() - 1)]
    steps += [("space", 1 << n) for n in range(1, stages)]
    for axis, bit in steps:
        new = swapped(pack, axis, bit)
        if (axis, bit) != steps[-1]:
            state, pack = call(
                functools.partial(state_kernel, axis == "space"),
                [struct((STATE, channels)), struct((STATE, channels), bf16)],
                [VMEM] * 2, [state, new],
            )

    share, tap_grad, embedding = call(
        finish_kernel, [struct((rows, channels)), struct(kernel.shape), struct((1, channels))],
        [VMEM] * 4, [share, got, state, new],
    )

    part = call(
        middle_kernel, struct((pixels, channels)), [SMEM] + [VMEM] * 2, [wanted, grad, kernel],
        scratch=[pltpu.VMEM((parts, capacity, 8, 24, LANES), f32)],
    )
    grad_tiles = call(
        outer_kernel, struct((pixels, channels), bf16),
        [SMEM] * 2 + [VMEM, SMEM] + [VMEM] * 6,
        [wanted, place, counts, pool_weight, part, core, cross, kernel, up, slide_cot],
        scratch=[pltpu.VMEM((parts, capacity, 6, 24, LANES), f32)],
    )
    return (
        embedding,
        grad_tiles.reshape(tiles_in.shape),
        share,
        tap_grad,
    )


def solution(mesh):
    return jax.shard_map(
        whole_pass,
        mesh=mesh,
        in_specs=(
            P("dp", "space", None, None, None),
            P("dp", "space", None, None, None),
            P("dp", "space"),
            P("dp", None),
            P("dp", "space", None),
            P("dp", "space"),
            P(),
            P(),
            P(),
            P(),
            P(),
        ),
        out_specs=(P("dp", None), P("dp", "space", None, None, None), P("space", None), P()),
        check_vma=False,
    )
```

```python
import functools

import jax
import jax.numpy as jnp
from jax import lax
from jax.experimental import pallas as pl
from jax.experimental.pallas import tpu as pltpu
from jax.sharding import PartitionSpec as P

sqrt_half = 0.7071067811865476
inv_root_two_pi = 0.3989422804014327
f32 = jnp.float32
bf16 = jnp.bfloat16
LANES = 128

VMEM = pl.BlockSpec(memory_space=pltpu.VMEM)
SMEM = pl.BlockSpec(memory_space=pltpu.SMEM)
HBM = pl.BlockSpec(memory_space=pltpu.HBM)
STATE = 56
TAPS = 49
CHUNK = 384
BACK_CHUNK = 384
EDGE_COST = 5_000_000_000


def call(body, out_shape, in_specs, args, flops=0, scratch=(), limit=16 << 20, out_specs=None):
    outs = out_shape if isinstance(out_shape, (list, tuple)) else [out_shape]
    total = sum(a.size * a.dtype.itemsize for a in list(args) + list(outs))
    return pl.pallas_call(
        body,
        out_shape=out_shape,
        in_specs=in_specs,
        out_specs=out_specs or jax.tree.map(lambda _: VMEM, out_shape),
        scratch_shapes=scratch,
        compiler_params=pltpu.CompilerParams(vmem_limit_bytes=limit),
        cost_estimate=pl.CostEstimate(flops=flops, bytes_accessed=total, transcendentals=0),
    )(*args)


def struct(shape, dtype=f32):
    return jax.ShapeDtypeStruct(shape, dtype)


def swapped(value, axis, bit):
    count = lax.axis_size(axis)
    return lax.ppermute(value, axis, [(source, source ^ bit) for source in range(count)])


def crossed(value):
    groups, count = lax.axis_size("dp"), lax.axis_size("space")
    targets = []
    for group in range(groups):
        for n in range(count):
            step = 1 if n % 2 else -1
            if 0 <= n + step < count:
                targets.append((group * count + n, group * count + n + step))
            elif (group ^ 1) < groups:
                targets.append((group * count + n, (group ^ 1) * count + n))
    return lax.ppermute(value, ("dp", "space"), targets)


def valid(entry):
    return jnp.where(entry >= 0, 1.0, 0.0).astype(f32)


def local(entry, capacity):
    return lax.rem(jnp.maximum(entry, 0), capacity)


def place(pad_ref, tile, row, part, value, parts):
    for lane in range(parts):
        pad_ref[lane, tile, row, pl.ds(part * 8, 8), :] = value[:, lane * LANES : (lane + 1) * LANES]


def fill_middle(pad_ref, own_at, adj_ref, capacity, first_row, parts):
    for tile in range(capacity):
        west, east = adj_ref[tile, 2], adj_ref[tile, 3]
        for row in range(8):
            place(pad_ref, tile, first_row + row, 0, own_at(local(west, capacity), row) * valid(west), parts)
            place(pad_ref, tile, first_row + row, 1, own_at(tile, row), parts)
            place(pad_ref, tile, first_row + row, 2, own_at(local(east, capacity), row) * valid(east), parts)


def fill_edge(pad_ref, odd_ref, even_ref, odd, adj_ref, capacity, entries, first_row, parts):
    for tile in range(capacity):
        for part, entry in enumerate(entries):
            wanted = adj_ref[tile, entry]
            index, keep = local(wanted, capacity), valid(wanted)
            for row in range(3):
                value = odd_ref[index, row].astype(f32) * (keep * odd)
                value = value + even_ref[index, row].astype(f32) * (keep * (1.0 - odd))
                place(pad_ref, tile, first_row + row, part, value, parts)


def is_live(counts_ref, tile):
    return jnp.where(tile < counts_ref[...], 1.0, 0.0).astype(f32)


def is_odd(place_ref):
    return lax.rem(place_ref[0, 0], 2).astype(f32)


UPPER, LOWER = (4, 0, 5), (6, 1, 7)


def convolve(pads, tap_row, finish, capacity, parts, between=()):
    for lane in range(parts):

        def one_tile(tile):
            sums = [None] * 8
            for col in range(7):
                taps = [tap_row(row, col, lane) for row in range(7)]
                for ref, rows, base in pads:
                    for held in range(rows):
                        window = ref[lane, tile, held, pl.ds(5 + col, 8), :]
                        for out in range(8):
                            tap = held + base - out
                            if 0 <= tap < 7:
                                term = window * taps[tap]
                                sums[out] = term if sums[out] is None else sums[out] + term
            finish(tile, lane, sums)
            return 0

        for tile in range(capacity):
            one_tile(tile)
            if lane * capacity + tile < len(between):
                between[lane * capacity + tile]()


def lanes(lane):
    return slice(lane * LANES, (lane + 1) * LANES)


def swap_edges(last, first, odd, core_ref, cross_ref):
    core_ref[...] = (first * odd + last * (1.0 - odd)).astype(bf16)
    cross_ref[...] = (last * odd + first * (1.0 - odd)).astype(bf16)


def edge_kernel(place_ref, tiles_ref, core_ref, cross_ref):
    swap_edges(
        tiles_ref[:, 5:8].astype(f32), tiles_ref[:, 0:3].astype(f32), is_odd(place_ref), core_ref, cross_ref
    )


def early_kernel(
    adj_ref, counts_ref, pool_ref, cot_ref, scale_ref, kern_ref, tiles_ref, up_ref, w_out_ref,
    pad_ref, conv_ref, mixed_ref, act_grad_ref, own_sum_ref,
):
    capacity, parts = tiles_ref.shape[0], tiles_ref.shape[3] // LANES
    pixels = 64
    channels = tiles_ref.shape[3]
    fill_middle(pad_ref, lambda t, r: tiles_ref[t, r].astype(f32), adj_ref, capacity, 0, parts)
    own_sum = jnp.zeros((1, channels), f32)
    scale = scale_ref[...].reshape(1, channels)
    for tile in range(capacity):
        live = is_live(counts_ref, tile)
        pool = pool_ref[0, tile]
        rows = slice(tile * pixels, (tile + 1) * pixels)
        out_grad = live * (up_ref[rows, :].astype(f32) + pool * cot_ref[...] * 0.125)
        mixed_ref[rows, 0:channels] = (out_grad * scale).astype(bf16)
        column = lax.broadcasted_iota(jnp.int32, (pixels, LANES), 1)
        mixed_ref[rows, channels:] = jnp.where(column == tile, 1.0, 0.0).astype(bf16)
        own = tiles_ref[tile].astype(f32)
        own_sum += live * pool * jnp.sum(own.reshape(pixels, channels), axis=0, keepdims=True)
    own_sum_ref[...] = own_sum

    def product(at):
        act_grad_ref[:, at] = lax.dot_general(
            mixed_ref[:, 0:channels], w_out_ref[at, :], (((1,), (1,)), ((), ())), preferred_element_type=f32
        )

    hidden = w_out_ref.shape[0]
    step = 256 if hidden % 256 == 0 else hidden
    products = [functools.partial(product, slice(n, n + step)) for n in range(0, hidden, step)]

    def finish(tile, lane, sums):
        for row in range(8):
            conv_ref[pl.ds(tile * pixels + row * 8, 8), lanes(lane)] = sums[row]

    convolve(
        [(pad_ref, 8, 3)],
        lambda row, col, lane: kern_ref[row, col : col + 1, lanes(lane)],
        finish, capacity, parts, products,
    )


def split_pieces(value_ref, rows, place_ref, stage, keep_ref, send_ref):
    side = lax.rem(lax.div(place_ref[0, 0], 1 << stage), 2)
    for pair in range(value_ref.shape[0] // (2 * rows)):
        here = pl.ds(pair * rows, rows)
        mine = pl.ds(pl.multiple_of((2 * pair + side) * rows, 8), rows)
        other = pl.ds(pl.multiple_of((2 * pair + 1 - side) * rows, 8), rows)
        keep_ref[here, :] = value_ref[mine, :]
        send_ref[here, :] = value_ref[other, :].astype(bf16)


def forward_kernel(
    rows, adj_ref, place_ref, core_ref, cross_ref, conv_ref, kern_ref, gain_ref, w_in_ref, mixed_ref,
    edge_ref, normed_ref, inv_ref, lifted_ref, *outs,
):
    *outs, whole_ref = outs
    capacity, parts = adj_ref.shape[0], conv_ref.shape[1] // LANES
    channels = conv_ref.shape[1]
    pixels = 64
    odd = is_odd(place_ref)
    fill_edge(edge_ref, core_ref, cross_ref, odd, adj_ref, capacity, UPPER, 0, parts)
    fill_edge(edge_ref, cross_ref, core_ref, odd, adj_ref, capacity, LOWER, 3, parts)

    def finish(tile, lane, sums):
        for row in range(8):
            at = pl.ds(tile * pixels + row * 8, 8)
            total = conv_ref[at, lanes(lane)]
            if sums[row] is not None:
                total = total + sums[row]
            whole_ref[at, lanes(lane)] = total

    convolve(
        [(edge_ref.at[:, :, 0:3], 3, 0), (edge_ref.at[:, :, 3:6], 3, 11)],
        lambda row, col, lane: kern_ref[row, col : col + 1, lanes(lane)],
        finish, capacity, parts,
    )
    conv = whole_ref[...]
    centred = conv - jnp.mean(conv, axis=-1, keepdims=True)
    inv_std = lax.rsqrt(jnp.mean(centred * centred, axis=-1, keepdims=True) + 1e-06)
    normed = centred * inv_std
    normed_ref[...] = normed
    inv_ref[...] = inv_std
    lifted_ref[...] = (normed * gain_ref[...].reshape(1, channels)).astype(bf16)
    expand(rows, 0, place_ref, lifted_ref, w_in_ref, mixed_ref, *outs)


def rest_kernel(rows, place_ref, lifted_ref, w_in_ref, mixed_ref, *outs):
    expand(rows, w_in_ref.shape[1] // 2, place_ref, lifted_ref, w_in_ref, mixed_ref, *outs)


def expand(rows, base, place_ref, lifted_ref, w_in_ref, mixed_ref, pre_ref, cdf_ref, keep_ref, send_ref, pooled_ref):
    channels = lifted_ref.shape[1]
    hidden = pre_ref.shape[1]
    side = lax.rem(place_ref[0, 0], 2)
    chunk = CHUNK if hidden % CHUNK == 0 and CHUNK % (2 * rows) == 0 else hidden
    lifted = lifted_ref[...]

    def project(first):
        return jnp.dot(lifted, w_in_ref[:, base + first : base + first + chunk], preferred_element_type=f32)

    following = project(0)
    for first in range(0, hidden, chunk):
        at = slice(first, first + chunk)
        pre = following
        if first + chunk < hidden:
            following = project(first + chunk)
        cdf = 0.5 * (1.0 + lax.erf(pre * sqrt_half))
        pre_ref[:, at] = pre
        cdf_ref[:, at] = cdf
        activated = (pre * cdf).astype(bf16)
        both = lax.dot_general(
            activated, mixed_ref[...], (((0,), (0,)), ((), ())), preferred_element_type=f32
        )
        pooled_ref[at, :] = both[:, channels:]
        for block in range(0, chunk, 2 * rows):
            even = both[block : block + rows, 0:channels]
            odd_rows = both[block + rows : block + 2 * rows, 0:channels]
            out = pl.ds((first + block) // 2, rows)
            keep_ref[out, :] = jnp.where(side == 0, even, odd_rows)
            send_ref[out, :] = jnp.where(side == 0, odd_rows, even).astype(bf16)


def back_kernel(
    place_ref, counts_ref, pool_ref, pre_a_ref, cdf_a_ref, pre_b_ref, cdf_b_ref, act_grad_ref, w_in_ref,
    normed_ref, inv_ref, gain_ref, pooled_a_ref, pooled_b_ref, w_out_ref,
    scale_ref, own_sum_ref, grad_ref, core_ref, cross_ref, emb_ref,
):
    channels = normed_ref.shape[1]
    capacity = core_ref.shape[0]
    half = w_in_ref.shape[1] // 2
    chunk = BACK_CHUNK if half % BACK_CHUNK == 0 else half
    lift = None
    for base, pre_ref, cdf_ref in ((0, pre_a_ref, cdf_a_ref), (half, pre_b_ref, cdf_b_ref)):
        for first in range(0, half, chunk):
            at = slice(first, first + chunk)
            whole = slice(base + first, base + first + chunk)
            pre = pre_ref[:, at]
            density = jnp.exp(-0.5 * pre * pre) * inv_root_two_pi
            pre_grad = (act_grad_ref[:, whole] * (cdf_ref[:, at] + pre * density)).astype(bf16)
            term = lax.dot_general(
                pre_grad, w_in_ref[:, whole], (((1,), (1,)), ((), ())), preferred_element_type=f32
            )
            lift = term if lift is None else lift + term
    grad_normed = lift * gain_ref[...].reshape(1, channels)
    normed = normed_ref[...]
    grad = inv_ref[...] * (
        grad_normed
        - jnp.mean(grad_normed, axis=-1, keepdims=True)
        - normed * jnp.mean(grad_normed * normed, axis=-1, keepdims=True)
    )
    grad_ref[...] = grad
    shaped = grad.reshape(capacity, 8, 8, channels)
    swap_edges(shaped[:, 5:8], shaped[:, 0:3], is_odd(place_ref), core_ref, cross_ref)
    column = lax.broadcasted_iota(jnp.int32, (1, LANES), 1)
    weights = jnp.zeros((1, LANES), f32)
    for tile in range(capacity):
        amount = is_live(counts_ref, tile) * pool_ref[0, tile]
        weights = jnp.where(column == tile, amount, weights)
    mixed = jnp.zeros((1, channels), f32)
    for base, pooled_ref in ((0, pooled_a_ref), (half, pooled_b_ref)):
        hidden = jnp.sum(pooled_ref[...] * weights, axis=1, keepdims=True)
        mixed += jnp.sum(hidden * w_out_ref[base : base + half, :].astype(f32), axis=0, keepdims=True)
    emb_ref[...] = (own_sum_ref[...] + scale_ref[...].reshape(1, channels) * mixed) * 0.125


def taps_kernel(pad_ref, edge_ref, grad_ref, emb_ref, state_ref, pack_ref, part_ref):
    parts, capacity = pad_ref.shape[0], pad_ref.shape[1]
    for lane in range(parts):

        def one_column(col):
            def one_tile(tile, sums):
                sums = list(sums)
                grads = [grad_ref[pl.ds(tile * 64 + row * 8, 8), lanes(lane)] for row in range(8)]
                for held in range(14):
                    if 3 <= held < 11:
                        window = pad_ref[lane, tile, held - 3, pl.ds(5 + col, 8), :]
                    else:
                        row = held if held < 3 else held - 8
                        window = edge_ref[lane, tile, row, pl.ds(5 + col, 8), :]
                    for out in range(8):
                        tap = held - out
                        if 0 <= tap < 7:
                            sums[tap] = sums[tap] + window * grads[out]
                return tuple(sums)

            sums = tuple(jnp.zeros((8, LANES), f32) for _ in range(7))
            for tile in range(capacity):
                sums = one_tile(tile, sums)
            for row in range(7):
                part_ref[row * 7 + col, :, lanes(lane)] = sums[row]
            return 0

        for col in range(7):
            one_column(col)
    state_ref[0:TAPS, :] = jnp.sum(part_ref[...], axis=1)
    state_ref[TAPS : TAPS + 1, :] = emb_ref[...]
    state_ref[TAPS + 1 :, :] = jnp.zeros((STATE - TAPS - 1, emb_ref.shape[1]), f32)
    pack_ref[...] = packed(state_ref)


def packed(state_ref):
    state = state_ref[...]
    high = state.astype(bf16)
    low = pltpu.roll(state - high.astype(f32), 1, 0)
    row = lax.broadcasted_iota(jnp.int32, state.shape, 0)
    return jnp.where(row == TAPS + 1, low, high.astype(f32)).astype(bf16)


def merged(state_ref, got, with_embedding=True):
    total = packed(state_ref).astype(f32) + got.astype(f32)
    row = lax.broadcasted_iota(jnp.int32, total.shape, 0)
    if with_embedding:
        embedding = total + pltpu.roll(total, STATE - 1, 0)
    else:
        embedding = state_ref[...]
    return jnp.where(row < TAPS, total, jnp.where(row == TAPS, embedding, 0.0))


def state_kernel(with_embedding, state_ref, got_ref, new_ref, pack_ref):
    new_ref[...] = merged(state_ref, got_ref[...], with_embedding)
    pack_ref[...] = packed(new_ref)


def merge_kernel(splits, terms, place_ref, *refs):
    sums, refs = refs[: 2 * terms], refs[2 * terms :]
    outs = max(1, len(splits))
    keeps, sends, sum_ref = refs[0 : 2 * outs : 2], refs[1 : 2 * outs : 2], refs[2 * outs]
    first = 0
    for keep_ref, got_ref in zip(sums[0::2], sums[1::2]):
        count = keep_ref.shape[0]
        sum_ref[first : first + count, :] = keep_ref[...] + got_ref[...].astype(f32)
        first += count
    for keep_ref, send_ref, (start, count, rows, bit) in zip(keeps, sends, splits):
        split_pieces(sum_ref.at[start : start + count], rows, place_ref, bit, keep_ref, send_ref)
    if not splits:
        keeps[0][...] = sum_ref[...]
        sends[0][...] = sum_ref[...].astype(bf16)


def pair_kernel(keep_ref, got_ref, new_ref, send_ref):
    total = keep_ref[...].astype(bf16).astype(f32) + got_ref[...].astype(f32)
    new_ref[...] = total
    send_ref[...] = total.astype(bf16)


def finish_kernel(keep_ref, got_ref, state_ref, new_ref, share_ref, taps_ref, emb_ref):
    share_ref[...] = keep_ref[...].astype(bf16).astype(f32) + got_ref[...].astype(f32)
    total = merged(state_ref, new_ref[...])
    for row in range(7):
        taps_ref[row] = total[row * 7 : row * 7 + 7, :]
    emb_ref[...] = total[TAPS : TAPS + 1, :]


def middle_kernel(adj_ref, grad_ref, kern_ref, out_ref, pad_ref):
    capacity, parts = adj_ref.shape[0], grad_ref.shape[1] // LANES

    def own_at(tile, row):
        at = tile * 64 + row * 8
        return grad_ref[pl.ds(at if isinstance(at, int) else pl.multiple_of(at, 8), 8), :]

    fill_middle(pad_ref, own_at, adj_ref, capacity, 0, parts)

    def finish(tile, lane, sums):
        for row in range(8):
            out_ref[pl.ds(tile * 64 + row * 8, 8), lanes(lane)] = sums[row]

    convolve(
        [(pad_ref, 8, 3)],
        lambda row, col, lane: kern_ref[6 - row, 6 - col : 7 - col, lanes(lane)],
        finish, capacity, parts,
    )


def outer_kernel(
    adj_ref, place_ref, counts_ref, pool_ref, part_ref, core_ref, cross_ref, kern_ref, up_ref, cot_ref,
    out_ref, pad_ref,
):
    capacity, parts = adj_ref.shape[0], part_ref.shape[1] // LANES
    odd = is_odd(place_ref)
    fill_edge(pad_ref, core_ref, cross_ref, odd, adj_ref, capacity, UPPER, 0, parts)
    fill_edge(pad_ref, cross_ref, core_ref, odd, adj_ref, capacity, LOWER, 3, parts)

    def finish(tile, lane, sums):
        live = is_live(counts_ref, tile)
        extra = pool_ref[0, tile] * cot_ref[:, lanes(lane)] * 0.125
        for row in range(8):
            at = pl.ds(tile * 64 + row * 8, 8)
            total = live * (up_ref[at, lanes(lane)].astype(f32) + extra) + part_ref[at, lanes(lane)]
            if sums[row] is not None:
                total = total + sums[row]
            out_ref[at, lanes(lane)] = (live * total).astype(bf16)

    convolve(
        [(pad_ref.at[:, :, 0:3], 3, 0), (pad_ref.at[:, :, 3:6], 3, 11)],
        lambda row, col, lane: kern_ref[6 - row, 6 - col : 7 - col, lanes(lane)],
        finish, capacity, parts,
    )


def whole_pass(
    tiles_in, upstream, pool_weight, slide_cot, adjacency, counts, kernel, norm_gain, w_in, w_out,
    layer_scale,
):
    own = tiles_in[0]
    capacity, _, _, channels = own.shape
    parts = channels // LANES
    hidden = w_in.shape[1]
    pixels = capacity * 64
    up = upstream.reshape(pixels, channels)
    wanted = adjacency[0]
    edge_shape = (capacity, 3, 8, channels)
    count = lax.axis_size("space")
    stages = count.bit_length() - 1
    rows = hidden // count
    place = lax.axis_index("space").astype(jnp.int32).reshape(1, 1)

    core, cross = call(
        edge_kernel, [struct(edge_shape, bf16)] * 2, [SMEM, VMEM], [place, own],
        flops=EDGE_COST,
    )
    cross = crossed(cross)
    core = swapped(core, "space", 1)

    pad, conv, mixed, act_grad, own_sum = call(
        early_kernel,
        [
            struct((parts, capacity, 8, 24, LANES)),
            struct((pixels, channels)),
            struct((pixels, channels + LANES), bf16),
            struct((pixels, hidden)),
            struct((1, channels)),
        ],
        [SMEM, VMEM, SMEM] + [VMEM] * 6,
        [wanted, counts, pool_weight, slide_cot, layer_scale, kernel, own, up, w_out],
        flops=2 * pixels * channels * hidden,
    )
    half = hidden // 2
    expanded = [
        struct((pixels, half)),
        struct((pixels, half)),
        struct((half // 2, channels)),
        struct((half // 2, channels), bf16),
        struct((half, LANES)),
    ]
    edge, normed, inv, lifted, pre_a, cdf_a, keep_a, send_a, pooled_a = call(
        functools.partial(forward_kernel, rows),
        [
            struct((parts, capacity, 6, 24, LANES)),
            struct((pixels, channels)),
            struct((pixels, 1)),
            struct((pixels, channels), bf16),
        ] + expanded,
        [SMEM] * 2 + [VMEM] * 7,
        [wanted, place, core, cross, conv, kernel, norm_gain, w_in, mixed],
        flops=2 * pixels * channels * hidden,
        scratch=[pltpu.VMEM((pixels, channels), f32)],
    )
    got_a = swapped(send_a, "space", 1)
    pre_b, cdf_b, keep_b, send_b, pooled_b = call(
        functools.partial(rest_kernel, rows), expanded, [SMEM] + [VMEM] * 3, [place, lifted, w_in, mixed],
        flops=2 * pixels * channels * hidden,
    )
    got_b = swapped(send_b, "space", 1)

    grad, core, cross, emb = call(
        back_kernel,
        [
            struct((pixels, channels)),
            struct(edge_shape, bf16),
            struct(edge_shape, bf16),
            struct((1, channels)),
        ],
        [SMEM, VMEM, SMEM] + [VMEM] * 14,
        [place, counts, pool_weight, pre_a, cdf_a, pre_b, cdf_b, act_grad, w_in, normed, inv, norm_gain,
         pooled_a, pooled_b, w_out, layer_scale, own_sum],
        flops=2 * pixels * channels * hidden,
    )
    cross = crossed(cross)
    core = swapped(core, "space", 1)

    def merge(parts_, splits):
        held = sum(keep.shape[0] for keep, _ in parts_)
        shapes = []
        for size in [count // 2 for _, count, _, _ in splits] or [held]:
            shapes += [struct((size, channels)), struct((size, channels), bf16)]
        operands = [array for pair in parts_ for array in pair]
        out = call(
            functools.partial(merge_kernel, splits, len(parts_)), shapes,
            [SMEM] + [VMEM] * len(operands), [place] + operands,
            scratch=[pltpu.VMEM((held, channels), f32)],
        )
        return list(zip(out[0::2], out[1::2]))

    half = hidden // 4
    ((keep_a, send_a),) = merge([(keep_a, got_a)], [(0, half, rows, 1)])
    got_a = swapped(send_a, "space", 2)
    ((keep_b, send_b),) = merge([(keep_b, got_b)], [(0, half, 2 * rows, 2)])
    got_b = swapped(send_b, "space", 4)
    half //= 2
    ((keep_a, send_a),) = merge([(keep_a, got_a)], [(0, half, rows, 2)])
    ((keep_b, send_b),) = merge([(keep_b, got_b)], [(0, half, rows, 1)])
    got_a = swapped(send_a, "space", 4)
    got_b = swapped(send_b, "space", 2)
    held = [(keep_a, got_a), (keep_b, got_b)]
    for stage in range(3, stages):
        size = hidden >> stage
        ((keep, send),) = merge(held, [(0, size, rows, stage)])
        got = swapped(send, "space", 1 << stage)
        held = [(keep, got)]
    ((share, send),) = merge(held, [])
    groups = lax.axis_size("dp")
    bit = 1
    while bit < groups:
        got = swapped(send, "dp", bit)
        bit *= 2
        if bit < groups:
            share, send = call(pair_kernel, [struct(share.shape), struct(send.shape, bf16)], [VMEM] * 2, [share, got])

    state, pack = call(
        taps_kernel, [struct((STATE, channels)), struct((STATE, channels), bf16)],
        [VMEM] * 4, [pad, edge, grad, emb],
        scratch=[pltpu.VMEM((TAPS, 8, channels), f32)],
    )
    steps = [("space", 1)] + [("dp", 1 << n) for n in range(groups.bit_length() - 1)]
    steps += [("space", 4), ("space", 2)] + [("space", 1 << n) for n in range(3, stages)]
    for axis, bit in steps:
        new = swapped(pack, axis, bit)
        if (axis, bit) != steps[-1]:
            state, pack = call(
                functools.partial(state_kernel, axis == "space"),
                [struct((STATE, channels)), struct((STATE, channels), bf16)],
                [VMEM] * 2, [state, new],
            )

    share, tap_grad, embedding = call(
        finish_kernel, [struct((rows, channels)), struct(kernel.shape), struct((1, channels))],
        [VMEM] * 4, [share, got, state, new],
    )

    part = call(
        middle_kernel, struct((pixels, channels)), [SMEM] + [VMEM] * 2, [wanted, grad, kernel],
        scratch=[pltpu.VMEM((parts, capacity, 8, 24, LANES), f32)],
    )
    grad_tiles = call(
        outer_kernel, struct((pixels, channels), bf16),
        [SMEM] * 2 + [VMEM, SMEM] + [VMEM] * 6,
        [wanted, place, counts, pool_weight, part, core, cross, kernel, up, slide_cot],
        scratch=[pltpu.VMEM((parts, capacity, 6, 24, LANES), f32)],
    )
    return (
        embedding,
        grad_tiles.reshape(tiles_in.shape),
        share,
        tap_grad,
    )


def solution(mesh):
    return jax.shard_map(
        whole_pass,
        mesh=mesh,
        in_specs=(
            P("dp", "space", None, None, None),
            P("dp", "space", None, None, None),
            P("dp", "space"),
            P("dp", None),
            P("dp", "space", None),
            P("dp", "space"),
            P(),
            P(),
            P(),
            P(),
            P(),
        ),
        out_specs=(P("dp", None), P("dp", "space", None, None, None), P("space", None), P()),
        check_vma=False,
    )
```

```python
import functools

import jax
import jax.numpy as jnp
from jax import lax
from jax.experimental import pallas as pl
from jax.experimental.pallas import tpu as pltpu
from jax.sharding import PartitionSpec as P

sqrt_half = 0.7071067811865476
inv_root_two_pi = 0.3989422804014327
half_log2_e = -0.7213475204444817
f32 = jnp.float32
bf16 = jnp.bfloat16
LANES = 128

VMEM = pl.BlockSpec(memory_space=pltpu.VMEM)
SMEM = pl.BlockSpec(memory_space=pltpu.SMEM)
HBM = pl.BlockSpec(memory_space=pltpu.HBM)
STATE = 56
TAPS = 49
CHUNK = 384
BACK_CHUNK = 512
EDGE_COST = 5_000_000_000


def call(body, out_shape, in_specs, args, flops=0, scratch=(), limit=16 << 20, out_specs=None):
    outs = out_shape if isinstance(out_shape, (list, tuple)) else [out_shape]
    total = sum(a.size * a.dtype.itemsize for a in list(args) + list(outs))
    return pl.pallas_call(
        body,
        out_shape=out_shape,
        in_specs=in_specs,
        out_specs=out_specs or jax.tree.map(lambda _: VMEM, out_shape),
        scratch_shapes=scratch,
        compiler_params=pltpu.CompilerParams(vmem_limit_bytes=limit),
        cost_estimate=pl.CostEstimate(flops=flops, bytes_accessed=total, transcendentals=0),
    )(*args)


def struct(shape, dtype=f32):
    return jax.ShapeDtypeStruct(shape, dtype)


def swapped(value, axis, bit):
    count = lax.axis_size(axis)
    return lax.ppermute(value, axis, [(source, source ^ bit) for source in range(count)])


def crossed(value):
    groups, count = lax.axis_size("dp"), lax.axis_size("space")
    targets = []
    for group in range(groups):
        for n in range(count):
            step = 1 if n % 2 else -1
            if 0 <= n + step < count:
                targets.append((group * count + n, group * count + n + step))
            elif (group ^ 1) < groups:
                targets.append((group * count + n, (group ^ 1) * count + n))
    return lax.ppermute(value, ("dp", "space"), targets)


def valid(entry):
    return jnp.where(entry >= 0, 1.0, 0.0).astype(f32)


def local(entry, capacity):
    return lax.rem(jnp.maximum(entry, 0), capacity)


def place(pad_ref, tile, row, part, value, parts):
    for lane in range(parts):
        pad_ref[lane, tile, row, pl.ds(part * 8, 8), :] = value[:, lane * LANES : (lane + 1) * LANES]


def fill_middle(pad_ref, own_at, adj_ref, capacity, first_row, parts):
    for tile in range(capacity):
        west, east = adj_ref[tile, 2], adj_ref[tile, 3]
        for row in range(8):
            place(pad_ref, tile, first_row + row, 0, own_at(local(west, capacity), row) * valid(west), parts)
            place(pad_ref, tile, first_row + row, 1, own_at(tile, row), parts)
            place(pad_ref, tile, first_row + row, 2, own_at(local(east, capacity), row) * valid(east), parts)


def fill_edge(pad_ref, edge_ref, adj_ref, capacity, entries, first_row, parts):
    for tile in range(capacity):
        for part, entry in enumerate(entries):
            wanted = adj_ref[tile, entry]
            index, keep = local(wanted, capacity), valid(wanted)
            for row in range(3):
                value = edge_ref[index, row].astype(f32) * keep
                place(pad_ref, tile, first_row + row, part, value, parts)


def fill_edges(pad_ref, core_ref, cross_ref, place_ref, adj_ref, capacity, parts):
    odd = lax.rem(place_ref[0, 0], 2)
    for parity, upper_ref, lower_ref in ((1, core_ref, cross_ref), (0, cross_ref, core_ref)):

        @pl.when(odd == parity)
        def _():
            fill_edge(pad_ref, upper_ref, adj_ref, capacity, UPPER, 0, parts)
            fill_edge(pad_ref, lower_ref, adj_ref, capacity, LOWER, 3, parts)


def is_live(counts_ref, tile):
    return jnp.where(tile < counts_ref[...], 1.0, 0.0).astype(f32)


def is_odd(place_ref):
    return lax.rem(place_ref[0, 0], 2).astype(f32)


UPPER, LOWER = (4, 0, 5), (6, 1, 7)


def convolve(pads, tap_row, finish, capacity, parts, between=()):
    for lane in range(parts):

        def one_tile(tile):
            sums = [None] * 8
            for col in range(7):
                taps = [tap_row(row, col, lane) for row in range(7)]
                for ref, rows, base in pads:
                    for held in range(rows):
                        window = ref[lane, tile, held, pl.ds(5 + col, 8), :]
                        for out in range(8):
                            tap = held + base - out
                            if 0 <= tap < 7:
                                term = window * taps[tap]
                                sums[out] = term if sums[out] is None else sums[out] + term
            finish(tile, lane, sums)
            return 0

        for tile in range(capacity):
            one_tile(tile)
            if lane * capacity + tile < len(between):
                between[lane * capacity + tile]()


def lanes(lane):
    return slice(lane * LANES, (lane + 1) * LANES)


def swap_edges(last, first, odd, core_ref, cross_ref):
    core_ref[...] = (first * odd + last * (1.0 - odd)).astype(bf16)
    cross_ref[...] = (last * odd + first * (1.0 - odd)).astype(bf16)


def edge_kernel(place_ref, tiles_ref, core_ref, cross_ref):
    swap_edges(
        tiles_ref[:, 5:8].astype(f32), tiles_ref[:, 0:3].astype(f32), is_odd(place_ref), core_ref, cross_ref
    )


def early_kernel(
    adj_ref, counts_ref, pool_ref, cot_ref, scale_ref, kern_ref, tiles_ref, up_ref, w_out_ref,
    pad_ref, conv_ref, mixed_ref, act_grad_ref, own_sum_ref,
):
    capacity, parts = tiles_ref.shape[0], tiles_ref.shape[3] // LANES
    pixels = 64
    channels = tiles_ref.shape[3]
    fill_middle(pad_ref, lambda t, r: tiles_ref[t, r].astype(f32), adj_ref, capacity, 0, parts)
    own_sum = jnp.zeros((1, channels), f32)
    scale = scale_ref[...].reshape(1, channels)
    for tile in range(capacity):
        live = is_live(counts_ref, tile)
        pool = pool_ref[0, tile]
        rows = slice(tile * pixels, (tile + 1) * pixels)
        out_grad = live * (up_ref[rows, :].astype(f32) + pool * cot_ref[...] * 0.125)
        mixed_ref[rows, 0:channels] = (out_grad * scale).astype(bf16)
        column = lax.broadcasted_iota(jnp.int32, (pixels, LANES), 1)
        mixed_ref[rows, channels:] = jnp.where(column == tile, 1.0, 0.0).astype(bf16)
        own = tiles_ref[tile].astype(f32)
        own_sum += live * pool * jnp.sum(own.reshape(pixels, channels), axis=0, keepdims=True)
    own_sum_ref[...] = own_sum

    def product(at):
        act_grad_ref[:, at] = lax.dot_general(
            mixed_ref[:, 0:channels], w_out_ref[at, :], (((1,), (1,)), ((), ())), preferred_element_type=f32
        )

    hidden = w_out_ref.shape[0]
    step = 256 if hidden % 256 == 0 else hidden
    products = [functools.partial(product, slice(n, n + step)) for n in range(0, hidden, step)]

    def finish(tile, lane, sums):
        for row in range(8):
            conv_ref[pl.ds(tile * pixels + row * 8, 8), lanes(lane)] = sums[row]

    convolve(
        [(pad_ref, 8, 3)],
        lambda row, col, lane: kern_ref[row, col : col + 1, lanes(lane)],
        finish, capacity, parts, products,
    )


def split_pieces(value_ref, rows, place_ref, stage, keep_ref, send_ref):
    side = lax.rem(lax.div(place_ref[0, 0], 1 << stage), 2)
    for pair in range(value_ref.shape[0] // (2 * rows)):
        here = pl.ds(pair * rows, rows)
        mine = pl.ds(pl.multiple_of((2 * pair + side) * rows, 8), rows)
        other = pl.ds(pl.multiple_of((2 * pair + 1 - side) * rows, 8), rows)
        keep_ref[here, :] = value_ref[mine, :]
        send_ref[here, :] = value_ref[other, :].astype(bf16)


def forward_kernel(
    rows, adj_ref, place_ref, core_ref, cross_ref, conv_ref, kern_ref, gain_ref, w_in_ref, mixed_ref,
    edge_ref, normed_ref, inv_ref, pre_ref, cdf_ref, keep_ref, send_ref, pooled_ref, whole_ref,
):
    capacity, parts = adj_ref.shape[0], conv_ref.shape[1] // LANES
    channels = conv_ref.shape[1]
    pixels = 64
    fill_edges(edge_ref, core_ref, cross_ref, place_ref, adj_ref, capacity, parts)

    def finish(tile, lane, sums):
        for row in range(8):
            at = pl.ds(tile * pixels + row * 8, 8)
            total = conv_ref[at, lanes(lane)]
            if sums[row] is not None:
                total = total + sums[row]
            whole_ref[at, lanes(lane)] = total

    convolve(
        [(edge_ref.at[:, :, 0:3], 3, 0), (edge_ref.at[:, :, 3:6], 3, 11)],
        lambda row, col, lane: kern_ref[row, col : col + 1, lanes(lane)],
        finish, capacity, parts,
    )
    conv = whole_ref[...]
    centred = conv - jnp.mean(conv, axis=-1, keepdims=True)
    inv_std = lax.rsqrt(jnp.mean(centred * centred, axis=-1, keepdims=True) + 1e-06)
    normed = centred * inv_std
    normed_ref[...] = normed
    inv_ref[...] = inv_std
    lifted = (normed * gain_ref[...].reshape(1, channels)).astype(bf16)
    hidden = w_in_ref.shape[1]
    side = lax.rem(place_ref[0, 0], 2)
    chunk = CHUNK if hidden % CHUNK == 0 and CHUNK % (2 * rows) == 0 else hidden

    def project(first):
        return jnp.dot(lifted, w_in_ref[:, first : first + chunk], preferred_element_type=f32)

    following = project(0)
    for first in range(0, hidden, chunk):
        at = slice(first, first + chunk)
        pre = following
        if first + chunk < hidden:
            following = project(first + chunk)
        cdf = 0.5 * (1.0 + lax.erf(pre * sqrt_half))
        pre_ref[:, at] = pre
        cdf_ref[:, at] = cdf
        activated = (pre * cdf).astype(bf16)
        both = lax.dot_general(
            activated, mixed_ref[...], (((0,), (0,)), ((), ())), preferred_element_type=f32
        )
        pooled_ref[at, :] = both[:, channels:]
        for block in range(0, chunk, 2 * rows):
            even = both[block : block + rows, 0:channels]
            odd_rows = both[block + rows : block + 2 * rows, 0:channels]
            out = pl.ds((first + block) // 2, rows)
            keep_ref[out, :] = jnp.where(side == 0, even, odd_rows)
            send_ref[out, :] = jnp.where(side == 0, odd_rows, even).astype(bf16)


def back_kernel(
    place_ref, counts_ref, pool_ref, pre_ref, cdf_ref, act_grad_ref, w_in_ref, normed_ref, inv_ref, gain_ref, pooled_ref, w_out_ref,
    scale_ref, own_sum_ref, grad_ref, core_ref, cross_ref, emb_ref,
):
    channels = normed_ref.shape[1]
    capacity = core_ref.shape[0]
    hidden = w_in_ref.shape[1]
    chunk = BACK_CHUNK if hidden % BACK_CHUNK == 0 else hidden
    lift = None
    for first in range(0, hidden, chunk):
        at = slice(first, first + chunk)
        pre = pre_ref[:, at]
        density = jnp.exp2(pre * pre * half_log2_e) * inv_root_two_pi
        pre_grad = (act_grad_ref[:, at] * (cdf_ref[:, at] + pre * density)).astype(bf16)
        term = lax.dot_general(
            pre_grad, w_in_ref[:, at], (((1,), (1,)), ((), ())), preferred_element_type=f32
        )
        lift = term if lift is None else lift + term
    grad_normed = lift * gain_ref[...].reshape(1, channels)
    normed = normed_ref[...]
    grad = inv_ref[...] * (
        grad_normed
        - jnp.mean(grad_normed, axis=-1, keepdims=True)
        - normed * jnp.mean(grad_normed * normed, axis=-1, keepdims=True)
    )
    grad_ref[...] = grad
    shaped = grad.reshape(capacity, 8, 8, channels)
    swap_edges(shaped[:, 5:8], shaped[:, 0:3], is_odd(place_ref), core_ref, cross_ref)
    column = lax.broadcasted_iota(jnp.int32, (1, LANES), 1)
    weights = jnp.zeros((1, LANES), f32)
    for tile in range(capacity):
        amount = is_live(counts_ref, tile) * pool_ref[0, tile]
        weights = jnp.where(column == tile, amount, weights)
    hidden = jnp.sum(pooled_ref[...] * weights, axis=1, keepdims=True)
    mixed = jnp.sum(hidden * w_out_ref[...].astype(f32), axis=0, keepdims=True)
    emb_ref[...] = (own_sum_ref[...] + scale_ref[...].reshape(1, channels) * mixed) * 0.125


def taps_kernel(pad_ref, edge_ref, grad_ref, emb_ref, state_ref, pack_ref, part_ref):
    parts, capacity = pad_ref.shape[0], pad_ref.shape[1]
    for lane in range(parts):

        def one_column(col):
            def one_tile(tile, sums):
                sums = list(sums)
                grads = [grad_ref[pl.ds(tile * 64 + row * 8, 8), lanes(lane)] for row in range(8)]
                for held in range(14):
                    if 3 <= held < 11:
                        window = pad_ref[lane, tile, held - 3, pl.ds(5 + col, 8), :]
                    else:
                        row = held if held < 3 else held - 8
                        window = edge_ref[lane, tile, row, pl.ds(5 + col, 8), :]
                    for out in range(8):
                        tap = held - out
                        if 0 <= tap < 7:
                            sums[tap] = sums[tap] + window * grads[out]
                return tuple(sums)

            sums = tuple(jnp.zeros((8, LANES), f32) for _ in range(7))
            for tile in range(capacity):
                sums = one_tile(tile, sums)
            for row in range(7):
                part_ref[row * 7 + col, :, lanes(lane)] = sums[row]
            return 0

        for col in range(7):
            one_column(col)
    state_ref[0:TAPS, :] = jnp.sum(part_ref[...], axis=1)
    state_ref[TAPS : TAPS + 1, :] = emb_ref[...]
    state_ref[TAPS + 1 :, :] = jnp.zeros((STATE - TAPS - 1, emb_ref.shape[1]), f32)
    pack_ref[...] = packed(state_ref)


def packed(state_ref):
    state = state_ref[...]
    high = state.astype(bf16)
    low = pltpu.roll(state - high.astype(f32), 1, 0)
    row = lax.broadcasted_iota(jnp.int32, state.shape, 0)
    return jnp.where(row == TAPS + 1, low, high.astype(f32)).astype(bf16)


def merged(state_ref, got, with_embedding=True):
    total = packed(state_ref).astype(f32) + got.astype(f32)
    row = lax.broadcasted_iota(jnp.int32, total.shape, 0)
    if with_embedding:
        embedding = total + pltpu.roll(total, STATE - 1, 0)
    else:
        embedding = state_ref[...]
    return jnp.where(row < TAPS, total, jnp.where(row == TAPS, embedding, 0.0))


def state_kernel(with_embedding, state_ref, got_ref, new_ref, pack_ref):
    new_ref[...] = merged(state_ref, got_ref[...], with_embedding)
    pack_ref[...] = packed(new_ref)


def merge_kernel(splits, terms, place_ref, *refs):
    sums, refs = refs[: 2 * terms], refs[2 * terms :]
    outs = max(1, len(splits))
    keeps, sends, sum_ref = refs[0 : 2 * outs : 2], refs[1 : 2 * outs : 2], refs[2 * outs]
    first = 0
    for keep_ref, got_ref in zip(sums[0::2], sums[1::2]):
        count = keep_ref.shape[0]
        sum_ref[first : first + count, :] = keep_ref[...] + got_ref[...].astype(f32)
        first += count
    for keep_ref, send_ref, (start, count, rows, bit) in zip(keeps, sends, splits):
        split_pieces(sum_ref.at[start : start + count], rows, place_ref, bit, keep_ref, send_ref)
    if not splits:
        keeps[0][...] = sum_ref[...]
        sends[0][...] = sum_ref[...].astype(bf16)


def pair_kernel(keep_ref, got_ref, new_ref, send_ref):
    total = keep_ref[...].astype(bf16).astype(f32) + got_ref[...].astype(f32)
    new_ref[...] = total
    send_ref[...] = total.astype(bf16)


def finish_kernel(keep_ref, got_ref, state_ref, new_ref, share_ref, taps_ref, emb_ref):
    share_ref[...] = keep_ref[...].astype(bf16).astype(f32) + got_ref[...].astype(f32)
    total = merged(state_ref, new_ref[...])
    for row in range(7):
        taps_ref[row] = total[row * 7 : row * 7 + 7, :]
    emb_ref[...] = total[TAPS : TAPS + 1, :]


def middle_kernel(adj_ref, grad_ref, kern_ref, out_ref, pad_ref):
    capacity, parts = adj_ref.shape[0], grad_ref.shape[1] // LANES

    def own_at(tile, row):
        at = tile * 64 + row * 8
        return grad_ref[pl.ds(at if isinstance(at, int) else pl.multiple_of(at, 8), 8), :]

    fill_middle(pad_ref, own_at, adj_ref, capacity, 0, parts)

    def finish(tile, lane, sums):
        for row in range(8):
            out_ref[pl.ds(tile * 64 + row * 8, 8), lanes(lane)] = sums[row]

    convolve(
        [(pad_ref, 8, 3)],
        lambda row, col, lane: kern_ref[6 - row, 6 - col : 7 - col, lanes(lane)],
        finish, capacity, parts,
    )


def outer_kernel(
    adj_ref, place_ref, counts_ref, pool_ref, part_ref, core_ref, cross_ref, kern_ref, up_ref, cot_ref,
    out_ref, pad_ref,
):
    capacity, parts = adj_ref.shape[0], part_ref.shape[1] // LANES
    fill_edges(pad_ref, core_ref, cross_ref, place_ref, adj_ref, capacity, parts)

    def finish(tile, lane, sums):
        live = is_live(counts_ref, tile)
        extra = pool_ref[0, tile] * cot_ref[:, lanes(lane)] * 0.125
        for row in range(8):
            at = pl.ds(tile * 64 + row * 8, 8)
            total = live * (up_ref[at, lanes(lane)].astype(f32) + extra) + part_ref[at, lanes(lane)]
            if sums[row] is not None:
                total = total + sums[row]
            out_ref[at, lanes(lane)] = (live * total).astype(bf16)

    convolve(
        [(pad_ref.at[:, :, 0:3], 3, 0), (pad_ref.at[:, :, 3:6], 3, 11)],
        lambda row, col, lane: kern_ref[6 - row, 6 - col : 7 - col, lanes(lane)],
        finish, capacity, parts,
    )


def whole_pass(
    tiles_in, upstream, pool_weight, slide_cot, adjacency, counts, kernel, norm_gain, w_in, w_out,
    layer_scale,
):
    own = tiles_in[0]
    capacity, _, _, channels = own.shape
    parts = channels // LANES
    hidden = w_in.shape[1]
    pixels = capacity * 64
    up = upstream.reshape(pixels, channels)
    wanted = adjacency[0]
    edge_shape = (capacity, 3, 8, channels)
    count = lax.axis_size("space")
    stages = count.bit_length() - 1
    rows = hidden // count
    place = lax.axis_index("space").astype(jnp.int32).reshape(1, 1)

    core, cross = call(
        edge_kernel, [struct(edge_shape, bf16)] * 2, [SMEM, VMEM], [place, own],
        flops=EDGE_COST,
    )
    cross = crossed(cross)
    core = swapped(core, "space", 1)

    pad, conv, mixed, act_grad, own_sum = call(
        early_kernel,
        [
            struct((parts, capacity, 8, 24, LANES)),
            struct((pixels, channels)),
            struct((pixels, channels + LANES), bf16),
            struct((pixels, hidden)),
            struct((1, channels)),
        ],
        [SMEM, VMEM, SMEM] + [VMEM] * 6,
        [wanted, counts, pool_weight, slide_cot, layer_scale, kernel, own, up, w_out],
        flops=2 * pixels * channels * hidden,
    )
    edge, normed, inv, pre, cdf, keep, send, pooled = call(
        functools.partial(forward_kernel, rows),
        [
            struct((parts, capacity, 6, 24, LANES)),
            struct((pixels, channels)),
            struct((pixels, 1)),
            struct((pixels, hidden)),
            struct((pixels, hidden)),
            struct((hidden // 2, channels)),
            struct((hidden // 2, channels), bf16),
            struct((hidden, LANES)),
        ],
        [SMEM] * 2 + [VMEM] * 7,
        [wanted, place, core, cross, conv, kernel, norm_gain, w_in, mixed],
        flops=4 * pixels * channels * hidden,
        scratch=[pltpu.VMEM((pixels, channels), f32)],
    )
    got = swapped(send, "space", 1)

    grad, core, cross, emb = call(
        back_kernel,
        [
            struct((pixels, channels)),
            struct(edge_shape, bf16),
            struct(edge_shape, bf16),
            struct((1, channels)),
        ],
        [SMEM, VMEM, SMEM] + [VMEM] * 11,
        [place, counts, pool_weight, pre, cdf, act_grad, w_in, normed, inv, norm_gain, pooled, w_out, layer_scale, own_sum],
        flops=2 * pixels * channels * hidden,
    )
    cross = crossed(cross)
    core = swapped(core, "space", 1)

    def merge(parts_, splits):
        held = sum(keep.shape[0] for keep, _ in parts_)
        shapes = []
        for size in [count // 2 for _, count, _, _ in splits] or [held]:
            shapes += [struct((size, channels)), struct((size, channels), bf16)]
        operands = [array for pair in parts_ for array in pair]
        out = call(
            functools.partial(merge_kernel, splits, len(parts_)), shapes,
            [SMEM] + [VMEM] * len(operands), [place] + operands,
            scratch=[pltpu.VMEM((held, channels), f32)],
        )
        return list(zip(out[0::2], out[1::2]))

    half = hidden // 4
    (keep_a, send_a), (keep_b, send_b) = merge([(keep, got)], [(0, half, rows, 1), (half, half, 2 * rows, 2)])
    got_a = swapped(send_a, "space", 2)
    got_b = swapped(send_b, "space", 4)
    half //= 2
    (keep_a, send_a), (keep_b, send_b) = merge(
        [(keep_a, got_a), (keep_b, got_b)], [(0, half, rows, 2), (half, half, rows, 1)]
    )
    got_a = swapped(send_a, "space", 4)
    got_b = swapped(send_b, "space", 2)
    held = [(keep_a, got_a), (keep_b, got_b)]
    for stage in range(3, stages):
        size = hidden >> stage
        ((keep, send),) = merge(held, [(0, size, rows, stage)])
        got = swapped(send, "space", 1 << stage)
        held = [(keep, got)]
    ((share, send),) = merge(held, [])
    groups = lax.axis_size("dp")
    bit = 1
    while bit < groups:
        got = swapped(send, "dp", bit)
        bit *= 2
        if bit < groups:
            share, send = call(pair_kernel, [struct(share.shape), struct(send.shape, bf16)], [VMEM] * 2, [share, got])

    state, pack = call(
        taps_kernel, [struct((STATE, channels)), struct((STATE, channels), bf16)],
        [VMEM] * 4, [pad, edge, grad, emb],
        scratch=[pltpu.VMEM((TAPS, 8, channels), f32)],
    )
    steps = [("space", 1)] + [("dp", 1 << n) for n in range(groups.bit_length() - 1)]
    steps += [("space", 1 << n) for n in range(1, stages)]
    for axis, bit in steps:
        new = swapped(pack, axis, bit)
        if (axis, bit) != steps[-1]:
            state, pack = call(
                functools.partial(state_kernel, axis == "space"),
                [struct((STATE, channels)), struct((STATE, channels), bf16)],
                [VMEM] * 2, [state, new],
            )

    share, tap_grad, embedding = call(
        finish_kernel, [struct((rows, channels)), struct(kernel.shape), struct((1, channels))],
        [VMEM] * 4, [share, got, state, new],
    )

    part = call(
        middle_kernel, struct((pixels, channels)), [SMEM] + [VMEM] * 2, [wanted, grad, kernel],
        scratch=[pltpu.VMEM((parts, capacity, 8, 24, LANES), f32)],
    )
    grad_tiles = call(
        outer_kernel, struct((pixels, channels), bf16),
        [SMEM] * 2 + [VMEM, SMEM] + [VMEM] * 6,
        [wanted, place, counts, pool_weight, part, core, cross, kernel, up, slide_cot],
        scratch=[pltpu.VMEM((parts, capacity, 6, 24, LANES), f32)],
    )
    return (
        embedding,
        grad_tiles.reshape(tiles_in.shape),
        share,
        tap_grad,
    )


def solution(mesh):
    return jax.shard_map(
        whole_pass,
        mesh=mesh,
        in_specs=(
            P("dp", "space", None, None, None),
            P("dp", "space", None, None, None),
            P("dp", "space"),
            P("dp", None),
            P("dp", "space", None),
            P("dp", "space"),
            P(),
            P(),
            P(),
            P(),
            P(),
        ),
        out_specs=(P("dp", None), P("dp", "space", None, None, None), P("space", None), P()),
        check_vma=False,
    )
```

```python
import functools

import jax
import jax.numpy as jnp
from jax import lax
from jax.experimental import pallas as pl
from jax.experimental.pallas import tpu as pltpu
from jax.sharding import PartitionSpec as P

sqrt_half = 0.7071067811865476
inv_root_two_pi = 0.3989422804014327
half_log2_e = -0.7213475204444817
f32 = jnp.float32
bf16 = jnp.bfloat16
LANES = 128

VMEM = pl.BlockSpec(memory_space=pltpu.VMEM)
SMEM = pl.BlockSpec(memory_space=pltpu.SMEM)
HBM = pl.BlockSpec(memory_space=pltpu.HBM)
STATE = 64
HALF = STATE // 2
TAPS = 49
CHUNK = 384
BACK_CHUNK = 512
EDGE_COST = 5_000_000_000


def call(body, out_shape, in_specs, args, flops=0, scratch=(), limit=16 << 20, out_specs=None):
    outs = out_shape if isinstance(out_shape, (list, tuple)) else [out_shape]
    total = sum(a.size * a.dtype.itemsize for a in list(args) + list(outs))
    return pl.pallas_call(
        body,
        out_shape=out_shape,
        in_specs=in_specs,
        out_specs=out_specs or jax.tree.map(lambda _: VMEM, out_shape),
        scratch_shapes=scratch,
        compiler_params=pltpu.CompilerParams(vmem_limit_bytes=limit),
        cost_estimate=pl.CostEstimate(flops=flops, bytes_accessed=total, transcendentals=0),
    )(*args)


def struct(shape, dtype=f32):
    return jax.ShapeDtypeStruct(shape, dtype)


def swapped(value, axis, bit):
    count = lax.axis_size(axis)
    return lax.ppermute(value, axis, [(source, source ^ bit) for source in range(count)])


def crossed(value):
    groups, count = lax.axis_size("dp"), lax.axis_size("space")
    targets = []
    for group in range(groups):
        for n in range(count):
            step = 1 if n % 2 else -1
            if 0 <= n + step < count:
                targets.append((group * count + n, group * count + n + step))
            elif (group ^ 1) < groups:
                targets.append((group * count + n, (group ^ 1) * count + n))
    return lax.ppermute(value, ("dp", "space"), targets)


def valid(entry):
    return jnp.where(entry >= 0, 1.0, 0.0).astype(f32)


def local(entry, capacity):
    return lax.rem(jnp.maximum(entry, 0), capacity)


def place(pad_ref, tile, row, part, value, parts):
    for lane in range(parts):
        pad_ref[lane, tile, row, pl.ds(part * 8, 8), :] = value[:, lane * LANES : (lane + 1) * LANES]


def fill_middle(pad_ref, own_at, adj_ref, capacity, first_row, parts):
    for tile in range(capacity):
        west, east = adj_ref[tile, 2], adj_ref[tile, 3]
        for row in range(8):
            place(pad_ref, tile, first_row + row, 0, own_at(local(west, capacity), row) * valid(west), parts)
            place(pad_ref, tile, first_row + row, 1, own_at(tile, row), parts)
            place(pad_ref, tile, first_row + row, 2, own_at(local(east, capacity), row) * valid(east), parts)


def fill_edge(pad_ref, edge_ref, adj_ref, capacity, entries, first_row, parts):
    for tile in range(capacity):
        for part, entry in enumerate(entries):
            wanted = adj_ref[tile, entry]
            index, keep = local(wanted, capacity), valid(wanted)
            for row in range(3):
                value = edge_ref[index, row].astype(f32) * keep
                place(pad_ref, tile, first_row + row, part, value, parts)


def fill_edges(pad_ref, core_ref, cross_ref, place_ref, adj_ref, capacity, parts):
    odd = lax.rem(place_ref[0, 0], 2)
    for parity, upper_ref, lower_ref in ((1, core_ref, cross_ref), (0, cross_ref, core_ref)):

        @pl.when(odd == parity)
        def _():
            fill_edge(pad_ref, upper_ref, adj_ref, capacity, UPPER, 0, parts)
            fill_edge(pad_ref, lower_ref, adj_ref, capacity, LOWER, 3, parts)


def is_live(counts_ref, tile):
    return jnp.where(tile < counts_ref[...], 1.0, 0.0).astype(f32)


def is_odd(place_ref):
    return lax.rem(place_ref[0, 0], 2).astype(f32)


UPPER, LOWER = (4, 0, 5), (6, 1, 7)


def convolve(pads, tap_row, finish, capacity, parts, between=()):
    for lane in range(parts):

        def one_tile(tile):
            sums = [None] * 8
            for col in range(7):
                taps = [tap_row(row, col, lane) for row in range(7)]
                for ref, rows, base in pads:
                    for held in range(rows):
                        window = ref[lane, tile, held, pl.ds(5 + col, 8), :]
                        for out in range(8):
                            tap = held + base - out
                            if 0 <= tap < 7:
                                term = window * taps[tap]
                                sums[out] = term if sums[out] is None else sums[out] + term
            finish(tile, lane, sums)
            return 0

        for tile in range(capacity):
            one_tile(tile)
            if lane * capacity + tile < len(between):
                between[lane * capacity + tile]()


def lanes(lane):
    return slice(lane * LANES, (lane + 1) * LANES)


def swap_edges(last, first, odd, core_ref, cross_ref):
    core_ref[...] = (first * odd + last * (1.0 - odd)).astype(bf16)
    cross_ref[...] = (last * odd + first * (1.0 - odd)).astype(bf16)


def edge_kernel(place_ref, tiles_ref, core_ref, cross_ref):
    swap_edges(
        tiles_ref[:, 5:8].astype(f32), tiles_ref[:, 0:3].astype(f32), is_odd(place_ref), core_ref, cross_ref
    )


def early_kernel(
    adj_ref, counts_ref, pool_ref, cot_ref, scale_ref, kern_ref, tiles_ref, up_ref, w_out_ref,
    pad_ref, conv_ref, mixed_ref, act_grad_ref, own_sum_ref,
):
    capacity, parts = tiles_ref.shape[0], tiles_ref.shape[3] // LANES
    pixels = 64
    channels = tiles_ref.shape[3]
    fill_middle(pad_ref, lambda t, r: tiles_ref[t, r].astype(f32), adj_ref, capacity, 0, parts)
    own_sum = jnp.zeros((1, channels), f32)
    scale = scale_ref[...].reshape(1, channels)
    for tile in range(capacity):
        live = is_live(counts_ref, tile)
        pool = pool_ref[0, tile]
        rows = slice(tile * pixels, (tile + 1) * pixels)
        out_grad = live * (up_ref[rows, :].astype(f32) + pool * cot_ref[...] * 0.125)
        mixed_ref[rows, 0:channels] = (out_grad * scale).astype(bf16)
        column = lax.broadcasted_iota(jnp.int32, (pixels, LANES), 1)
        mixed_ref[rows, channels:] = jnp.where(column == tile, 1.0, 0.0).astype(bf16)
        own = tiles_ref[tile].astype(f32)
        own_sum += live * pool * jnp.sum(own.reshape(pixels, channels), axis=0, keepdims=True)
    own_sum_ref[...] = own_sum

    def product(at):
        act_grad_ref[:, at] = lax.dot_general(
            mixed_ref[:, 0:channels], w_out_ref[at, :], (((1,), (1,)), ((), ())), preferred_element_type=f32
        )

    hidden = w_out_ref.shape[0]
    step = 256 if hidden % 256 == 0 else hidden
    products = [functools.partial(product, slice(n, n + step)) for n in range(0, hidden, step)]

    def finish(tile, lane, sums):
        for row in range(8):
            conv_ref[pl.ds(tile * pixels + row * 8, 8), lanes(lane)] = sums[row]

    convolve(
        [(pad_ref, 8, 3)],
        lambda row, col, lane: kern_ref[row, col : col + 1, lanes(lane)],
        finish, capacity, parts, products,
    )


def split_pieces(value_ref, rows, place_ref, stage, keep_ref, send_ref):
    side = lax.rem(lax.div(place_ref[0, 0], 1 << stage), 2)
    for pair in range(value_ref.shape[0] // (2 * rows)):
        here = pl.ds(pair * rows, rows)
        mine = pl.ds(pl.multiple_of((2 * pair + side) * rows, 8), rows)
        other = pl.ds(pl.multiple_of((2 * pair + 1 - side) * rows, 8), rows)
        keep_ref[here, :] = value_ref[mine, :]
        send_ref[here, :] = value_ref[other, :].astype(bf16)


def forward_kernel(
    rows, adj_ref, place_ref, core_ref, cross_ref, conv_ref, kern_ref, gain_ref, w_in_ref, mixed_ref,
    edge_ref, normed_ref, inv_ref, pre_ref, cdf_ref, keep_ref, send_ref, pooled_ref, whole_ref,
):
    capacity, parts = adj_ref.shape[0], conv_ref.shape[1] // LANES
    channels = conv_ref.shape[1]
    pixels = 64
    fill_edges(edge_ref, core_ref, cross_ref, place_ref, adj_ref, capacity, parts)

    def finish(tile, lane, sums):
        for row in range(8):
            at = pl.ds(tile * pixels + row * 8, 8)
            total = conv_ref[at, lanes(lane)]
            if sums[row] is not None:
                total = total + sums[row]
            whole_ref[at, lanes(lane)] = total

    convolve(
        [(edge_ref.at[:, :, 0:3], 3, 0), (edge_ref.at[:, :, 3:6], 3, 11)],
        lambda row, col, lane: kern_ref[row, col : col + 1, lanes(lane)],
        finish, capacity, parts,
    )
    conv = whole_ref[...]
    centred = conv - jnp.mean(conv, axis=-1, keepdims=True)
    inv_std = lax.rsqrt(jnp.mean(centred * centred, axis=-1, keepdims=True) + 1e-06)
    normed = centred * inv_std
    normed_ref[...] = normed
    inv_ref[...] = inv_std
    lifted = (normed * gain_ref[...].reshape(1, channels)).astype(bf16)
    hidden = w_in_ref.shape[1]
    side = lax.rem(place_ref[0, 0], 2)
    chunk = CHUNK if hidden % CHUNK == 0 and CHUNK % (2 * rows) == 0 else hidden

    def project(first):
        return jnp.dot(lifted, w_in_ref[:, first : first + chunk], preferred_element_type=f32)

    following = project(0)
    for first in range(0, hidden, chunk):
        at = slice(first, first + chunk)
        pre = following
        if first + chunk < hidden:
            following = project(first + chunk)
        cdf = 0.5 * (1.0 + lax.erf(pre * sqrt_half))
        pre_ref[:, at] = pre
        cdf_ref[:, at] = cdf
        activated = (pre * cdf).astype(bf16)
        both = lax.dot_general(
            activated, mixed_ref[...], (((0,), (0,)), ((), ())), preferred_element_type=f32
        )
        pooled_ref[at, :] = both[:, channels:]
        for block in range(0, chunk, 2 * rows):
            even = both[block : block + rows, 0:channels]
            odd_rows = both[block + rows : block + 2 * rows, 0:channels]
            out = pl.ds((first + block) // 2, rows)
            keep_ref[out, :] = jnp.where(side == 0, even, odd_rows)
            send_ref[out, :] = jnp.where(side == 0, odd_rows, even).astype(bf16)


def back_kernel(
    place_ref, counts_ref, pool_ref, pre_ref, cdf_ref, act_grad_ref, w_in_ref, normed_ref, inv_ref, gain_ref, pooled_ref, w_out_ref,
    scale_ref, own_sum_ref, grad_ref, core_ref, cross_ref, emb_ref,
):
    channels = normed_ref.shape[1]
    capacity = core_ref.shape[0]
    hidden = w_in_ref.shape[1]
    chunk = BACK_CHUNK if hidden % BACK_CHUNK == 0 else hidden
    lift = None
    for first in range(0, hidden, chunk):
        at = slice(first, first + chunk)
        pre = pre_ref[:, at]
        density = jnp.exp2(pre * pre * half_log2_e) * inv_root_two_pi
        pre_grad = (act_grad_ref[:, at] * (cdf_ref[:, at] + pre * density)).astype(bf16)
        term = lax.dot_general(
            pre_grad, w_in_ref[:, at], (((1,), (1,)), ((), ())), preferred_element_type=f32
        )
        lift = term if lift is None else lift + term
    grad_normed = lift * gain_ref[...].reshape(1, channels)
    normed = normed_ref[...]
    grad = inv_ref[...] * (
        grad_normed
        - jnp.mean(grad_normed, axis=-1, keepdims=True)
        - normed * jnp.mean(grad_normed * normed, axis=-1, keepdims=True)
    )
    grad_ref[...] = grad
    shaped = grad.reshape(capacity, 8, 8, channels)
    swap_edges(shaped[:, 5:8], shaped[:, 0:3], is_odd(place_ref), core_ref, cross_ref)
    column = lax.broadcasted_iota(jnp.int32, (1, LANES), 1)
    weights = jnp.zeros((1, LANES), f32)
    for tile in range(capacity):
        amount = is_live(counts_ref, tile) * pool_ref[0, tile]
        weights = jnp.where(column == tile, amount, weights)
    hidden = jnp.sum(pooled_ref[...] * weights, axis=1, keepdims=True)
    mixed = jnp.sum(hidden * w_out_ref[...].astype(f32), axis=0, keepdims=True)
    emb_ref[...] = (own_sum_ref[...] + scale_ref[...].reshape(1, channels) * mixed) * 0.125


def taps_kernel(place_ref, pad_ref, edge_ref, grad_ref, emb_ref, keep_ref, send_ref, part_ref, state_ref, pack_ref):
    parts, capacity = pad_ref.shape[0], pad_ref.shape[1]
    for lane in range(parts):

        def one_column(col):
            def one_tile(tile, sums):
                sums = list(sums)
                grads = [grad_ref[pl.ds(tile * 64 + row * 8, 8), lanes(lane)] for row in range(8)]
                for held in range(14):
                    if 3 <= held < 11:
                        window = pad_ref[lane, tile, held - 3, pl.ds(5 + col, 8), :]
                    else:
                        row = held if held < 3 else held - 8
                        window = edge_ref[lane, tile, row, pl.ds(5 + col, 8), :]
                    for out in range(8):
                        tap = held - out
                        if 0 <= tap < 7:
                            sums[tap] = sums[tap] + window * grads[out]
                return tuple(sums)

            sums = tuple(jnp.zeros((8, LANES), f32) for _ in range(7))
            for tile in range(capacity):
                sums = one_tile(tile, sums)
            for row in range(7):
                part_ref[row * 7 + col, :, lanes(lane)] = sums[row]
            return 0

        for col in range(7):
            one_column(col)
    state_ref[0:TAPS, :] = jnp.sum(part_ref[...], axis=1)
    state_ref[TAPS : TAPS + 1, :] = emb_ref[...]
    state_ref[TAPS + 1 :, :] = jnp.zeros((STATE - TAPS - 1, emb_ref.shape[1]), f32)
    pack_ref[...] = packed(state_ref, 0).astype(f32)
    mine = lax.rem(place_ref[0, 0], 2) * HALF
    keep_ref[...] = state_ref[pl.ds(pl.multiple_of(mine, 8), HALF), :]
    send_ref[...] = pack_ref[pl.ds(pl.multiple_of(HALF - mine, 8), HALF), :].astype(bf16)


def packed(state_ref, first):
    state = state_ref[...]
    high = state.astype(bf16)
    low = pltpu.roll(state - high.astype(f32), 1, 0)
    row = lax.broadcasted_iota(jnp.int32, state.shape, 0) + first
    return jnp.where(row == TAPS + 1, low, high.astype(f32)).astype(bf16)


def state_kernel(with_embedding, symmetric, place_ref, state_ref, got_ref, new_ref, pack_ref):
    first = lax.rem(place_ref[0, 0], 2) * HALF
    own = packed(state_ref, first).astype(f32) if symmetric else state_ref[...]
    total = own + got_ref[...].astype(f32)
    row = lax.broadcasted_iota(jnp.int32, total.shape, 0) + first
    if with_embedding:
        embedding = total + pltpu.roll(total, HALF - 1, 0)
    else:
        embedding = state_ref[...]
    new_ref[...] = jnp.where(row < TAPS, total, jnp.where(row == TAPS, embedding, 0.0))
    pack_ref[...] = packed(new_ref, first)


def merge_kernel(splits, terms, place_ref, *refs):
    sums, refs = refs[: 2 * terms], refs[2 * terms :]
    outs = max(1, len(splits))
    keeps, sends, sum_ref = refs[0 : 2 * outs : 2], refs[1 : 2 * outs : 2], refs[2 * outs]
    first = 0
    for keep_ref, got_ref in zip(sums[0::2], sums[1::2]):
        count = keep_ref.shape[0]
        sum_ref[first : first + count, :] = keep_ref[...] + got_ref[...].astype(f32)
        first += count
    for keep_ref, send_ref, (start, count, rows, bit) in zip(keeps, sends, splits):
        split_pieces(sum_ref.at[start : start + count], rows, place_ref, bit, keep_ref, send_ref)
    if not splits:
        keeps[0][...] = sum_ref[...]
        sends[0][...] = sum_ref[...].astype(bf16)


def pair_kernel(keep_ref, got_ref, new_ref, send_ref):
    total = keep_ref[...].astype(bf16).astype(f32) + got_ref[...].astype(f32)
    new_ref[...] = total
    send_ref[...] = total.astype(bf16)


def finish_kernel(place_ref, keep_ref, got_ref, state_ref, other_ref, share_ref, taps_ref, emb_ref, total_ref):
    share_ref[...] = keep_ref[...].astype(bf16).astype(f32) + got_ref[...].astype(f32)
    mine = lax.rem(place_ref[0, 0], 2) * HALF
    total_ref[pl.ds(pl.multiple_of(mine, 8), HALF), :] = state_ref[...]
    total_ref[pl.ds(pl.multiple_of(HALF - mine, 8), HALF), :] = other_ref[...]
    for row in range(7):
        taps_ref[row] = total_ref[row * 7 : row * 7 + 7, :]
    emb_ref[...] = total_ref[TAPS : TAPS + 1, :]


def middle_kernel(adj_ref, grad_ref, kern_ref, out_ref, pad_ref):
    capacity, parts = adj_ref.shape[0], grad_ref.shape[1] // LANES

    def own_at(tile, row):
        at = tile * 64 + row * 8
        return grad_ref[pl.ds(at if isinstance(at, int) else pl.multiple_of(at, 8), 8), :]

    fill_middle(pad_ref, own_at, adj_ref, capacity, 0, parts)

    def finish(tile, lane, sums):
        for row in range(8):
            out_ref[pl.ds(tile * 64 + row * 8, 8), lanes(lane)] = sums[row]

    convolve(
        [(pad_ref, 8, 3)],
        lambda row, col, lane: kern_ref[6 - row, 6 - col : 7 - col, lanes(lane)],
        finish, capacity, parts,
    )


def outer_kernel(
    adj_ref, place_ref, counts_ref, pool_ref, part_ref, core_ref, cross_ref, kern_ref, up_ref, cot_ref,
    out_ref, pad_ref,
):
    capacity, parts = adj_ref.shape[0], part_ref.shape[1] // LANES
    fill_edges(pad_ref, core_ref, cross_ref, place_ref, adj_ref, capacity, parts)

    def finish(tile, lane, sums):
        live = is_live(counts_ref, tile)
        extra = pool_ref[0, tile] * cot_ref[:, lanes(lane)] * 0.125
        for row in range(8):
            at = pl.ds(tile * 64 + row * 8, 8)
            total = live * (up_ref[at, lanes(lane)].astype(f32) + extra) + part_ref[at, lanes(lane)]
            if sums[row] is not None:
                total = total + sums[row]
            out_ref[at, lanes(lane)] = (live * total).astype(bf16)

    convolve(
        [(pad_ref.at[:, :, 0:3], 3, 0), (pad_ref.at[:, :, 3:6], 3, 11)],
        lambda row, col, lane: kern_ref[6 - row, 6 - col : 7 - col, lanes(lane)],
        finish, capacity, parts,
    )


def whole_pass(
    tiles_in, upstream, pool_weight, slide_cot, adjacency, counts, kernel, norm_gain, w_in, w_out,
    layer_scale,
):
    own = tiles_in[0]
    capacity, _, _, channels = own.shape
    parts = channels // LANES
    hidden = w_in.shape[1]
    pixels = capacity * 64
    up = upstream.reshape(pixels, channels)
    wanted = adjacency[0]
    edge_shape = (capacity, 3, 8, channels)
    count = lax.axis_size("space")
    stages = count.bit_length() - 1
    rows = hidden // count
    place = lax.axis_index("space").astype(jnp.int32).reshape(1, 1)

    core, cross = call(
        edge_kernel, [struct(edge_shape, bf16)] * 2, [SMEM, VMEM], [place, own],
        flops=EDGE_COST,
    )
    cross = crossed(cross)
    core = swapped(core, "space", 1)

    pad, conv, mixed, act_grad, own_sum = call(
        early_kernel,
        [
            struct((parts, capacity, 8, 24, LANES)),
            struct((pixels, channels)),
            struct((pixels, channels + LANES), bf16),
            struct((pixels, hidden)),
            struct((1, channels)),
        ],
        [SMEM, VMEM, SMEM] + [VMEM] * 6,
        [wanted, counts, pool_weight, slide_cot, layer_scale, kernel, own, up, w_out],
        flops=2 * pixels * channels * hidden,
    )
    edge, normed, inv, pre, cdf, keep, send, pooled = call(
        functools.partial(forward_kernel, rows),
        [
            struct((parts, capacity, 6, 24, LANES)),
            struct((pixels, channels)),
            struct((pixels, 1)),
            struct((pixels, hidden)),
            struct((pixels, hidden)),
            struct((hidden // 2, channels)),
            struct((hidden // 2, channels), bf16),
            struct((hidden, LANES)),
        ],
        [SMEM] * 2 + [VMEM] * 7,
        [wanted, place, core, cross, conv, kernel, norm_gain, w_in, mixed],
        flops=4 * pixels * channels * hidden,
        scratch=[pltpu.VMEM((pixels, channels), f32)],
    )
    got = swapped(send, "space", 1)

    grad, core, cross, emb = call(
        back_kernel,
        [
            struct((pixels, channels)),
            struct(edge_shape, bf16),
            struct(edge_shape, bf16),
            struct((1, channels)),
        ],
        [SMEM, VMEM, SMEM] + [VMEM] * 11,
        [place, counts, pool_weight, pre, cdf, act_grad, w_in, normed, inv, norm_gain, pooled, w_out, layer_scale, own_sum],
        flops=2 * pixels * channels * hidden,
    )
    cross = crossed(cross)
    core = swapped(core, "space", 1)

    def merge(parts_, splits):
        held = sum(keep.shape[0] for keep, _ in parts_)
        shapes = []
        for size in [count // 2 for _, count, _, _ in splits] or [held]:
            shapes += [struct((size, channels)), struct((size, channels), bf16)]
        operands = [array for pair in parts_ for array in pair]
        out = call(
            functools.partial(merge_kernel, splits, len(parts_)), shapes,
            [SMEM] + [VMEM] * len(operands), [place] + operands,
            scratch=[pltpu.VMEM((held, channels), f32)],
        )
        return list(zip(out[0::2], out[1::2]))

    half = hidden // 4
    (keep_a, send_a), (keep_b, send_b) = merge([(keep, got)], [(0, half, rows, 1), (half, half, 2 * rows, 2)])
    got_a = swapped(send_a, "space", 2)
    got_b = swapped(send_b, "space", 4)
    half //= 2
    (keep_a, send_a), (keep_b, send_b) = merge(
        [(keep_a, got_a), (keep_b, got_b)], [(0, half, rows, 2), (half, half, rows, 1)]
    )
    got_a = swapped(send_a, "space", 4)
    got_b = swapped(send_b, "space", 2)
    held = [(keep_a, got_a), (keep_b, got_b)]
    for stage in range(3, stages):
        size = hidden >> stage
        ((keep, send),) = merge(held, [(0, size, rows, stage)])
        got = swapped(send, "space", 1 << stage)
        held = [(keep, got)]
    ((share, send),) = merge(held, [])
    groups = lax.axis_size("dp")
    bit = 1
    while bit < groups:
        got = swapped(send, "dp", bit)
        bit *= 2
        if bit < groups:
            share, send = call(pair_kernel, [struct(share.shape), struct(send.shape, bf16)], [VMEM] * 2, [share, got])

    half_shapes = [struct((HALF, channels)), struct((HALF, channels), bf16)]
    state, pack = call(
        taps_kernel, half_shapes, [SMEM] + [VMEM] * 4, [place, pad, edge, grad, emb],
        scratch=[pltpu.VMEM((TAPS, 8, channels), f32)] + [pltpu.VMEM((STATE, channels), f32)] * 2,
    )
    steps = [("space", 1)] + [("dp", 1 << n) for n in range(groups.bit_length() - 1)]
    steps += [("space", 1 << n) for n in range(1, stages)]
    for axis, bit in steps:
        new = swapped(pack, axis, bit)
        state, pack = call(
            functools.partial(state_kernel, axis == "space", (axis, bit) != steps[0]), half_shapes,
            [SMEM] + [VMEM] * 2, [place, state, new],
        )
    other = swapped(state, "space", 1)

    share, tap_grad, embedding = call(
        finish_kernel, [struct((rows, channels)), struct(kernel.shape), struct((1, channels))],
        [SMEM] + [VMEM] * 4, [place, share, got, state, other],
        scratch=[pltpu.VMEM((STATE, channels), f32)],
    )

    part = call(
        middle_kernel, struct((pixels, channels)), [SMEM] + [VMEM] * 2, [wanted, grad, kernel],
        scratch=[pltpu.VMEM((parts, capacity, 8, 24, LANES), f32)],
    )
    grad_tiles = call(
        outer_kernel, struct((pixels, channels), bf16),
        [SMEM] * 2 + [VMEM, SMEM] + [VMEM] * 6,
        [wanted, place, counts, pool_weight, part, core, cross, kernel, up, slide_cot],
        scratch=[pltpu.VMEM((parts, capacity, 6, 24, LANES), f32)],
    )
    return (
        embedding,
        grad_tiles.reshape(tiles_in.shape),
        share,
        tap_grad,
    )


def solution(mesh):
    return jax.shard_map(
        whole_pass,
        mesh=mesh,
        in_specs=(
            P("dp", "space", None, None, None),
            P("dp", "space", None, None, None),
            P("dp", "space"),
            P("dp", None),
            P("dp", "space", None),
            P("dp", "space"),
            P(),
            P(),
            P(),
            P(),
            P(),
        ),
        out_specs=(P("dp", None), P("dp", "space", None, None, None), P("space", None), P()),
        check_vma=False,
    )
```

```python
import functools

import jax
import jax.numpy as jnp
from jax import lax
from jax.experimental import pallas as pl
from jax.experimental.pallas import tpu as pltpu
from jax.sharding import PartitionSpec as P

sqrt_half = 0.7071067811865476
inv_root_two_pi = 0.3989422804014327
half_log2_e = -0.7213475204444817
f32 = jnp.float32
bf16 = jnp.bfloat16
LANES = 128

VMEM = pl.BlockSpec(memory_space=pltpu.VMEM)
SMEM = pl.BlockSpec(memory_space=pltpu.SMEM)
HBM = pl.BlockSpec(memory_space=pltpu.HBM)
STATE = 56
TAPS = 49
CHUNK = 384
BACK_CHUNK = 512
EDGE_COST = 5_000_000_000


def call(body, out_shape, in_specs, args, flops=0, scratch=(), limit=16 << 20, out_specs=None):
    outs = out_shape if isinstance(out_shape, (list, tuple)) else [out_shape]
    total = sum(a.size * a.dtype.itemsize for a in list(args) + list(outs))
    return pl.pallas_call(
        body,
        out_shape=out_shape,
        in_specs=in_specs,
        out_specs=out_specs or jax.tree.map(lambda _: VMEM, out_shape),
        scratch_shapes=scratch,
        compiler_params=pltpu.CompilerParams(vmem_limit_bytes=limit),
        cost_estimate=pl.CostEstimate(flops=flops, bytes_accessed=total, transcendentals=0),
    )(*args)


def struct(shape, dtype=f32):
    return jax.ShapeDtypeStruct(shape, dtype)


def swapped(value, axis, bit):
    count = lax.axis_size(axis)
    return lax.ppermute(value, axis, [(source, source ^ bit) for source in range(count)])


def crossed(value):
    groups, count = lax.axis_size("dp"), lax.axis_size("space")
    targets = []
    for group in range(groups):
        for n in range(count):
            step = 1 if n % 2 else -1
            if 0 <= n + step < count:
                targets.append((group * count + n, group * count + n + step))
            elif (group ^ 1) < groups:
                targets.append((group * count + n, (group ^ 1) * count + n))
    return lax.ppermute(value, ("dp", "space"), targets)


def valid(entry):
    return jnp.where(entry >= 0, 1.0, 0.0).astype(f32)


def local(entry, capacity):
    return lax.rem(jnp.maximum(entry, 0), capacity)


def place(pad_ref, tile, row, part, value, parts):
    for lane in range(parts):
        pad_ref[lane, tile, row, pl.ds(part * 8, 8), :] = value[:, lane * LANES : (lane + 1) * LANES]


def fill_middle(pad_ref, own_at, adj_ref, capacity, first_row, parts):
    for tile in range(capacity):
        west, east = adj_ref[tile, 2], adj_ref[tile, 3]
        for row in range(8):
            place(pad_ref, tile, first_row + row, 0, own_at(local(west, capacity), row) * valid(west), parts)
            place(pad_ref, tile, first_row + row, 1, own_at(tile, row), parts)
            place(pad_ref, tile, first_row + row, 2, own_at(local(east, capacity), row) * valid(east), parts)


def fill_edge(pad_ref, edge_ref, adj_ref, capacity, entries, first_row, parts):
    for tile in range(capacity):
        for part, entry in enumerate(entries):
            wanted = adj_ref[tile, entry]
            index, keep = local(wanted, capacity), valid(wanted)
            for row in range(3):
                value = edge_ref[index, row].astype(f32) * keep
                place(pad_ref, tile, first_row + row, part, value, parts)


def fill_edges(pad_ref, core_ref, cross_ref, place_ref, adj_ref, capacity, parts):
    odd = lax.rem(place_ref[0, 0], 2)
    for parity, upper_ref, lower_ref in ((1, core_ref, cross_ref), (0, cross_ref, core_ref)):

        @pl.when(odd == parity)
        def _():
            fill_edge(pad_ref, upper_ref, adj_ref, capacity, UPPER, 0, parts)
            fill_edge(pad_ref, lower_ref, adj_ref, capacity, LOWER, 3, parts)


def is_live(counts_ref, tile):
    return jnp.where(tile < counts_ref[...], 1.0, 0.0).astype(f32)


def is_odd(place_ref):
    return lax.rem(place_ref[0, 0], 2).astype(f32)


UPPER, LOWER = (4, 0, 5), (6, 1, 7)


def convolve(pads, tap_row, finish, capacity, parts, between=()):
    for lane in range(parts):

        def one_tile(tile):
            sums = [None] * 8
            for col in range(7):
                taps = [tap_row(row, col, lane) for row in range(7)]
                for ref, rows, base in pads:
                    for held in range(rows):
                        window = ref[lane, tile, held, pl.ds(5 + col, 8), :]
                        for out in range(8):
                            tap = held + base - out
                            if 0 <= tap < 7:
                                term = window * taps[tap]
                                sums[out] = term if sums[out] is None else sums[out] + term
            finish(tile, lane, sums)
            return 0

        for tile in range(capacity):
            one_tile(tile)
            if lane * capacity + tile < len(between):
                between[lane * capacity + tile]()


def lanes(lane):
    return slice(lane * LANES, (lane + 1) * LANES)


def swap_edges(last, first, odd, core_ref, cross_ref):
    core_ref[...] = (first * odd + last * (1.0 - odd)).astype(bf16)
    cross_ref[...] = (last * odd + first * (1.0 - odd)).astype(bf16)


def edge_kernel(place_ref, tiles_ref, core_ref, cross_ref):
    swap_edges(
        tiles_ref[:, 5:8].astype(f32), tiles_ref[:, 0:3].astype(f32), is_odd(place_ref), core_ref, cross_ref
    )


def early_kernel(
    adj_ref, counts_ref, pool_ref, cot_ref, scale_ref, kern_ref, tiles_ref, up_ref, w_out_ref,
    pad_ref, conv_ref, mixed_ref, act_grad_ref, own_sum_ref,
):
    capacity, parts = tiles_ref.shape[0], tiles_ref.shape[3] // LANES
    pixels = 64
    channels = tiles_ref.shape[3]
    fill_middle(pad_ref, lambda t, r: tiles_ref[t, r].astype(f32), adj_ref, capacity, 0, parts)
    own_sum = jnp.zeros((1, channels), f32)
    scale = scale_ref[...].reshape(1, channels)
    for tile in range(capacity):
        live = is_live(counts_ref, tile)
        pool = pool_ref[0, tile]
        rows = slice(tile * pixels, (tile + 1) * pixels)
        out_grad = live * (up_ref[rows, :].astype(f32) + pool * cot_ref[...] * 0.125)
        mixed_ref[rows, 0:channels] = (out_grad * scale).astype(bf16)
        column = lax.broadcasted_iota(jnp.int32, (pixels, LANES), 1)
        mixed_ref[rows, channels:] = jnp.where(column == tile, 1.0, 0.0).astype(bf16)
        own = tiles_ref[tile].astype(f32)
        own_sum += live * pool * jnp.sum(own.reshape(pixels, channels), axis=0, keepdims=True)
    own_sum_ref[...] = own_sum

    def product(at):
        act_grad_ref[:, at] = lax.dot_general(
            mixed_ref[:, 0:channels], w_out_ref[at, :], (((1,), (1,)), ((), ())), preferred_element_type=f32
        )

    hidden = w_out_ref.shape[0]
    step = 256 if hidden % 256 == 0 else hidden
    products = [functools.partial(product, slice(n, n + step)) for n in range(0, hidden, step)]

    def finish(tile, lane, sums):
        for row in range(8):
            conv_ref[pl.ds(tile * pixels + row * 8, 8), lanes(lane)] = sums[row]

    convolve(
        [(pad_ref, 8, 3)],
        lambda row, col, lane: kern_ref[row, col : col + 1, lanes(lane)],
        finish, capacity, parts, products,
    )


def split_pieces(value_ref, rows, place_ref, stage, keep_ref, send_ref):
    side = lax.rem(lax.div(place_ref[0, 0], 1 << stage), 2)
    for pair in range(value_ref.shape[0] // (2 * rows)):
        here = pl.ds(pair * rows, rows)
        mine = pl.ds(pl.multiple_of((2 * pair + side) * rows, 8), rows)
        other = pl.ds(pl.multiple_of((2 * pair + 1 - side) * rows, 8), rows)
        keep_ref[here, :] = value_ref[mine, :]
        send_ref[here, :] = value_ref[other, :].astype(bf16)


def forward_kernel(
    rows, adj_ref, place_ref, core_ref, cross_ref, conv_ref, kern_ref, gain_ref, w_in_ref, mixed_ref,
    edge_ref, normed_ref, inv_ref, pre_ref, cdf_ref, keep_ref, send_ref, pooled_ref, whole_ref,
):
    capacity, parts = adj_ref.shape[0], conv_ref.shape[1] // LANES
    channels = conv_ref.shape[1]
    pixels = 64
    fill_edges(edge_ref, core_ref, cross_ref, place_ref, adj_ref, capacity, parts)

    def finish(tile, lane, sums):
        for row in range(8):
            at = pl.ds(tile * pixels + row * 8, 8)
            total = conv_ref[at, lanes(lane)]
            if sums[row] is not None:
                total = total + sums[row]
            whole_ref[at, lanes(lane)] = total

    convolve(
        [(edge_ref.at[:, :, 0:3], 3, 0), (edge_ref.at[:, :, 3:6], 3, 11)],
        lambda row, col, lane: kern_ref[row, col : col + 1, lanes(lane)],
        finish, capacity, parts,
    )
    conv = whole_ref[...]
    centred = conv - jnp.mean(conv, axis=-1, keepdims=True)
    inv_std = lax.rsqrt(jnp.mean(centred * centred, axis=-1, keepdims=True) + 1e-06)
    normed = centred * inv_std
    normed_ref[...] = normed
    inv_ref[...] = inv_std
    lifted = (normed * gain_ref[...].reshape(1, channels)).astype(bf16)
    hidden = w_in_ref.shape[1]
    side = lax.rem(place_ref[0, 0], 2)
    chunk = CHUNK if hidden % CHUNK == 0 and CHUNK % (2 * rows) == 0 else hidden

    def project(first):
        return jnp.dot(lifted, w_in_ref[:, first : first + chunk], preferred_element_type=f32)

    following = project(0)
    for first in range(0, hidden, chunk):
        at = slice(first, first + chunk)
        pre = following
        if first + chunk < hidden:
            following = project(first + chunk)
        cdf = 0.5 * (1.0 + lax.erf(pre * sqrt_half))
        pre_ref[:, at] = pre
        cdf_ref[:, at] = cdf
        activated = (pre * cdf).astype(bf16)
        both = lax.dot_general(
            activated, mixed_ref[...], (((0,), (0,)), ((), ())), preferred_element_type=f32
        )
        pooled_ref[at, :] = both[:, channels:]
        for block in range(0, chunk, 2 * rows):
            even = both[block : block + rows, 0:channels]
            odd_rows = both[block + rows : block + 2 * rows, 0:channels]
            out = pl.ds((first + block) // 2, rows)
            keep_ref[out, :] = jnp.where(side == 0, even, odd_rows)
            send_ref[out, :] = jnp.where(side == 0, odd_rows, even).astype(bf16)


def back_kernel(
    place_ref, counts_ref, pool_ref, pre_ref, cdf_ref, act_grad_ref, w_in_ref, normed_ref, inv_ref, gain_ref, pooled_ref, w_out_ref,
    scale_ref, own_sum_ref, grad_ref, core_ref, cross_ref, emb_ref,
):
    channels = normed_ref.shape[1]
    capacity = core_ref.shape[0]
    hidden = w_in_ref.shape[1]
    chunk = BACK_CHUNK if hidden % BACK_CHUNK == 0 else hidden
    lift = None
    for first in range(0, hidden, chunk):
        at = slice(first, first + chunk)
        pre = pre_ref[:, at]
        density = jnp.exp2(pre * pre * half_log2_e) * inv_root_two_pi
        pre_grad = (act_grad_ref[:, at] * (cdf_ref[:, at] + pre * density)).astype(bf16)
        term = lax.dot_general(
            pre_grad, w_in_ref[:, at], (((1,), (1,)), ((), ())), preferred_element_type=f32
        )
        lift = term if lift is None else lift + term
    grad_normed = lift * gain_ref[...].reshape(1, channels)
    normed = normed_ref[...]
    grad = inv_ref[...] * (
        grad_normed
        - jnp.mean(grad_normed, axis=-1, keepdims=True)
        - normed * jnp.mean(grad_normed * normed, axis=-1, keepdims=True)
    )
    grad_ref[...] = grad
    shaped = grad.reshape(capacity, 8, 8, channels)
    swap_edges(shaped[:, 5:8], shaped[:, 0:3], is_odd(place_ref), core_ref, cross_ref)
    column = lax.broadcasted_iota(jnp.int32, (1, LANES), 1)
    weights = jnp.zeros((1, LANES), f32)
    for tile in range(capacity):
        amount = is_live(counts_ref, tile) * pool_ref[0, tile]
        weights = jnp.where(column == tile, amount, weights)
    hidden = jnp.sum(pooled_ref[...] * weights, axis=1, keepdims=True)
    mixed = jnp.sum(hidden * w_out_ref[...].astype(f32), axis=0, keepdims=True)
    emb_ref[...] = (own_sum_ref[...] + scale_ref[...].reshape(1, channels) * mixed) * 0.125


def taps_kernel(pad_ref, edge_ref, grad_ref, emb_ref, state_ref, pack_ref, part_ref):
    parts, capacity = pad_ref.shape[0], pad_ref.shape[1]
    for lane in range(parts):

        def one_column(col):
            def one_tile(tile, sums):
                sums = list(sums)
                grads = [grad_ref[pl.ds(tile * 64 + row * 8, 8), lanes(lane)] for row in range(8)]
                for held in range(14):
                    if 3 <= held < 11:
                        window = pad_ref[lane, tile, held - 3, pl.ds(5 + col, 8), :]
                    else:
                        row = held if held < 3 else held - 8
                        window = edge_ref[lane, tile, row, pl.ds(5 + col, 8), :]
                    for out in range(8):
                        tap = held - out
                        if 0 <= tap < 7:
                            sums[tap] = sums[tap] + window * grads[out]
                return tuple(sums)

            sums = tuple(jnp.zeros((8, LANES), f32) for _ in range(7))
            for tile in range(capacity):
                sums = one_tile(tile, sums)
            for row in range(7):
                part_ref[row * 7 + col, :, lanes(lane)] = sums[row]
            return 0

        for col in range(7):
            one_column(col)
    state_ref[0:TAPS, :] = jnp.sum(part_ref[...], axis=1)
    state_ref[TAPS : TAPS + 1, :] = emb_ref[...]
    state_ref[TAPS + 1 :, :] = jnp.zeros((STATE - TAPS - 1, emb_ref.shape[1]), f32)
    pack_ref[...] = packed(state_ref)


def packed(state_ref):
    state = state_ref[...]
    high = state.astype(bf16)
    low = pltpu.roll(state - high.astype(f32), 1, 0)
    row = lax.broadcasted_iota(jnp.int32, state.shape, 0)
    return jnp.where(row == TAPS + 1, low, high.astype(f32)).astype(bf16)


def merged(state_ref, got, with_embedding=True):
    total = packed(state_ref).astype(f32) + got.astype(f32)
    row = lax.broadcasted_iota(jnp.int32, total.shape, 0)
    if with_embedding:
        embedding = total + pltpu.roll(total, STATE - 1, 0)
    else:
        embedding = state_ref[...]
    return jnp.where(row < TAPS, total, jnp.where(row == TAPS, embedding, 0.0))


def state_kernel(with_embedding, state_ref, got_ref, new_ref, pack_ref):
    new_ref[...] = merged(state_ref, got_ref[...], with_embedding)
    pack_ref[...] = packed(new_ref)


def merge_kernel(splits, terms, place_ref, *refs):
    sums, refs = refs[: 2 * terms], refs[2 * terms :]
    outs = max(1, len(splits))
    keeps, sends, sum_ref = refs[0 : 2 * outs : 2], refs[1 : 2 * outs : 2], refs[2 * outs]
    first = 0
    for keep_ref, got_ref in zip(sums[0::2], sums[1::2]):
        count = keep_ref.shape[0]
        sum_ref[first : first + count, :] = keep_ref[...] + got_ref[...].astype(f32)
        first += count
    for keep_ref, send_ref, (start, count, rows, bit) in zip(keeps, sends, splits):
        split_pieces(sum_ref.at[start : start + count], rows, place_ref, bit, keep_ref, send_ref)
    if not splits:
        keeps[0][...] = sum_ref[...]
        sends[0][...] = sum_ref[...].astype(bf16)


def pair_kernel(keep_ref, got_ref, new_ref, send_ref):
    total = keep_ref[...].astype(bf16).astype(f32) + got_ref[...].astype(f32)
    new_ref[...] = total
    send_ref[...] = total.astype(bf16)


def finish_kernel(keep_ref, got_ref, state_ref, new_ref, share_ref, taps_ref, emb_ref):
    share_ref[...] = keep_ref[...].astype(bf16).astype(f32) + got_ref[...].astype(f32)
    total = merged(state_ref, new_ref[...])
    for row in range(7):
        taps_ref[row] = total[row * 7 : row * 7 + 7, :]
    emb_ref[...] = total[TAPS : TAPS + 1, :]


def middle_kernel(start, adj_ref, grad_ref, kern_ref, out_ref, pad_ref):
    capacity, parts = adj_ref.shape[0], out_ref.shape[1] // LANES
    columns = slice(start * LANES, (start + parts) * LANES)

    def own_at(tile, row):
        at = tile * 64 + row * 8
        return grad_ref[pl.ds(at if isinstance(at, int) else pl.multiple_of(at, 8), 8), columns]

    fill_middle(pad_ref, own_at, adj_ref, capacity, 0, parts)

    def finish(tile, lane, sums):
        for row in range(8):
            out_ref[pl.ds(tile * 64 + row * 8, 8), lanes(lane)] = sums[row]

    convolve(
        [(pad_ref, 8, 3)],
        lambda row, col, lane: kern_ref[6 - row, 6 - col : 7 - col, lanes(start + lane)],
        finish, capacity, parts,
    )


def outer_kernel(
    adj_ref, place_ref, counts_ref, pool_ref, first_ref, other_ref, core_ref, cross_ref, kern_ref, up_ref, cot_ref,
    out_ref, pad_ref,
):
    capacity, parts = adj_ref.shape[0], up_ref.shape[1] // LANES
    fill_edges(pad_ref, core_ref, cross_ref, place_ref, adj_ref, capacity, parts)

    def finish(tile, lane, sums):
        live = is_live(counts_ref, tile)
        extra = pool_ref[0, tile] * cot_ref[:, lanes(lane)] * 0.125
        for row in range(8):
            at = pl.ds(tile * 64 + row * 8, 8)
            part = first_ref[at, :] if lane == 0 else other_ref[at, lanes(lane - 1)]
            total = live * (up_ref[at, lanes(lane)].astype(f32) + extra) + part
            if sums[row] is not None:
                total = total + sums[row]
            out_ref[at, lanes(lane)] = (live * total).astype(bf16)

    convolve(
        [(pad_ref.at[:, :, 0:3], 3, 0), (pad_ref.at[:, :, 3:6], 3, 11)],
        lambda row, col, lane: kern_ref[6 - row, 6 - col : 7 - col, lanes(lane)],
        finish, capacity, parts,
    )


def whole_pass(
    tiles_in, upstream, pool_weight, slide_cot, adjacency, counts, kernel, norm_gain, w_in, w_out,
    layer_scale,
):
    own = tiles_in[0]
    capacity, _, _, channels = own.shape
    parts = channels // LANES
    hidden = w_in.shape[1]
    pixels = capacity * 64
    up = upstream.reshape(pixels, channels)
    wanted = adjacency[0]
    edge_shape = (capacity, 3, 8, channels)
    count = lax.axis_size("space")
    stages = count.bit_length() - 1
    rows = hidden // count
    place = lax.axis_index("space").astype(jnp.int32).reshape(1, 1)

    core, cross = call(
        edge_kernel, [struct(edge_shape, bf16)] * 2, [SMEM, VMEM], [place, own],
        flops=EDGE_COST,
    )
    cross = crossed(cross)
    core = swapped(core, "space", 1)

    pad, conv, mixed, act_grad, own_sum = call(
        early_kernel,
        [
            struct((parts, capacity, 8, 24, LANES)),
            struct((pixels, channels)),
            struct((pixels, channels + LANES), bf16),
            struct((pixels, hidden)),
            struct((1, channels)),
        ],
        [SMEM, VMEM, SMEM] + [VMEM] * 6,
        [wanted, counts, pool_weight, slide_cot, layer_scale, kernel, own, up, w_out],
        flops=2 * pixels * channels * hidden,
    )
    edge, normed, inv, pre, cdf, keep, send, pooled = call(
        functools.partial(forward_kernel, rows),
        [
            struct((parts, capacity, 6, 24, LANES)),
            struct((pixels, channels)),
            struct((pixels, 1)),
            struct((pixels, hidden)),
            struct((pixels, hidden)),
            struct((hidden // 2, channels)),
            struct((hidden // 2, channels), bf16),
            struct((hidden, LANES)),
        ],
        [SMEM] * 2 + [VMEM] * 7,
        [wanted, place, core, cross, conv, kernel, norm_gain, w_in, mixed],
        flops=4 * pixels * channels * hidden,
        scratch=[pltpu.VMEM((pixels, channels), f32)],
    )
    got = swapped(send, "space", 1)

    grad, core, cross, emb = call(
        back_kernel,
        [
            struct((pixels, channels)),
            struct(edge_shape, bf16),
            struct(edge_shape, bf16),
            struct((1, channels)),
        ],
        [SMEM, VMEM, SMEM] + [VMEM] * 11,
        [place, counts, pool_weight, pre, cdf, act_grad, w_in, normed, inv, norm_gain, pooled, w_out, layer_scale, own_sum],
        flops=2 * pixels * channels * hidden,
    )
    cross = crossed(cross)
    core = swapped(core, "space", 1)

    def merge(parts_, splits):
        held = sum(keep.shape[0] for keep, _ in parts_)
        shapes = []
        for size in [count // 2 for _, count, _, _ in splits] or [held]:
            shapes += [struct((size, channels)), struct((size, channels), bf16)]
        operands = [array for pair in parts_ for array in pair]
        out = call(
            functools.partial(merge_kernel, splits, len(parts_)), shapes,
            [SMEM] + [VMEM] * len(operands), [place] + operands,
            scratch=[pltpu.VMEM((held, channels), f32)],
        )
        return list(zip(out[0::2], out[1::2]))

    half = hidden // 4
    (keep_a, send_a), (keep_b, send_b) = merge([(keep, got)], [(0, half, rows, 1), (half, half, 2 * rows, 2)])
    got_a = swapped(send_a, "space", 2)
    got_b = swapped(send_b, "space", 4)
    half //= 2
    ((keep_a, send_a),) = merge([(keep_a, got_a)], [(0, half, rows, 2)])
    ((keep_b, send_b),) = merge([(keep_b, got_b)], [(0, half, rows, 1)])
    got_a = swapped(send_a, "space", 4)
    got_b = swapped(send_b, "space", 2)
    held = [(keep_a, got_a), (keep_b, got_b)]
    for stage in range(3, stages):
        size = hidden >> stage
        ((keep, send),) = merge(held, [(0, size, rows, stage)])
        got = swapped(send, "space", 1 << stage)
        held = [(keep, got)]
    ((share, send),) = merge(held, [])
    groups = lax.axis_size("dp")
    bit = 1
    while bit < groups:
        got = swapped(send, "dp", bit)
        bit *= 2
        if bit < groups:
            share, send = call(pair_kernel, [struct(share.shape), struct(send.shape, bf16)], [VMEM] * 2, [share, got])

    state, pack = call(
        taps_kernel, [struct((STATE, channels)), struct((STATE, channels), bf16)],
        [VMEM] * 4, [pad, edge, grad, emb],
        scratch=[pltpu.VMEM((TAPS, 8, channels), f32)],
    )
    steps = [("space", 1)] + [("dp", 1 << n) for n in range(groups.bit_length() - 1)]
    steps += [("space", 4), ("space", 2)] + [("space", 1 << n) for n in range(3, stages)]
    for axis, bit in steps:
        new = swapped(pack, axis, bit)
        if (axis, bit) != steps[-1]:
            state, pack = call(
                functools.partial(state_kernel, axis == "space"),
                [struct((STATE, channels)), struct((STATE, channels), bf16)],
                [VMEM] * 2, [state, new],
            )

    share, tap_grad, embedding = call(
        finish_kernel, [struct((rows, channels)), struct(kernel.shape), struct((1, channels))],
        [VMEM] * 4, [share, got, state, new],
    )

    middle = []
    for start, width in ((0, 1), (1, parts - 1)):
        middle.append(call(
            functools.partial(middle_kernel, start), struct((pixels, width * LANES)),
            [SMEM] + [VMEM] * 2, [wanted, grad, kernel],
            scratch=[pltpu.VMEM((width, capacity, 8, 24, LANES), f32)],
        ))
    grad_tiles = call(
        outer_kernel, struct((pixels, channels), bf16),
        [SMEM] * 2 + [VMEM, SMEM] + [VMEM] * 7,
        [wanted, place, counts, pool_weight, *middle, core, cross, kernel, up, slide_cot],
        scratch=[pltpu.VMEM((parts, capacity, 6, 24, LANES), f32)],
    )
    return (
        embedding,
        grad_tiles.reshape(tiles_in.shape),
        share,
        tap_grad,
    )


def solution(mesh):
    return jax.shard_map(
        whole_pass,
        mesh=mesh,
        in_specs=(
            P("dp", "space", None, None, None),
            P("dp", "space", None, None, None),
            P("dp", "space"),
            P("dp", None),
            P("dp", "space", None),
            P("dp", "space"),
            P(),
            P(),
            P(),
            P(),
            P(),
        ),
        out_specs=(P("dp", None), P("dp", "space", None, None, None), P("space", None), P()),
        check_vma=False,
    )
```

```python
import functools

import jax
import jax.numpy as jnp
from jax import lax
from jax.experimental import pallas as pl
from jax.experimental.pallas import tpu as pltpu
from jax.sharding import PartitionSpec as P

sqrt_half = 0.7071067811865476
inv_root_two_pi = 0.3989422804014327
half_log2_e = -0.7213475204444817
f32 = jnp.float32
bf16 = jnp.bfloat16
LANES = 128

VMEM = pl.BlockSpec(memory_space=pltpu.VMEM)
SMEM = pl.BlockSpec(memory_space=pltpu.SMEM)
HBM = pl.BlockSpec(memory_space=pltpu.HBM)
STATE = 56
TAPS = 49
CHUNK = 768
BACK_CHUNK = 512
EDGE_COST = 5_000_000_000


def call(body, out_shape, in_specs, args, flops=0, scratch=(), limit=16 << 20, out_specs=None):
    outs = out_shape if isinstance(out_shape, (list, tuple)) else [out_shape]
    total = sum(a.size * a.dtype.itemsize for a in list(args) + list(outs))
    return pl.pallas_call(
        body,
        out_shape=out_shape,
        in_specs=in_specs,
        out_specs=out_specs or jax.tree.map(lambda _: VMEM, out_shape),
        scratch_shapes=scratch,
        compiler_params=pltpu.CompilerParams(vmem_limit_bytes=limit),
        cost_estimate=pl.CostEstimate(flops=flops, bytes_accessed=total, transcendentals=0),
    )(*args)


def struct(shape, dtype=f32):
    return jax.ShapeDtypeStruct(shape, dtype)


def swapped(value, axis, bit):
    count = lax.axis_size(axis)
    return lax.ppermute(value, axis, [(source, source ^ bit) for source in range(count)])


def crossed(value):
    groups, count = lax.axis_size("dp"), lax.axis_size("space")
    targets = []
    for group in range(groups):
        for n in range(count):
            step = 1 if n % 2 else -1
            if 0 <= n + step < count:
                targets.append((group * count + n, group * count + n + step))
            elif (group ^ 1) < groups:
                targets.append((group * count + n, (group ^ 1) * count + n))
    return lax.ppermute(value, ("dp", "space"), targets)


def valid(entry):
    return jnp.where(entry >= 0, 1.0, 0.0).astype(f32)


def local(entry, capacity):
    return lax.rem(jnp.maximum(entry, 0), capacity)


def place(pad_ref, tile, row, part, value, parts):
    for lane in range(parts):
        pad_ref[lane, tile, row, pl.ds(part * 8, 8), :] = value[:, lane * LANES : (lane + 1) * LANES]


def fill_middle(pad_ref, own_at, adj_ref, capacity, first_row, parts):
    for tile in range(capacity):
        west, east = adj_ref[tile, 2], adj_ref[tile, 3]
        for row in range(8):
            place(pad_ref, tile, first_row + row, 0, own_at(local(west, capacity), row) * valid(west), parts)
            place(pad_ref, tile, first_row + row, 1, own_at(tile, row), parts)
            place(pad_ref, tile, first_row + row, 2, own_at(local(east, capacity), row) * valid(east), parts)


def fill_edge(pad_ref, edge_ref, adj_ref, capacity, entries, first_row, parts):
    for tile in range(capacity):
        for part, entry in enumerate(entries):
            wanted = adj_ref[tile, entry]
            index, keep = local(wanted, capacity), valid(wanted)
            for row in range(3):
                value = edge_ref[index, row].astype(f32) * keep
                place(pad_ref, tile, first_row + row, part, value, parts)


def fill_edges(pad_ref, core_ref, cross_ref, place_ref, adj_ref, capacity, parts):
    odd = lax.rem(place_ref[0, 0], 2)
    for parity, upper_ref, lower_ref in ((1, core_ref, cross_ref), (0, cross_ref, core_ref)):

        @pl.when(odd == parity)
        def _():
            fill_edge(pad_ref, upper_ref, adj_ref, capacity, UPPER, 0, parts)
            fill_edge(pad_ref, lower_ref, adj_ref, capacity, LOWER, 3, parts)


def is_live(counts_ref, tile):
    return jnp.where(tile < counts_ref[...], 1.0, 0.0).astype(f32)


def is_odd(place_ref):
    return lax.rem(place_ref[0, 0], 2).astype(f32)


UPPER, LOWER = (4, 0, 5), (6, 1, 7)


def convolve(pads, tap_row, finish, capacity, parts, between=()):
    for lane in range(parts):

        def one_tile(tile):
            sums = [None] * 8
            for col in range(7):
                taps = [tap_row(row, col, lane) for row in range(7)]
                for ref, rows, base in pads:
                    for held in range(rows):
                        window = ref[lane, tile, held, pl.ds(5 + col, 8), :]
                        for out in range(8):
                            tap = held + base - out
                            if 0 <= tap < 7:
                                term = window * taps[tap]
                                sums[out] = term if sums[out] is None else sums[out] + term
            finish(tile, lane, sums)
            return 0

        for tile in range(capacity):
            one_tile(tile)
            if lane * capacity + tile < len(between):
                between[lane * capacity + tile]()


def lanes(lane):
    return slice(lane * LANES, (lane + 1) * LANES)


def swap_edges(last, first, odd, core_ref, cross_ref):
    core_ref[...] = (first * odd + last * (1.0 - odd)).astype(bf16)
    cross_ref[...] = (last * odd + first * (1.0 - odd)).astype(bf16)


def edge_kernel(place_ref, tiles_ref, core_ref, cross_ref):
    swap_edges(
        tiles_ref[:, 5:8].astype(f32), tiles_ref[:, 0:3].astype(f32), is_odd(place_ref), core_ref, cross_ref
    )


def early_kernel(
    adj_ref, counts_ref, pool_ref, cot_ref, scale_ref, kern_ref, tiles_ref, up_ref, w_out_ref,
    pad_ref, conv_ref, mixed_ref, act_grad_ref, own_sum_ref,
):
    capacity, parts = tiles_ref.shape[0], tiles_ref.shape[3] // LANES
    pixels = 64
    channels = tiles_ref.shape[3]
    fill_middle(pad_ref, lambda t, r: tiles_ref[t, r].astype(f32), adj_ref, capacity, 0, parts)
    own_sum = jnp.zeros((1, channels), f32)
    scale = scale_ref[...].reshape(1, channels)
    for tile in range(capacity):
        live = is_live(counts_ref, tile)
        pool = pool_ref[0, tile]
        rows = slice(tile * pixels, (tile + 1) * pixels)
        out_grad = live * (up_ref[rows, :].astype(f32) + pool * cot_ref[...] * 0.125)
        mixed_ref[rows, 0:channels] = (out_grad * scale).astype(bf16)
        column = lax.broadcasted_iota(jnp.int32, (pixels, LANES), 1)
        mixed_ref[rows, channels:] = jnp.where(column == tile, 1.0, 0.0).astype(bf16)
        own = tiles_ref[tile].astype(f32)
        own_sum += live * pool * jnp.sum(own.reshape(pixels, channels), axis=0, keepdims=True)
    own_sum_ref[...] = own_sum

    def product(at):
        act_grad_ref[:, at] = lax.dot_general(
            mixed_ref[:, 0:channels], w_out_ref[at, :], (((1,), (1,)), ((), ())), preferred_element_type=f32
        )

    hidden = w_out_ref.shape[0]
    step = 256 if hidden % 256 == 0 else hidden
    products = [functools.partial(product, slice(n, n + step)) for n in range(0, hidden, step)]

    def finish(tile, lane, sums):
        for row in range(8):
            conv_ref[pl.ds(tile * pixels + row * 8, 8), lanes(lane)] = sums[row]

    convolve(
        [(pad_ref, 8, 3)],
        lambda row, col, lane: kern_ref[row, col : col + 1, lanes(lane)],
        finish, capacity, parts, products,
    )


def split_pieces(value_ref, rows, place_ref, stage, keep_ref, send_ref):
    side = lax.rem(lax.div(place_ref[0, 0], 1 << stage), 2)
    for pair in range(value_ref.shape[0] // (2 * rows)):
        here = pl.ds(pair * rows, rows)
        mine = pl.ds(pl.multiple_of((2 * pair + side) * rows, 8), rows)
        other = pl.ds(pl.multiple_of((2 * pair + 1 - side) * rows, 8), rows)
        keep_ref[here, :] = value_ref[mine, :]
        send_ref[here, :] = value_ref[other, :].astype(bf16)


def forward_kernel(
    rows, adj_ref, place_ref, core_ref, cross_ref, conv_ref, kern_ref, gain_ref, w_in_ref, mixed_ref,
    edge_ref, normed_ref, inv_ref, pre_ref, cdf_ref, keep_ref, send_ref, pooled_ref, whole_ref,
):
    capacity, parts = adj_ref.shape[0], conv_ref.shape[1] // LANES
    channels = conv_ref.shape[1]
    pixels = 64
    fill_edges(edge_ref, core_ref, cross_ref, place_ref, adj_ref, capacity, parts)

    def finish(tile, lane, sums):
        for row in range(8):
            at = pl.ds(tile * pixels + row * 8, 8)
            total = conv_ref[at, lanes(lane)]
            if sums[row] is not None:
                total = total + sums[row]
            whole_ref[at, lanes(lane)] = total

    convolve(
        [(edge_ref.at[:, :, 0:3], 3, 0), (edge_ref.at[:, :, 3:6], 3, 11)],
        lambda row, col, lane: kern_ref[row, col : col + 1, lanes(lane)],
        finish, capacity, parts,
    )
    conv = whole_ref[...]
    centred = conv - jnp.mean(conv, axis=-1, keepdims=True)
    inv_std = lax.rsqrt(jnp.mean(centred * centred, axis=-1, keepdims=True) + 1e-06)
    normed = centred * inv_std
    normed_ref[...] = normed
    inv_ref[...] = inv_std
    lifted = (normed * gain_ref[...].reshape(1, channels)).astype(bf16)
    hidden = w_in_ref.shape[1]
    side = lax.rem(place_ref[0, 0], 2)
    chunk = CHUNK if hidden % CHUNK == 0 and CHUNK % (2 * rows) == 0 else hidden

    def project(first):
        return jnp.dot(lifted, w_in_ref[:, first : first + chunk], preferred_element_type=f32)

    following = project(0)
    for first in range(0, hidden, chunk):
        at = slice(first, first + chunk)
        pre = following
        if first + chunk < hidden:
            following = project(first + chunk)
        cdf = 0.5 * (1.0 + lax.erf(pre * sqrt_half))
        pre_ref[:, at] = pre
        cdf_ref[:, at] = cdf
        activated = (pre * cdf).astype(bf16)
        both = lax.dot_general(
            activated, mixed_ref[...], (((0,), (0,)), ((), ())), preferred_element_type=f32
        )
        pooled_ref[at, :] = both[:, channels:]
        for block in range(0, chunk, 2 * rows):
            even = both[block : block + rows, 0:channels]
            odd_rows = both[block + rows : block + 2 * rows, 0:channels]
            out = pl.ds((first + block) // 2, rows)
            keep_ref[out, :] = jnp.where(side == 0, even, odd_rows)
            send_ref[out, :] = jnp.where(side == 0, odd_rows, even).astype(bf16)


def back_kernel(
    place_ref, counts_ref, pool_ref, pre_ref, cdf_ref, act_grad_ref, w_in_ref, normed_ref, inv_ref, gain_ref, pooled_ref, w_out_ref,
    scale_ref, own_sum_ref, grad_ref, core_ref, cross_ref, emb_ref,
):
    channels = normed_ref.shape[1]
    capacity = core_ref.shape[0]
    hidden = w_in_ref.shape[1]
    chunk = BACK_CHUNK if hidden % BACK_CHUNK == 0 else hidden
    lift = None
    for first in range(0, hidden, chunk):
        at = slice(first, first + chunk)
        pre = pre_ref[:, at]
        density = jnp.exp2(pre * pre * half_log2_e) * inv_root_two_pi
        pre_grad = (act_grad_ref[:, at] * (cdf_ref[:, at] + pre * density)).astype(bf16)
        term = lax.dot_general(
            pre_grad, w_in_ref[:, at], (((1,), (1,)), ((), ())), preferred_element_type=f32
        )
        lift = term if lift is None else lift + term
    grad_normed = lift * gain_ref[...].reshape(1, channels)
    normed = normed_ref[...]
    grad = inv_ref[...] * (
        grad_normed
        - jnp.mean(grad_normed, axis=-1, keepdims=True)
        - normed * jnp.mean(grad_normed * normed, axis=-1, keepdims=True)
    )
    grad_ref[...] = grad
    shaped = grad.reshape(capacity, 8, 8, channels)
    swap_edges(shaped[:, 5:8], shaped[:, 0:3], is_odd(place_ref), core_ref, cross_ref)
    column = lax.broadcasted_iota(jnp.int32, (1, LANES), 1)
    weights = jnp.zeros((1, LANES), f32)
    for tile in range(capacity):
        amount = is_live(counts_ref, tile) * pool_ref[0, tile]
        weights = jnp.where(column == tile, amount, weights)
    hidden = jnp.sum(pooled_ref[...] * weights, axis=1, keepdims=True)
    mixed = jnp.sum(hidden * w_out_ref[...].astype(f32), axis=0, keepdims=True)
    emb_ref[...] = (own_sum_ref[...] + scale_ref[...].reshape(1, channels) * mixed) * 0.125


def taps_kernel(pad_ref, edge_ref, grad_ref, emb_ref, state_ref, pack_ref, part_ref):
    parts, capacity = pad_ref.shape[0], pad_ref.shape[1]
    for lane in range(parts):

        def one_column(col):
            def one_tile(tile, sums):
                sums = list(sums)
                grads = [grad_ref[pl.ds(tile * 64 + row * 8, 8), lanes(lane)] for row in range(8)]
                for held in range(14):
                    if 3 <= held < 11:
                        window = pad_ref[lane, tile, held - 3, pl.ds(5 + col, 8), :]
                    else:
                        row = held if held < 3 else held - 8
                        window = edge_ref[lane, tile, row, pl.ds(5 + col, 8), :]
                    for out in range(8):
                        tap = held - out
                        if 0 <= tap < 7:
                            sums[tap] = sums[tap] + window * grads[out]
                return tuple(sums)

            sums = tuple(jnp.zeros((8, LANES), f32) for _ in range(7))
            for tile in range(capacity):
                sums = one_tile(tile, sums)
            for row in range(7):
                part_ref[row * 7 + col, :, lanes(lane)] = sums[row]
            return 0

        for col in range(7):
            one_column(col)
    state_ref[0:TAPS, :] = jnp.sum(part_ref[...], axis=1)
    state_ref[TAPS : TAPS + 1, :] = emb_ref[...]
    state_ref[TAPS + 1 :, :] = jnp.zeros((STATE - TAPS - 1, emb_ref.shape[1]), f32)
    pack_ref[...] = packed(state_ref)


def packed(state_ref):
    state = state_ref[...]
    high = state.astype(bf16)
    low = pltpu.roll(state - high.astype(f32), 1, 0)
    row = lax.broadcasted_iota(jnp.int32, state.shape, 0)
    return jnp.where(row == TAPS + 1, low, high.astype(f32)).astype(bf16)


def merged(state_ref, got, with_embedding=True):
    total = packed(state_ref).astype(f32) + got.astype(f32)
    row = lax.broadcasted_iota(jnp.int32, total.shape, 0)
    if with_embedding:
        embedding = total + pltpu.roll(total, STATE - 1, 0)
    else:
        embedding = state_ref[...]
    return jnp.where(row < TAPS, total, jnp.where(row == TAPS, embedding, 0.0))


def state_kernel(with_embedding, state_ref, got_ref, new_ref, pack_ref):
    new_ref[...] = merged(state_ref, got_ref[...], with_embedding)
    pack_ref[...] = packed(new_ref)


def merge_kernel(splits, terms, place_ref, *refs):
    sums, refs = refs[: 2 * terms], refs[2 * terms :]
    outs = max(1, len(splits))
    keeps, sends, sum_ref = refs[0 : 2 * outs : 2], refs[1 : 2 * outs : 2], refs[2 * outs]
    first = 0
    for keep_ref, got_ref in zip(sums[0::2], sums[1::2]):
        count = keep_ref.shape[0]
        sum_ref[first : first + count, :] = keep_ref[...] + got_ref[...].astype(f32)
        first += count
    for keep_ref, send_ref, (start, count, rows, bit) in zip(keeps, sends, splits):
        split_pieces(sum_ref.at[start : start + count], rows, place_ref, bit, keep_ref, send_ref)
    if not splits:
        keeps[0][...] = sum_ref[...]
        sends[0][...] = sum_ref[...].astype(bf16)


def pair_kernel(keep_ref, got_ref, new_ref, send_ref):
    total = keep_ref[...].astype(bf16).astype(f32) + got_ref[...].astype(f32)
    new_ref[...] = total
    send_ref[...] = total.astype(bf16)


def finish_kernel(keep_ref, got_ref, state_ref, new_ref, share_ref, taps_ref, emb_ref):
    share_ref[...] = keep_ref[...].astype(bf16).astype(f32) + got_ref[...].astype(f32)
    total = merged(state_ref, new_ref[...])
    for row in range(7):
        taps_ref[row] = total[row * 7 : row * 7 + 7, :]
    emb_ref[...] = total[TAPS : TAPS + 1, :]


def middle_kernel(adj_ref, grad_ref, kern_ref, out_ref, pad_ref):
    capacity, parts = adj_ref.shape[0], grad_ref.shape[1] // LANES

    def own_at(tile, row):
        at = tile * 64 + row * 8
        return grad_ref[pl.ds(at if isinstance(at, int) else pl.multiple_of(at, 8), 8), :]

    fill_middle(pad_ref, own_at, adj_ref, capacity, 0, parts)

    def finish(tile, lane, sums):
        for row in range(8):
            out_ref[pl.ds(tile * 64 + row * 8, 8), lanes(lane)] = sums[row]

    convolve(
        [(pad_ref, 8, 3)],
        lambda row, col, lane: kern_ref[6 - row, 6 - col : 7 - col, lanes(lane)],
        finish, capacity, parts,
    )


def outer_kernel(
    adj_ref, place_ref, counts_ref, pool_ref, part_ref, core_ref, cross_ref, kern_ref, up_ref, cot_ref,
    out_ref, pad_ref,
):
    capacity, parts = adj_ref.shape[0], part_ref.shape[1] // LANES
    fill_edges(pad_ref, core_ref, cross_ref, place_ref, adj_ref, capacity, parts)

    def finish(tile, lane, sums):
        live = is_live(counts_ref, tile)
        extra = pool_ref[0, tile] * cot_ref[:, lanes(lane)] * 0.125
        for row in range(8):
            at = pl.ds(tile * 64 + row * 8, 8)
            total = live * (up_ref[at, lanes(lane)].astype(f32) + extra) + part_ref[at, lanes(lane)]
            if sums[row] is not None:
                total = total + sums[row]
            out_ref[at, lanes(lane)] = (live * total).astype(bf16)

    convolve(
        [(pad_ref.at[:, :, 0:3], 3, 0), (pad_ref.at[:, :, 3:6], 3, 11)],
        lambda row, col, lane: kern_ref[6 - row, 6 - col : 7 - col, lanes(lane)],
        finish, capacity, parts,
    )


def whole_pass(
    tiles_in, upstream, pool_weight, slide_cot, adjacency, counts, kernel, norm_gain, w_in, w_out,
    layer_scale,
):
    own = tiles_in[0]
    capacity, _, _, channels = own.shape
    parts = channels // LANES
    hidden = w_in.shape[1]
    pixels = capacity * 64
    up = upstream.reshape(pixels, channels)
    wanted = adjacency[0]
    edge_shape = (capacity, 3, 8, channels)
    count = lax.axis_size("space")
    stages = count.bit_length() - 1
    rows = hidden // count
    place = lax.axis_index("space").astype(jnp.int32).reshape(1, 1)

    core, cross = call(
        edge_kernel, [struct(edge_shape, bf16)] * 2, [SMEM, VMEM], [place, own],
        flops=EDGE_COST,
    )
    cross = crossed(cross)
    core = swapped(core, "space", 1)

    pad, conv, mixed, act_grad, own_sum = call(
        early_kernel,
        [
            struct((parts, capacity, 8, 24, LANES)),
            struct((pixels, channels)),
            struct((pixels, channels + LANES), bf16),
            struct((pixels, hidden)),
            struct((1, channels)),
        ],
        [SMEM, VMEM, SMEM] + [VMEM] * 6,
        [wanted, counts, pool_weight, slide_cot, layer_scale, kernel, own, up, w_out],
        flops=2 * pixels * channels * hidden,
    )
    edge, normed, inv, pre, cdf, keep, send, pooled = call(
        functools.partial(forward_kernel, rows),
        [
            struct((parts, capacity, 6, 24, LANES)),
            struct((pixels, channels)),
            struct((pixels, 1)),
            struct((pixels, hidden)),
            struct((pixels, hidden)),
            struct((hidden // 2, channels)),
            struct((hidden // 2, channels), bf16),
            struct((hidden, LANES)),
        ],
        [SMEM] * 2 + [VMEM] * 7,
        [wanted, place, core, cross, conv, kernel, norm_gain, w_in, mixed],
        flops=4 * pixels * channels * hidden,
        scratch=[pltpu.VMEM((pixels, channels), f32)],
    )
    got = swapped(send, "space", 1)

    grad, core, cross, emb = call(
        back_kernel,
        [
            struct((pixels, channels)),
            struct(edge_shape, bf16),
            struct(edge_shape, bf16),
            struct((1, channels)),
        ],
        [SMEM, VMEM, SMEM] + [VMEM] * 11,
        [place, counts, pool_weight, pre, cdf, act_grad, w_in, normed, inv, norm_gain, pooled, w_out, layer_scale, own_sum],
        flops=2 * pixels * channels * hidden,
    )
    cross = crossed(cross)
    core = swapped(core, "space", 1)

    def merge(parts_, splits):
        held = sum(keep.shape[0] for keep, _ in parts_)
        shapes = []
        for size in [count // 2 for _, count, _, _ in splits] or [held]:
            shapes += [struct((size, channels)), struct((size, channels), bf16)]
        operands = [array for pair in parts_ for array in pair]
        out = call(
            functools.partial(merge_kernel, splits, len(parts_)), shapes,
            [SMEM] + [VMEM] * len(operands), [place] + operands,
            scratch=[pltpu.VMEM((held, channels), f32)],
        )
        return list(zip(out[0::2], out[1::2]))

    half = hidden // 4
    (keep_a, send_a), (keep_b, send_b) = merge([(keep, got)], [(0, half, rows, 1), (half, half, 2 * rows, 2)])
    got_a = swapped(send_a, "space", 2)
    got_b = swapped(send_b, "space", 4)
    half //= 2
    ((keep_a, send_a),) = merge([(keep_a, got_a)], [(0, half, rows, 2)])
    ((keep_b, send_b),) = merge([(keep_b, got_b)], [(0, half, rows, 1)])
    got_a = swapped(send_a, "space", 4)
    got_b = swapped(send_b, "space", 2)
    held = [(keep_a, got_a), (keep_b, got_b)]
    for stage in range(3, stages):
        size = hidden >> stage
        ((keep, send),) = merge(held, [(0, size, rows, stage)])
        got = swapped(send, "space", 1 << stage)
        held = [(keep, got)]
    ((share, send),) = merge(held, [])
    groups = lax.axis_size("dp")
    bit = 1
    while bit < groups:
        got = swapped(send, "dp", bit)
        bit *= 2
        if bit < groups:
            share, send = call(pair_kernel, [struct(share.shape), struct(send.shape, bf16)], [VMEM] * 2, [share, got])

    state, pack = call(
        taps_kernel, [struct((STATE, channels)), struct((STATE, channels), bf16)],
        [VMEM] * 4, [pad, edge, grad, emb],
        scratch=[pltpu.VMEM((TAPS, 8, channels), f32)],
    )
    steps = [("space", 1)] + [("dp", 1 << n) for n in range(groups.bit_length() - 1)]
    steps += [("space", 1 << n) for n in range(1, stages)]
    for axis, bit in steps:
        new = swapped(pack, axis, bit)
        if (axis, bit) != steps[-1]:
            state, pack = call(
                functools.partial(state_kernel, axis == "space"),
                [struct((STATE, channels)), struct((STATE, channels), bf16)],
                [VMEM] * 2, [state, new],
            )

    share, tap_grad, embedding = call(
        finish_kernel, [struct((rows, channels)), struct(kernel.shape), struct((1, channels))],
        [VMEM] * 4, [share, got, state, new],
    )

    part = call(
        middle_kernel, struct((pixels, channels)), [SMEM] + [VMEM] * 2, [wanted, grad, kernel],
        scratch=[pltpu.VMEM((parts, capacity, 8, 24, LANES), f32)],
    )
    grad_tiles = call(
        outer_kernel, struct((pixels, channels), bf16),
        [SMEM] * 2 + [VMEM, SMEM] + [VMEM] * 6,
        [wanted, place, counts, pool_weight, part, core, cross, kernel, up, slide_cot],
        scratch=[pltpu.VMEM((parts, capacity, 6, 24, LANES), f32)],
    )
    return (
        embedding,
        grad_tiles.reshape(tiles_in.shape),
        share,
        tap_grad,
    )


def solution(mesh):
    return jax.shard_map(
        whole_pass,
        mesh=mesh,
        in_specs=(
            P("dp", "space", None, None, None),
            P("dp", "space", None, None, None),
            P("dp", "space"),
            P("dp", None),
            P("dp", "space", None),
            P("dp", "space"),
            P(),
            P(),
            P(),
            P(),
            P(),
        ),
        out_specs=(P("dp", None), P("dp", "space", None, None, None), P("space", None), P()),
        check_vma=False,
    )
```
